32 devices in a mesh: shot: 4 (over z), sub: 8 (over y, x, core).
Axes of the slice: x: 2, y: 2, z: 4, core: 2. Of those that a mesh axis runs over, the one named last changes fastest.
Arguments:
- electric: float32 [4, 3, 32, 32, 128], P('shot', None, 'sub'), may hold values from -6 to 6
- magnetic: float32 [4, 3, 32, 32, 128], P('shot', None, 'sub'), may hold values from -6 to 6
- polar: float32 [4, 3, 32, 32, 128], P('shot', None, 'sub'), may hold values from -4 to 4
- adj_electric: float32 [4, 3, 32, 32, 128], P('shot', None, 'sub'), may hold values from -6 to 6
- adj_magnetic: float32 [4, 3, 32, 32, 128], P('shot', None, 'sub'), may hold values from -6 to 6
- adj_polar: float32 [4, 3, 32, 32, 128], P('shot', None, 'sub'), may hold values from -4 to 4
- permittivity: float32 [32, 32, 128], P('sub'), may hold values from 3 to 25
- conductivity: float32 [32, 32, 128], P('sub'), may hold values from 0.02 to 2
- debye_class: int32 [32, 32, 128], P('sub'), may hold values from 0 to 7
- debye_rate: float32 [8], replicated, may hold values from 0.3 to 0.95
- debye_strength: float32 [8], replicated, may hold values from 0.3 to 3
- wavelet: float32 [6], replicated, may hold values from -4 to 4
- src_cell: int32 [4, 64], P('shot'), may hold values from 0 to 131071
- src_sign: int32 [4, 64], P('shot'), may hold values from 0 to 1
- rec_owner: int32 [4, 1024, 1], P('shot', 'sub'), may hold values from 0 to 7; in each aligned block of 128 rows (0 to 127, 128 to 255, ..., all dimensions but the last counted through in order) at most 16 rows name the same one
- rec_pos: int32 [4, 1024], P('shot', 'sub'), may hold values from 0 to 16383
- observed: float32 [4, 6, 1024], P('shot', None, 'sub'), may hold values from -6 to 6
Outputs:
- grad_eps: float32 [32, 32, 128], P('sub')
- grad_sigma: float32 [32, 32, 128], P('sub')
The draws below stay inside these ranges and needn't reach their ends.
Inputs may be any that keep to these rules, and one draw needn't show every extreme that they name: Receiver r of a shot group lies in the x range of slab rec_owner; among the 128 receivers of each aligned block of the list at most 16 have the same owner.
All inputs are finite; a program needn't handle non-finite values.
Results may differ from the reference program's by a relative error of at most 0.0001.
Values sent between devices are 32-bit elements; how exact they have to be, the bound alone decides.
No kernel may reach another device: no remote copies, remote signals or barrier semaphores. Data moves between devices by JAX's collectives and lax.ppermute only.
A program may use at most 64 MiB of HBM per device.

```python
import math
import jax
import jax.numpy as jnp
import numpy as np
from jax import lax

CX = 4
NY = 128
NZ = 32
STEPS = 6
NCLASS = 8
NSRC = 64
REC_DEV = 128
CAP = 16
SHOTS = 4
NX = 32
NREC = 1024
N_SUB = 8


def plant(drawn, own_key, least, largest):
    spot = [jax.random.randint(jax.random.fold_in(own_key, axis), (), 0, length) for axis, length in enumerate(drawn.shape)]
    widest = drawn.shape.index(max(drawn.shape))
    beside = spot[:widest] + [(spot[widest] + 1) % drawn.shape[widest]] + spot[widest + 1:]
    return drawn.at[tuple(spot)].set(least).at[tuple(beside)].set(largest)


def levels(stream_key, shape, pieces, low, top_value):
    level, own = 1.0, jax.random.fold_in(stream_key, 6)
    for dim, blocks in pieces:
        steps = jnp.exp(jax.random.uniform(jax.random.fold_in(own, dim), (blocks,), jnp.float32, low / len(pieces), top_value / len(pieces)))
        level = level * jnp.repeat(steps, shape[dim] // blocks).reshape([-1 if axis == dim else 1 for axis in range(len(shape))])
    return level


def assign_block(own_key, own, number, rows, count, top, limit, lean):
    ranking = jax.random.permutation(own_key, count)
    crowded, usual = load_shares(count, rows * top, limit, lean, True), load_shares(count, rows * top, limit, lean, False)
    places = jnp.arange(count)

    def named(lengths, rotation):
        used = int((lengths > 0).sum())
        fixed = max(1, used // 4)
        moved = fixed + (places - fixed + rotation * (used - fixed)) % max(1, count - fixed)
        return jnp.zeros((count,), jnp.int32).at[ranking[jnp.where(places < fixed, places, moved)]].set(jnp.asarray(lengths, jnp.int32))

    lengths = jnp.where(number % 4 == 0, named(crowded, number // 4), named(usual, number - number // 4 - 1))
    mixed = jax.random.permutation(jax.random.fold_in(own, 3), count)
    giver, receiver = mixed[0:count // 2 * 2:2], mixed[1:count // 2 * 2:2]
    room = jnp.minimum(lengths[giver] - 1, limit - lengths[receiver]) // 2
    room = jnp.where((giver == ranking[0]) | (receiver == ranking[0]) | (lengths[receiver] == 0), 0, jnp.maximum(room, 0))
    moved = jax.random.randint(jax.random.fold_in(own, 4), (count // 2,), 0, 1 << 20) % (room + 1)
    lengths = lengths.at[giver].add(-moved).at[receiver].add(moved)
    labels = jnp.searchsorted(jnp.cumsum(lengths), jnp.arange(rows * top), side="right").astype(jnp.int32)
    table = labels.reshape(top, rows).T
    table = table[jax.random.permutation(jax.random.fold_in(own, 1), rows)]
    rotation = jax.random.randint(jax.random.fold_in(own, 2), (rows, 1), 0, top)
    return jnp.take_along_axis(table, (jnp.arange(top)[None, :] + rotation) % top, axis=1)


def load_shares(amount, total, most, slope, full):
    weights = [(1 << 20) // math.isqrt(rank ** slope) + 1 for rank in range(1, amount + 1)]
    largest = most if full else min(most, max(-(-total // amount), total * weights[0] // sum(weights)))
    least = 1 if total - largest >= amount - 1 else 0
    given, spare = [largest] + [least] * (amount - 1), total - largest - least * (amount - 1)
    while spare > 0:
        free = [i for i in range(1, amount) if given[i] < largest] or [i for i in range(1, amount) if given[i] < most]
        pool, budget = sum([weights[i] for i in free]), spare
        for i in free:
            addition = min(most - given[i], max(1, budget * weights[i] // pool), spare)
            given[i] = given[i] + addition
            spare = spare - addition
    return np.array(given)


def normal_values(stream_key, extent, scale, limit, shards=(), dtype=jnp.bfloat16):
    loudness = levels(stream_key, extent, shards, -0.22, 0.18) if shards else 1.0
    values = jax.random.normal(stream_key, extent, jnp.float32) * scale * loudness
    return jnp.minimum(jnp.maximum(values, -limit), limit).astype(dtype)


def setup_inputs(seed: int = 0) -> dict:
    key_of = jax.random.split(jax.random.key(seed), 18)
    electric = normal_values(key_of[0], (SHOTS, 3, NX, NZ, NY), 1.0, 6.0, ((0, 4), (2, 8)), jnp.float32)
    magnetic = normal_values(key_of[1], (SHOTS, 3, NX, NZ, NY), 1.0, 6.0, ((0, 4), (2, 8)), jnp.float32)
    polar = normal_values(key_of[2], (SHOTS, 3, NX, NZ, NY), 0.5, 4.0, ((0, 4), (2, 8)), jnp.float32)
    adj_electric = normal_values(key_of[3], (SHOTS, 3, NX, NZ, NY), 1.0, 6.0, ((0, 4), (2, 8)), jnp.float32)
    adj_magnetic = normal_values(key_of[4], (SHOTS, 3, NX, NZ, NY), 1.0, 6.0, ((0, 4), (2, 8)), jnp.float32)
    adj_polar = normal_values(key_of[5], (SHOTS, 3, NX, NZ, NY), 0.5, 4.0, ((0, 4), (2, 8)), jnp.float32)
    permittivity = jnp.clip(jnp.exp(math.log(25.0) - 2.1202635 * jax.random.uniform(key_of[6], (NX, NZ, NY), jnp.float32) ** levels(key_of[6], (NX, NZ, NY), ((0, 8),), -0.2, 0.2)), 3.0, 25.0)
    conductivity = jnp.clip(jnp.exp(math.log(2.0) - 4.6051702 * jax.random.uniform(key_of[7], (NX, NZ, NY), jnp.float32) ** levels(key_of[7], (NX, NZ, NY), ((0, 8),), -0.2, 0.2)), 0.02, 2.0)
    debye_class = plant(jax.random.randint(key_of[8], (NX, NZ, NY), 0, NCLASS), jax.random.fold_in(key_of[8], 1), 0, NCLASS - 1).astype(jnp.int32)
    debye_rate = jnp.clip(jax.random.uniform(key_of[9], (NCLASS,), jnp.float32, 0.3, 0.95), 0.3, 0.95)
    debye_strength = jnp.clip(jnp.exp(jax.random.uniform(key_of[10], (NCLASS,), jnp.float32, math.log(0.3), math.log(3.0))), 0.3, 3.0)
    wavelet = normal_values(key_of[11], (STEPS,), 1.0, 4.0, (), jnp.float32)
    src_cell = plant(jax.random.randint(key_of[12], (SHOTS, NSRC), 0, NX * NY * NZ), jax.random.fold_in(key_of[12], 1), 0, (NX * NY * NZ) - 1).astype(jnp.int32)
    src_sign = plant(jax.random.randint(key_of[13], (SHOTS, NSRC), 0, 2), jax.random.fold_in(key_of[13], 1), 0, 1).astype(jnp.int32)
    rec_owner_keys = jax.random.split(jax.random.fold_in(key_of[14], 1), SHOTS * NREC // REC_DEV)
    rec_owner_turns = jax.random.permutation(jax.random.fold_in(key_of[14], 3), SHOTS * NREC // REC_DEV)
    rec_owner = jax.vmap(lambda own, number: assign_block(jax.random.fold_in(key_of[14], 2), own, number, REC_DEV, N_SUB, 1, CAP, 2))(rec_owner_keys, rec_owner_turns).reshape((SHOTS, NREC, 1))
    rec_pos = plant(jax.random.randint(key_of[15], (SHOTS, NREC), 0, CX * NY * NZ), jax.random.fold_in(key_of[15], 1), 0, (CX * NY * NZ) - 1).astype(jnp.int32)
    observed = normal_values(key_of[16], (SHOTS, STEPS, NREC), 1.0, 6.0, ((0, 4), (2, 8)), jnp.float32)
    return dict(electric=electric, magnetic=magnetic, polar=polar, adj_electric=adj_electric, adj_magnetic=adj_magnetic, adj_polar=adj_polar, permittivity=permittivity, conductivity=conductivity, debye_class=debye_class, debye_rate=debye_rate, debye_strength=debye_strength, wavelet=wavelet, src_cell=src_cell, src_sign=src_sign, rec_owner=rec_owner, rec_pos=rec_pos, observed=observed)


def diff_forward(u, axis):
    tail = lax.slice_in_dim(u, 1, u.shape[axis], axis=axis)
    edge = jnp.zeros_like(lax.slice_in_dim(u, 0, 1, axis=axis))
    return jnp.concatenate([tail, edge], axis) - u


def diff_backward(u, axis):
    head = lax.slice_in_dim(u, 0, u.shape[axis] - 1, axis=axis)
    edge = jnp.zeros_like(lax.slice_in_dim(u, 0, 1, axis=axis))
    return u - jnp.concatenate([edge, head], axis)


def advance(e_field, h_field, p_field, coef_a, coef_b, rate, strength, inject):
    curl_e = jnp.stack([
        diff_forward(e_field[2], 2) - diff_forward(e_field[1], 1),
        diff_forward(e_field[0], 1) - diff_forward(e_field[2], 0),
        diff_forward(e_field[1], 0) - diff_forward(e_field[0], 2)])
    h_new = h_field - 0.5 * curl_e
    curl_h = jnp.stack([
        diff_backward(h_new[2], 2) - diff_backward(h_new[1], 1),
        diff_backward(h_new[0], 1) - diff_backward(h_new[2], 0),
        diff_backward(h_new[1], 0) - diff_backward(h_new[0], 2)])
    e_new = coef_a * e_field + coef_b * (curl_h - p_field)
    e_new = e_new.at[1].add(inject)
    p_new = rate * p_field + (1.0 - rate) * strength * e_new
    return e_new, h_new, p_new


def reference(electric, magnetic, polar, adj_electric, adj_magnetic, adj_polar, permittivity, conductivity, debye_class, debye_rate, debye_strength, wavelet, src_cell, src_sign, rec_owner, rec_pos, observed):
    ratio = conductivity / (2.0 * permittivity)
    coef_a = (1.0 - ratio) / (1.0 + ratio)
    coef_b = 0.5 / (permittivity * (1.0 + ratio))
    rate = debye_rate[debye_class]
    strength = debye_strength[debye_class]
    corr_eps = jnp.zeros((NX, NZ, NY), jnp.float32)
    corr_sigma = jnp.zeros((NX, NZ, NY), jnp.float32)
    for group in range(SHOTS):
        flat = src_cell[group]
        src_x = flat % NX
        src_y = (flat // NX) % NY
        src_z = flat // (NX * NY)
        signs = (2 * src_sign[group] - 1).astype(jnp.float32)
        cellpos = rec_pos[group]
        rec_x = rec_owner[group, :, 0] * CX + cellpos % CX
        rec_y = (cellpos // CX) % NY
        rec_z = cellpos // (CX * NY)
        state = (electric[group], magnetic[group], polar[group])
        history = [electric[group]]
        synth = []
        for step in range(STEPS):
            source = jnp.zeros((NX, NZ, NY), jnp.float32).at[src_x, src_z, src_y].add(signs * wavelet[step])
            state = advance(state[0], state[1], state[2], coef_a, coef_b, rate, strength, source)
            history.append(state[0])
            synth.append(state[0][1][rec_x, rec_z, rec_y])
        resid = jnp.stack(synth) - observed[group]
        state = (adj_electric[group], adj_magnetic[group], adj_polar[group])
        for back in range(STEPS):
            later = STEPS - back
            source = jnp.zeros((NX, NZ, NY), jnp.float32).at[rec_x, rec_z, rec_y].add(resid[later - 1])
            state = advance(state[0], state[1], state[2], coef_a, coef_b, rate, strength, source)
            adjoint = state[0]
            corr_eps = corr_eps + jnp.sum(adjoint * (history[later] - history[later - 1]), axis=0)
            corr_sigma = corr_sigma + jnp.sum(adjoint * history[later], axis=0)
    return -(corr_eps / (STEPS * SHOTS)), -(corr_sigma / (STEPS * SHOTS))
```

```python
import jax
import jax.numpy as jnp
from jax import lax
from jax.experimental import pallas as pl
from jax.experimental.pallas import tpu as pltpu
from jax.sharding import PartitionSpec as P

ROUND = 3
F32 = jnp.float32


def pair_swap(block, axis, first):
    route = []
    for i in range(first, lax.axis_size(axis) - 1, 2):
        route += [(i, i + 1), (i + 1, i)]
    return lax.ppermute(block, axis, route)


def exchange(inner, outer):
    got_outer = pair_swap(outer, "sub", 1)
    got_inner = pair_swap(inner, "sub", 0)
    return got_inner, got_outer


def shot_sum(x):
    n = lax.axis_size("shot")
    if n & (n - 1):
        return lax.psum(x, "shot")
    flip = 1
    while flip < n:
        x = x + lax.ppermute(x, "shot", [(i, i ^ flip) for i in range(n)])
        flip = 2 * flip + 1
    return x


def split_index(v, n):
    if n & (n - 1) == 0:
        return v & (n - 1), v >> (n.bit_length() - 1)
    return v % n, v // n


def ahead(u, axis):
    n = u.shape[axis]
    edge = lax.broadcasted_iota(jnp.int32, u.shape, axis) == n - 1
    return jnp.where(edge, 0.0, pltpu.roll(u, n - 1, axis))


def behind(u, axis):
    edge = lax.broadcasted_iota(jnp.int32, u.shape, axis) == 0
    return jnp.where(edge, 0.0, pltpu.roll(u, 1, axis))


def dfy(u):
    return ahead(u, 1) - u


def dfz(u):
    return ahead(u, 0) - u


def dby(u):
    return u - behind(u, 1)


def dbz(u):
    return u - behind(u, 0)


def h_step(h, e, e_next, keep=None, parts=(0, 1, 2)):
    ex, ey, ez = e
    new = {}
    if 0 in parts:
        new[0] = h[0] - 0.5 * (dfy(ez) - dfz(ey))
    ny, nz = e_next[1], e_next[2]
    if keep is not None:
        ny, nz = ny * keep, nz * keep
    new[1] = h[1] - 0.5 * (dfz(ex) - (nz - ez))
    new[2] = h[2] - 0.5 * ((ny - ey) - dfy(ex))
    return new


def e_step(e, h, h_prev, p, coef, inject, parts=(0, 1, 2)):
    ca, cb = coef[0], coef[1]
    new = {}
    for c in parts:
        if c == 0:
            curl = dby(h[2]) - dbz(h[1])
        elif c == 1:
            curl = dbz(h[0]) - (h[2] - h_prev[2])
        else:
            curl = (h[1] - h_prev[1]) - dby(h[0])
        new[c] = ca * e[c] + cb * (curl - p[c])
        if c == 1:
            new[c] = new[c] + inject
    return new


def p_step(p, e_new, coef):
    return {c: coef[2] * p[c] + coef[3] * e_new[c] for c in e_new}


class Planes:
    def __init__(self):
        self.at = {}

    def put(self, key, ref, *idx):
        self.at[key] = (ref, idx)

    def get(self, kind, c, i):
        ref, idx = self.at[kind, c, i]
        return ref[idx]

    def triple(self, kind, i, parts=(0, 1, 2)):
        return {c: self.get(kind, c, i) for c in parts}


def pick(even, a_ref, b_ref, k, low):
    a, b = a_ref[k], b_ref[k]
    return jnp.where(even, b, a) if low else jnp.where(even, a, b)


def emit(even, a_ref, b_ref, k, right, left):
    if right is None:
        right = left
    if left is None:
        left = right
    a_ref[k] = jnp.where(even, right, left)
    b_ref[k] = jnp.where(even, left, right)


def pre_steps(planes, coef_of, inject):
    h1, e1 = {}, {}
    last = planes.last
    sides = (0, 1, 2) if last <= 3 else (0, 1, last - 2, last - 1)
    for i in sides:
        e = [planes.get("E", c, i) for c in range(3)]
        nxt = {c: planes.get("E", c, i + 1) for c in (1, 2)}
        h1[i] = h_step(planes.triple("H", i), e, nxt)
    for i in (1, last - 1):
        parts = (0, 1, 2) if i == last - 1 else (1, 2)
        e1[i] = e_step(planes.triple("E", i), h1[i], h1[i - 1], planes.triple("P", i), coef_of(i), inject(i), parts)
    return h1, e1


def emit_state(even, planes, h1, e1, a_ref, b_ref, full):
    last = planes.last
    right = [planes.get("E", c, last) for c in range(3)]
    right += [h1[last - 1][1], h1[last - 1][2]] + [e1[last - 1][c] for c in range(3)]
    left = [planes.get("E", c, 0) for c in range(3)]
    left += [h1[0][c] for c in range(3)] + [e1[1][1], e1[1][2]]
    if full:
        right += [planes.get("P", c, last) for c in range(3)] + [planes.get("H", c, last) for c in range(3)]
        left += [planes.get("P", c, 0) for c in range(3)] + [None] * 3
    for k, (r, l) in enumerate(zip(right, left)):
        emit(even, a_ref, b_ref, k, r, l)


def own_planes(e_ref, h_ref, p_ref, h_at=0, p_at=0):
    planes = Planes()
    width = e_ref.shape[1]
    planes.last = width - 1
    for i in range(width):
        for c in range(3):
            planes.put(("E", c, i), e_ref, c, i)
            planes.put(("H", c, i), h_ref, c, i + h_at)
            planes.put(("P", c, i), p_ref, c, i + p_at)
    return planes


def source_map(cell_ref, sign_ref, mine, width, depth, span, full_x):
    flat = cell_ref[...]
    x, rest = split_index(flat, full_x)
    y, z = split_index(rest, span)
    row = (x - (mine * width - 1)) * depth + z
    rows = (width + 2) * depth
    n = flat.shape[1]
    hot = lax.broadcasted_iota(jnp.int32, (rows, n), 0) == row
    amp = (2 * sign_ref[...] - 1).astype(F32)
    where_y = lax.broadcasted_iota(jnp.int32, (span, n), 0) == y
    left = jnp.where(hot, 1.0, 0.0).astype(jnp.bfloat16)
    right = jnp.where(where_y, amp, 0.0).astype(jnp.bfloat16)
    return lax.dot_general(left, right, (((1,), (1,)), ((), ())), preferred_element_type=F32)


def first_kernel(full_x, meta, rate_t, strength_t, wavelet, e_ref, h_ref, p_ref, perm, cond, cls, cells, signs,
                 coef_ref, src_ref, a_ref, b_ref):
    even = meta[1] == 0
    width, depth, span = perm.shape
    src = source_map(cells, signs, meta[0], width, depth, span, full_x)
    src_ref[...] = src.reshape(width + 2, depth, span)
    for i in range(width):
        ratio = cond[i] / (2.0 * perm[i])
        coef_ref[0, i] = (1.0 - ratio) / (1.0 + ratio)
        coef_ref[1, i] = 0.5 / (perm[i] * (1.0 + ratio))
        kind = cls[i]
        rate = jnp.zeros((depth, span), F32)
        gain = jnp.zeros((depth, span), F32)
        for k in range(rate_t.shape[0]):
            rate = jnp.where(kind == k, rate_t[k], rate)
            gain = jnp.where(kind == k, (1.0 - rate_t[k]) * strength_t[k], gain)
        coef_ref[2, i] = rate
        coef_ref[3, i] = gain
    planes = own_planes(e_ref, h_ref, p_ref)
    h1, e1 = pre_steps(planes, lambda i: [coef_ref[k, i] for k in range(4)], lambda i: src_ref[i + 1] * wavelet[0])
    emit_state(even, planes, h1, e1, a_ref, b_ref, True)
    last = width - 1
    emit(even, a_ref, b_ref, 14, coef_ref[0, last], coef_ref[0, 0])
    emit(even, a_ref, b_ref, 15, coef_ref[1, last], coef_ref[1, 0])
    emit(even, a_ref, b_ref, 16, cls[last].astype(F32), cls[0].astype(F32))


def adjoint_first_kernel(meta, e_ref, h_ref, p_ref, coef_ref, a_ref, b_ref):
    planes = own_planes(e_ref, h_ref, p_ref)
    h1, e1 = pre_steps(planes, lambda i: [coef_ref[k, i] for k in range(4)], lambda i: 0.0)
    emit_state(meta[1] == 0, planes, h1, e1, a_ref, b_ref, True)


def receiver_kernel(meta, width, depth, got, maps_ref, acc):
    mine = meta[0]
    rows = (width + 2) * depth
    span = acc.shape[2]
    blocks, lists, n = got.shape
    steps = lists - 2
    acc[...] = jnp.zeros(acc.shape, F32)

    def block(b, carry):
        row = got[b, 0:1, :] - ((mine * width - 1) * depth).astype(F32)
        y = got[b, 1:2, :]
        hot = lax.broadcasted_iota(jnp.int32, (rows, n), 0).astype(F32) == row
        left = jnp.where(hot, 1.0, 0.0).astype(jnp.bfloat16)
        left3 = jnp.concatenate([left, left, left], axis=1)
        at_y = lax.broadcasted_iota(jnp.int32, (span, n), 0).astype(F32) == y
        one = jnp.where(at_y, 1.0, 0.0).astype(jnp.bfloat16)
        dims = (((1,), (1,)), ((), ()))
        acc[0] += lax.dot_general(left, one, dims, preferred_element_type=F32)
        for s in range(steps):
            v = got[b, 2 + s:3 + s, :]
            high = v.astype(jnp.bfloat16).astype(F32)
            mid = (v - high).astype(jnp.bfloat16).astype(F32)
            low = (v - high) - mid
            parts = [jnp.where(at_y, u, 0.0).astype(jnp.bfloat16) for u in (high, mid, low)]
            right = jnp.concatenate(parts, axis=1)
            acc[1 + s] += lax.dot_general(left3, right, dims, preferred_element_type=F32)
        return carry

    lax.fori_loop(0, blocks, block, 0)
    maps_ref[...] = acc[...].reshape(maps_ref.shape)


def round_body(planes, meta, coef_ref, coefh_ref, a_ref, b_ref, full, inject, first_extra, dest, prestep, seen):
    even = meta[1] == 0
    keep = jnp.where(meta[0] > 0, 1.0, 0.0).astype(F32)
    last = planes.last
    w = last + 1

    def low(k):
        return pick(even, a_ref, b_ref, k, True)

    def high(k):
        return pick(even, a_ref, b_ref, k, False)

    def coef_of(i):
        if i == -1:
            return [coefh_ref[0, k] for k in range(4)]
        if i == w:
            return [coefh_ref[1, k] for k in range(4)]
        return [coef_ref[k, i] for k in range(4)]

    held = {}
    for c in range(3):
        held["E", c, -1] = low(c)
        held["E", c, w] = high(c)
        held["H", c, w] = high(3 + c)
    held["H", 1, -2], held["H", 2, -2] = low(3), low(4)
    if full:
        for c in range(3):
            held["P", c, -1] = low(8 + c)
            held["H", c, -1] = low(11 + c)
            held["P", c, w] = high(8 + c)
    else:
        for i in (-1, w):
            cf = coef_of(i)
            for c in range(3):
                held["P", c, i] = cf[2] * planes.get("P", c, i) + cf[3] * held["E", c, i]

    def get(kind, c, i):
        if (kind, c, i) in held:
            return held[kind, c, i]
        return planes.get(kind, c, i)

    def store(kind, c, i, level, value):
        held.pop((kind, c, i), None)
        ref, idx = dest(kind, c, i, level)
        ref[idx] = value
        planes.put((kind, c, i), ref, *idx)

    for level in (1, 2, 3):
        if level == 2:
            for c in range(3):
                v = low(5 + c)
                if c == 1 and first_extra is not None:
                    v = v + first_extra(-2)
                held["E", c, -2] = v
            for c in (1, 2):
                v = high(5 + c)
                if c == 1 and first_extra is not None:
                    v = v + first_extra(w + 1)
                held["E", c, w + 1] = v
        h_lo = {1: -1, 2: -2, 3: -1}[level]
        h_hi = {1: last, 2: w, 3: last}[level]
        e_lo, e_hi = (0, last) if level == 3 else (-1, w)
        h_prev = None
        if h_lo > e_lo - 1:
            h_prev = {c: get("H", c, e_lo - 1) for c in (1, 2)}
        for i in range(h_lo, max(h_hi, e_hi) + 1):
            e = [get("E", c, i) for c in range(3)]
            if i <= h_hi:
                parts = (1, 2) if i == -2 else (0, 1, 2)
                h = h_step({c: get("H", c, i) for c in parts}, e, {c: get("E", c, i + 1) for c in (1, 2)},
                           keep if i == -1 else None, parts)
                for c in parts:
                    store("H", c, i, level, h[c])
            else:
                h = {c: get("H", c, i) for c in range(3)}
            if e_lo <= i <= e_hi:
                p = {c: get("P", c, i) for c in range(3)}
                cf = coef_of(i)
                new = e_step(e, h, h_prev, p, cf, inject(level, i))
                pn = p_step(p, new, cf)
                for c in range(3):
                    store("E", c, i, level, new[c])
                    store("P", c, i, level, pn[c])
                if seen is not None:
                    seen(level, i, new)
            h_prev = h
    if prestep is None:
        return
    h1, e1 = pre_steps(planes, coef_of, lambda i: inject(4, i))
    emit_state(even, planes, h1, e1, prestep[0], prestep[1], False)


def scratch_dest(es, hs, ps, own_e=None, width=4):
    def dest(kind, c, i, level):
        if kind == "E":
            if own_e is not None and 0 <= i < width:
                return own_e, (level - 1, c, i)
            return es, (c, i + 1)
        if kind == "H":
            return hs, (c, i + 2)
        return ps, (c, i + 1)

    return dest


def forward_one_kernel(meta, rate_t, strength_t, wavelet, e_ref, h_ref, p_ref, coef_ref, src_ref, a_ref, b_ref,
                       hist_ref, hs_ref, ps_ref, coefh_ref, eyh_ref, oa_ref, ob_ref, es_ref):
    even = meta[1] == 0
    width = e_ref.shape[1]
    for side in (0, 1):
        coefh_ref[side, 0] = pick(even, a_ref, b_ref, 14, side == 0)
        coefh_ref[side, 1] = pick(even, a_ref, b_ref, 15, side == 0)
        kind = pick(even, a_ref, b_ref, 16, side == 0)
        rate = jnp.zeros(kind.shape, F32)
        gain = jnp.zeros(kind.shape, F32)
        for k in range(rate_t.shape[0]):
            rate = jnp.where(kind == float(k), rate_t[k], rate)
            gain = jnp.where(kind == float(k), (1.0 - rate_t[k]) * strength_t[k], gain)
        coefh_ref[side, 2] = rate
        coefh_ref[side, 3] = gain
    planes = own_planes(e_ref, h_ref, p_ref)

    def seen(level, i, e):
        if level == 2 and i in (-1, width):
            eyh_ref[0 if i < 0 else 1] = e[1]

    round_body(planes, meta, coef_ref, coefh_ref, a_ref, b_ref, True,
               lambda level, i: src_ref[i + 1] * wavelet[level - 1], None,
               scratch_dest(es_ref, hs_ref, ps_ref, hist_ref, width), (oa_ref, ob_ref), seen)


def state_planes(e_ref, hs_ref, ps_ref, level=None):
    planes = Planes()
    width = e_ref.shape[-3]
    planes.last = width - 1
    for c in range(3):
        for i in range(width):
            if level is None:
                planes.put(("E", c, i), e_ref, c, i + 0)
            else:
                planes.put(("E", c, i), e_ref, level, c, i)
        for i in range(-1, width):
            planes.put(("H", c, i), hs_ref, c, i + 2)
        for i in range(-1, width + 1):
            planes.put(("P", c, i), ps_ref, c, i + 1)
    return planes


def forward_two_kernel(meta, wavelet, hist_in, hs_in, ps_in, coef_ref, coefh_ref, src_ref, maps_ref, a_ref, b_ref,
                       hist_ref, eyh_ref, oa_ref, ob_ref, es_ref, hs_ref, ps_ref):
    even = meta[1] == 0
    width = hist_in.shape[2]
    planes = state_planes(hist_in, hs_in, ps_in, 2)
    eyh_ref[0] = pick(even, a_ref, b_ref, 1, True)
    eyh_ref[1] = pick(even, a_ref, b_ref, 1, False)

    def seen(level, i, e):
        if level == 2 and i in (-1, width):
            eyh_ref[2 if i < 0 else 3] = e[1]

    round_body(planes, meta, coef_ref, coefh_ref, a_ref, b_ref, False,
               lambda level, i: src_ref[i + 1] * wavelet[ROUND + level - 1], None,
               scratch_dest(es_ref, hs_ref, ps_ref, hist_ref, width), None, seen)
    steps = 2 * ROUND

    def resid(i):
        return maps_ref[0, i + 1] * hist_ref[2, 1, i] - maps_ref[steps, i + 1]

    last = width - 1
    emit(even, oa_ref, ob_ref, 0, resid(last), resid(0))
    emit(even, oa_ref, ob_ref, 1, resid(last - 1), resid(1))


def correlate(corr_ref, i, b, now, prev, add):
    eps = b[0] * (now[0] - prev[0]) + b[1] * (now[1] - prev[1]) + b[2] * (now[2] - prev[2])
    sig = b[0] * now[0] + b[1] * now[1] + b[2] * now[2]
    if add is not None:
        eps, sig = eps + add[0, i], sig + add[1, i]
    corr_ref[0, i] = eps
    corr_ref[1, i] = sig


def adjoint_one_kernel(meta, e_ref, h_ref, p_ref, coef_ref, coefh_ref, maps_ref, hist1_ref, hist2_ref, eyh_ref,
                       a_ref, b_ref, ra_ref, rb_ref, e_out, hs_ref, ps_ref, corr_ref, oa_ref, ob_ref, es_ref):
    even = meta[1] == 0
    width = e_ref.shape[1]
    steps = 2 * ROUND
    planes = own_planes(e_ref, h_ref, p_ref)

    def ey(n, i):
        if 0 <= i < width:
            return hist1_ref[n - 1, 1, i] if n <= ROUND else hist2_ref[n - 1 - ROUND, 1, i]
        at = {3: 0, 5: 2}[n]
        return eyh_ref[at if i < 0 else at + 1]

    def extra(i):
        if i < 0:
            return pick(even, ra_ref, rb_ref, -1 - i, True)
        return pick(even, ra_ref, rb_ref, i - width, False)

    def inject(level, i):
        n = steps + 1 - level
        if n == steps and not 0 <= i < width:
            return extra(i)
        return maps_ref[0, i + 1] * ey(n, i) - maps_ref[n, i + 1]

    def seen(level, i, e):
        if not 0 <= i < width:
            return
        n = steps + 1 - level
        now = [hist2_ref[n - 1 - ROUND, c, i] for c in range(3)]
        prev = [hist2_ref[n - 2 - ROUND, c, i] if n - 1 > ROUND else hist1_ref[n - 2, c, i] for c in range(3)]
        correlate(corr_ref, i, e, now, prev, corr_ref if level > 1 else None)

    def dest(kind, c, i, level):
        if kind == "E":
            if 0 <= i < width:
                return e_out, (c, i)
            return es_ref, (c, i + 1)
        if kind == "H":
            return hs_ref, (c, i + 2)
        return ps_ref, (c, i + 1)

    round_body(planes, meta, coef_ref, coefh_ref, a_ref, b_ref, True, inject, extra, dest, (oa_ref, ob_ref), seen)


def adjoint_two_kernel(meta, e_ref, hs_in, ps_in, coef_ref, coefh_ref, maps_ref, e0_ref, hist1_ref, ey2_ref, eyh_ref,
                       corr_in, a_ref, b_ref, corr_ref, es_ref, hs_ref, ps_ref):
    width = e_ref.shape[1]
    steps = 2 * ROUND
    planes = state_planes(e_ref, hs_in, ps_in)

    def ey(n, i):
        if 0 <= i < width:
            return hist1_ref[n - 1, 1, i]
        if n == 3:
            return eyh_ref[0 if i < 0 else 1]
        return ey2_ref[0 if i < 0 else 1]

    def inject(level, i):
        n = steps + 1 - ROUND - level
        return maps_ref[0, i + 1] * ey(n, i) - maps_ref[n, i + 1]

    def seen(level, i, e):
        if not 0 <= i < width:
            return
        n = steps + 1 - ROUND - level
        now = [hist1_ref[n - 1, c, i] for c in range(3)]
        prev = [hist1_ref[n - 2, c, i] if n > 1 else e0_ref[c, i] for c in range(3)]
        correlate(corr_ref, i, e, now, prev, corr_ref if level > 1 else corr_in)

    round_body(planes, meta, coef_ref, coefh_ref, a_ref, b_ref, False, inject, None,
               scratch_dest(es_ref, hs_ref, ps_ref), None, seen)


def call(body, name, inputs, scalars, outs, scratch=()):
    smem = pl.BlockSpec(memory_space=pltpu.SMEM)
    vmem = pl.BlockSpec(memory_space=pltpu.VMEM)
    return pl.pallas_call(
        body,
        name=name,
        out_shape=[jax.ShapeDtypeStruct(s, F32) for s in outs],
        in_specs=[smem] * len(scalars) + [vmem] * len(inputs),
        out_specs=[vmem] * len(outs),
        scratch_shapes=[pltpu.VMEM(s, F32) for s in scratch],
        compiler_params=pltpu.CompilerParams(vmem_limit_bytes=48 * 1024 * 1024),
    )(*scalars, *inputs)


def per_device(
    electric,
    magnetic,
    polar,
    adj_electric,
    adj_magnetic,
    adj_polar,
    permittivity,
    conductivity,
    debye_class,
    debye_rate,
    debye_strength,
    wavelet,
    src_cell,
    src_sign,
    rec_owner,
    rec_pos,
    observed,
):
    width, depth, span = permittivity.shape
    steps = wavelet.shape[0]
    nsub = lax.axis_size("sub")
    nshot = lax.axis_size("shot")
    mine = lax.axis_index("sub")
    meta = jnp.stack([mine, mine % 2]).astype(jnp.int32)
    plane = (depth, span)

    in_x, rest = split_index(rec_pos[0], width)
    rec_y, rec_z = split_index(rest, span)
    rec_row = (rec_owner[0, :, 0] * width + in_x) * depth + rec_z
    listed = jnp.concatenate([rec_row[None].astype(F32), rec_y[None].astype(F32), observed[0]], axis=0)
    got = lax.all_gather(listed, "sub")

    fields = (electric[0], magnetic[0], polar[0])
    adjoint = (adj_electric[0], adj_magnetic[0], adj_polar[0])

    coef, src, a1, b1 = call(
        lambda *refs: first_kernel(width * nsub, *refs),
        "first",
        [*fields, permittivity, conductivity, debye_class, src_cell, src_sign],
        [meta, debye_rate, debye_strength, wavelet],
        [(4, width, *plane), (width + 2, *plane), (17, *plane), (17, *plane)],
    )
    got_a1, got_b1 = exchange(a1, b1)
    a3, b3 = call(adjoint_first_kernel, "adjoint_first", [*adjoint, coef], [meta], [(14, *plane), (14, *plane)])
    (maps,) = call(
        lambda meta_ref, *refs: receiver_kernel(meta_ref, width, depth, *refs),
        "receivers",
        [got],
        [meta],
        [(steps + 1, width + 2, *plane)],
        [(steps + 1, (width + 2) * depth, span)],
    )
    e_sh, h_sh, p_sh = (3, width + 2, *plane), (3, width + 3, *plane), (3, width + 2, *plane)
    hist1, hs, ps, coefh, ey2, a2, b2 = call(
        forward_one_kernel,
        "forward_one",
        [*fields, coef, src, got_a1, got_b1],
        [meta, debye_rate, debye_strength, wavelet],
        [(ROUND, 3, width, *plane), h_sh, p_sh, (2, 4, *plane), (2, *plane), (8, *plane), (8, *plane)],
        [e_sh],
    )
    got_a2, got_b2 = exchange(a2, b2)
    got_a3, got_b3 = exchange(a3, b3)
    hist2, eyh, a4, b4 = call(
        forward_two_kernel,
        "forward_two",
        [hist1, hs, ps, coef, coefh, src, maps, got_a2, got_b2],
        [meta, wavelet],
        [(ROUND, 3, width, *plane), (4, *plane), (2, *plane), (2, *plane)],
        [e_sh, h_sh, p_sh],
    )
    got_a4, got_b4 = exchange(a4, b4)
    e_adj, hs, ps, corr, a5, b5 = call(
        adjoint_one_kernel,
        "adjoint_one",
        [*adjoint, coef, coefh, maps, hist1, hist2, eyh, got_a3, got_b3, got_a4, got_b4],
        [meta],
        [(3, width, *plane), h_sh, p_sh, (2, width, *plane), (8, *plane), (8, *plane)],
        [e_sh],
    )
    got_a5, got_b5 = exchange(a5, b5)
    (corr,) = call(
        adjoint_two_kernel,
        "adjoint_two",
        [e_adj, hs, ps, coef, coefh, maps, fields[0], hist1, ey2, eyh, corr, got_a5, got_b5],
        [meta],
        [(2, width, *plane)],
        [e_sh, h_sh, p_sh],
    )
    total = shot_sum(corr)
    return (-(total[0] / (steps * nshot)), -(total[1] / (steps * nshot)))


def solution(mesh):
    in_specs = (
        P("shot", None, "sub", None, None),
        P("shot", None, "sub", None, None),
        P("shot", None, "sub", None, None),
        P("shot", None, "sub", None, None),
        P("shot", None, "sub", None, None),
        P("shot", None, "sub", None, None),
        P("sub", None, None),
        P("sub", None, None),
        P("sub", None, None),
        P(),
        P(),
        P(),
        P("shot", None),
        P("shot", None),
        P("shot", "sub", None),
        P("shot", "sub"),
        P("shot", None, "sub"),
    )
    out_specs = (P("sub", None, None), P("sub", None, None))
    return jax.shard_map(
        per_device, mesh=mesh, in_specs=in_specs, out_specs=out_specs, check_vma=False
    )
```

```python
import jax
import jax.numpy as jnp
from jax import lax
from jax.experimental import pallas as pl
from jax.experimental.pallas import tpu as pltpu
from jax.sharding import PartitionSpec as P

ROUND = 3
F32 = jnp.float32


def pair_swap(block, axis, first):
    route = []
    for i in range(first, lax.axis_size(axis) - 1, 2):
        route += [(i, i + 1), (i + 1, i)]
    return lax.ppermute(block, axis, route)


def exchange(inner, outer):
    got_outer = pair_swap(outer, "sub", 1)
    got_inner = pair_swap(inner, "sub", 0)
    return got_inner, got_outer


def shot_sum(x):
    n = lax.axis_size("shot")
    if n & (n - 1):
        return lax.psum(x, "shot")
    flip = 1
    while flip < n:
        x = x + lax.ppermute(x, "shot", [(i, i ^ flip) for i in range(n)])
        flip = 2 * flip + 1
    return x


def split_index(v, n):
    if n & (n - 1) == 0:
        return v & (n - 1), v >> (n.bit_length() - 1)
    return v % n, v // n


def ahead(u, axis):
    n = u.shape[axis]
    edge = lax.broadcasted_iota(jnp.int32, u.shape, axis) == n - 1
    return jnp.where(edge, 0.0, pltpu.roll(u, n - 1, axis))


def behind(u, axis):
    edge = lax.broadcasted_iota(jnp.int32, u.shape, axis) == 0
    return jnp.where(edge, 0.0, pltpu.roll(u, 1, axis))


def dfy(u):
    return ahead(u, 1) - u


def dfz(u):
    return ahead(u, 0) - u


def dby(u):
    return u - behind(u, 1)


def dbz(u):
    return u - behind(u, 0)


def h_step(h, e, e_next, keep=None, parts=(0, 1, 2)):
    ex, ey, ez = e
    new = {}
    if 0 in parts:
        new[0] = h[0] - 0.5 * (dfy(ez) - dfz(ey))
    ny, nz = e_next[1], e_next[2]
    if keep is not None:
        ny, nz = ny * keep, nz * keep
    new[1] = h[1] - 0.5 * (dfz(ex) - (nz - ez))
    new[2] = h[2] - 0.5 * ((ny - ey) - dfy(ex))
    return new


def e_step(e, h, h_prev, p, coef, inject, parts=(0, 1, 2)):
    ca, cb = coef[0], coef[1]
    new = {}
    for c in parts:
        if c == 0:
            curl = dby(h[2]) - dbz(h[1])
        elif c == 1:
            curl = dbz(h[0]) - (h[2] - h_prev[2])
        else:
            curl = (h[1] - h_prev[1]) - dby(h[0])
        new[c] = ca * e[c] + cb * (curl - p[c])
        if c == 1:
            new[c] = new[c] + inject
    return new


def p_step(p, e_new, coef):
    return {c: coef[2] * p[c] + coef[3] * e_new[c] for c in e_new}


class Planes:
    def __init__(self):
        self.at = {}

    def put(self, key, ref, *idx):
        self.at[key] = (ref, idx)

    def get(self, kind, c, i):
        ref, idx = self.at[kind, c, i]
        return ref[idx]

    def triple(self, kind, i, parts=(0, 1, 2)):
        return {c: self.get(kind, c, i) for c in parts}


def pick(even, a_ref, b_ref, k, low):
    a, b = a_ref[k], b_ref[k]
    return jnp.where(even, b, a) if low else jnp.where(even, a, b)


def emit(even, a_ref, b_ref, k, right, left):
    if right is None:
        right = left
    if left is None:
        left = right
    a_ref[k] = jnp.where(even, right, left)
    b_ref[k] = jnp.where(even, left, right)


def pre_steps(planes, coef_of, inject):
    h1, e1 = {}, {}
    last = planes.last
    sides = (0, 1, 2) if last <= 3 else (0, 1, last - 2, last - 1)
    for i in sides:
        e = [planes.get("E", c, i) for c in range(3)]
        nxt = {c: planes.get("E", c, i + 1) for c in (1, 2)}
        h1[i] = h_step(planes.triple("H", i), e, nxt)
    for i in (1, last - 1):
        parts = (0, 1, 2) if i == last - 1 else (1, 2)
        e1[i] = e_step(planes.triple("E", i), h1[i], h1[i - 1], planes.triple("P", i), coef_of(i), inject(i), parts)
    return h1, e1


def emit_state(even, planes, h1, e1, a_ref, b_ref, full):
    last = planes.last
    right = [planes.get("E", c, last) for c in range(3)]
    right += [h1[last - 1][1], h1[last - 1][2]] + [e1[last - 1][c] for c in range(3)]
    left = [planes.get("E", c, 0) for c in range(3)]
    left += [h1[0][c] for c in range(3)] + [e1[1][1], e1[1][2]]
    if full:
        right += [planes.get("P", c, last) for c in range(3)] + [planes.get("H", c, last) for c in range(3)]
        left += [planes.get("P", c, 0) for c in range(3)] + [None] * 3
    for k, (r, l) in enumerate(zip(right, left)):
        emit(even, a_ref, b_ref, k, r, l)


def own_planes(e_ref, h_ref, p_ref, h_at=0, p_at=0):
    planes = Planes()
    width = e_ref.shape[1]
    planes.last = width - 1
    for i in range(width):
        for c in range(3):
            planes.put(("E", c, i), e_ref, c, i)
            planes.put(("H", c, i), h_ref, c, i + h_at)
            planes.put(("P", c, i), p_ref, c, i + p_at)
    return planes


def source_map(cell_ref, sign_ref, mine, width, depth, span, full_x):
    flat = cell_ref[...]
    x, rest = split_index(flat, full_x)
    y, z = split_index(rest, span)
    row = (x - (mine * width - 1)) * depth + z
    rows = (width + 2) * depth
    n = flat.shape[1]
    hot = lax.broadcasted_iota(jnp.int32, (rows, n), 0) == row
    amp = (2 * sign_ref[...] - 1).astype(F32)
    where_y = lax.broadcasted_iota(jnp.int32, (span, n), 0) == y
    left = jnp.where(hot, 1.0, 0.0).astype(jnp.bfloat16)
    right = jnp.where(where_y, amp, 0.0).astype(jnp.bfloat16)
    return lax.dot_general(left, right, (((1,), (1,)), ((), ())), preferred_element_type=F32)


def first_kernel(full_x, meta, rate_t, strength_t, wavelet, e_in, h_in, p_in, perm_in, cond_in, cls_in, cells, signs,
                 e_ref, h_ref, p_ref, coef_ref, src_ref, a_ref, b_ref, perm, cond, cls, sems):
    even = meta[1] == 0
    width, depth, span = perm.shape
    moves = [(perm_in, perm), (cond_in, cond), (cls_in, cls), (e_in, e_ref), (h_in, h_ref), (p_in, p_ref)]
    copies = [pltpu.make_async_copy(a, b, sems.at[k]) for k, (a, b) in enumerate(moves)]
    for copy in copies:
        copy.start()
    src = source_map(cells, signs, meta[0], width, depth, span, full_x)
    src_ref[...] = src.reshape(width + 2, depth, span)
    for copy in copies[:3]:
        copy.wait()
    for i in range(width):
        ratio = cond[i] / (2.0 * perm[i])
        coef_ref[0, i] = (1.0 - ratio) / (1.0 + ratio)
        coef_ref[1, i] = 0.5 / (perm[i] * (1.0 + ratio))
        kind = cls[i]
        rate = jnp.zeros((depth, span), F32)
        gain = jnp.zeros((depth, span), F32)
        for k in range(rate_t.shape[0]):
            rate = jnp.where(kind == k, rate_t[k], rate)
            gain = jnp.where(kind == k, (1.0 - rate_t[k]) * strength_t[k], gain)
        coef_ref[2, i] = rate
        coef_ref[3, i] = gain
    for copy in copies[3:]:
        copy.wait()
    planes = own_planes(e_ref, h_ref, p_ref)
    h1, e1 = pre_steps(planes, lambda i: [coef_ref[k, i] for k in range(4)], lambda i: src_ref[i + 1] * wavelet[0])
    emit_state(even, planes, h1, e1, a_ref, b_ref, True)
    last = width - 1
    emit(even, a_ref, b_ref, 14, coef_ref[0, last], coef_ref[0, 0])
    emit(even, a_ref, b_ref, 15, coef_ref[1, last], coef_ref[1, 0])
    emit(even, a_ref, b_ref, 16, cls[last].astype(F32), cls[0].astype(F32))


def adjoint_first_kernel(meta, e_ref, h_ref, p_ref, coef_ref, a_ref, b_ref):
    planes = own_planes(e_ref, h_ref, p_ref)
    h1, e1 = pre_steps(planes, lambda i: [coef_ref[k, i] for k in range(4)], lambda i: 0.0)
    emit_state(meta[1] == 0, planes, h1, e1, a_ref, b_ref, True)


def receiver_kernel(width, depth, meta, got, maps_ref, acc):
    mine = meta[0]
    rows = (width + 2) * depth
    span = acc.shape[1]
    blocks, lists, n = got.shape
    steps = lists - 2
    acc[...] = jnp.zeros(acc.shape, F32)
    first_row = ((mine * width - 1) * depth).astype(F32)
    row_at = lax.broadcasted_iota(jnp.int32, (rows, n), 0).astype(F32)
    y_at = lax.broadcasted_iota(jnp.int32, (span, n), 0).astype(F32)

    def block(b, carry):
        hot = row_at == got[b, 0:1, :] - first_row
        at_y = jnp.where(y_at == got[b, 1:2, :], 1.0, 0.0).astype(jnp.bfloat16)
        zero = jnp.zeros((rows, n), jnp.bfloat16)
        left = [jnp.concatenate([jnp.where(hot, 1.0, 0.0).astype(jnp.bfloat16), zero, zero], axis=1)]
        for s in range(steps):
            v = got[b, 2 + s:3 + s, :]
            high = v.astype(jnp.bfloat16).astype(F32)
            mid = (v - high).astype(jnp.bfloat16).astype(F32)
            low = (v - high) - mid
            parts = [jnp.where(hot, u, 0.0).astype(jnp.bfloat16) for u in (high, mid, low)]
            left.append(jnp.concatenate(parts, axis=1))
        acc[...] += lax.dot_general(
            jnp.concatenate(left, axis=0),
            jnp.concatenate([at_y, at_y, at_y], axis=1),
            (((1,), (1,)), ((), ())),
            preferred_element_type=F32,
        )
        return carry

    lax.fori_loop(0, blocks, block, 0)
    maps_ref[...] = acc[...].reshape(maps_ref.shape)


def round_body(planes, meta, coef_ref, coefh_ref, a_ref, b_ref, full, inject, first_extra, dest, prestep, seen):
    even = meta[1] == 0
    keep = jnp.where(meta[0] > 0, 1.0, 0.0).astype(F32)
    last = planes.last
    w = last + 1

    def low(k):
        return pick(even, a_ref, b_ref, k, True)

    def high(k):
        return pick(even, a_ref, b_ref, k, False)

    def coef_of(i):
        if i == -1:
            return [coefh_ref[0, k] for k in range(4)]
        if i == w:
            return [coefh_ref[1, k] for k in range(4)]
        return [coef_ref[k, i] for k in range(4)]

    held = {}
    for c in range(3):
        held["E", c, -1] = low(c)
        held["E", c, w] = high(c)
        held["H", c, w] = high(3 + c)
    held["H", 1, -2], held["H", 2, -2] = low(3), low(4)
    if full:
        for c in range(3):
            held["P", c, -1] = low(8 + c)
            held["H", c, -1] = low(11 + c)
            held["P", c, w] = high(8 + c)
    else:
        for i in (-1, w):
            cf = coef_of(i)
            for c in range(3):
                held["P", c, i] = cf[2] * planes.get("P", c, i) + cf[3] * held["E", c, i]

    def get(kind, c, i):
        if (kind, c, i) in held:
            return held[kind, c, i]
        return planes.get(kind, c, i)

    def store(kind, c, i, level, value):
        held.pop((kind, c, i), None)
        ref, idx = dest(kind, c, i, level)
        ref[idx] = value
        planes.put((kind, c, i), ref, *idx)

    for level in (1, 2, 3):
        if level == 2:
            for c in range(3):
                v = low(5 + c)
                if c == 1 and first_extra is not None:
                    v = v + first_extra(-2)
                held["E", c, -2] = v
            for c in (1, 2):
                v = high(5 + c)
                if c == 1 and first_extra is not None:
                    v = v + first_extra(w + 1)
                held["E", c, w + 1] = v
        h_lo = {1: -1, 2: -2, 3: -1}[level]
        h_hi = {1: last, 2: w, 3: last}[level]
        e_lo, e_hi = (0, last) if level == 3 else (-1, w)
        h_prev = None
        if h_lo > e_lo - 1:
            h_prev = {c: get("H", c, e_lo - 1) for c in (1, 2)}
        for i in range(h_lo, max(h_hi, e_hi) + 1):
            e = [get("E", c, i) for c in range(3)]
            if i <= h_hi:
                parts = (1, 2) if i == -2 else (0, 1, 2)
                h = h_step({c: get("H", c, i) for c in parts}, e, {c: get("E", c, i + 1) for c in (1, 2)},
                           keep if i == -1 else None, parts)
                for c in parts:
                    store("H", c, i, level, h[c])
            else:
                h = {c: get("H", c, i) for c in range(3)}
            if e_lo <= i <= e_hi:
                p = {c: get("P", c, i) for c in range(3)}
                cf = coef_of(i)
                new = e_step(e, h, h_prev, p, cf, inject(level, i))
                pn = p_step(p, new, cf)
                for c in range(3):
                    store("E", c, i, level, new[c])
                    store("P", c, i, level, pn[c])
                if seen is not None:
                    seen(level, i, new)
            h_prev = h
    if prestep is None:
        return
    h1, e1 = pre_steps(planes, coef_of, lambda i: inject(4, i))
    emit_state(even, planes, h1, e1, prestep[0], prestep[1], False)


def scratch_dest(es, hs, ps, own_e=None, width=4):
    def dest(kind, c, i, level):
        if kind == "E":
            if own_e is not None and 0 <= i < width:
                return own_e, (level - 1, c, i)
            return es, (c, i + 1)
        if kind == "H":
            return hs, (c, i + 2)
        return ps, (c, i + 1)

    return dest


def forward_one_kernel(meta, rate_t, strength_t, wavelet, e_ref, h_ref, p_ref, coef_ref, src_ref, a_ref, b_ref,
                       hist_ref, hs_ref, ps_ref, coefh_ref, eyh_ref, oa_ref, ob_ref, es_ref):
    even = meta[1] == 0
    width = e_ref.shape[1]
    for side in (0, 1):
        coefh_ref[side, 0] = pick(even, a_ref, b_ref, 14, side == 0)
        coefh_ref[side, 1] = pick(even, a_ref, b_ref, 15, side == 0)
        kind = pick(even, a_ref, b_ref, 16, side == 0)
        rate = jnp.zeros(kind.shape, F32)
        gain = jnp.zeros(kind.shape, F32)
        for k in range(rate_t.shape[0]):
            rate = jnp.where(kind == float(k), rate_t[k], rate)
            gain = jnp.where(kind == float(k), (1.0 - rate_t[k]) * strength_t[k], gain)
        coefh_ref[side, 2] = rate
        coefh_ref[side, 3] = gain
    planes = own_planes(e_ref, h_ref, p_ref)

    def seen(level, i, e):
        if level == 2 and i in (-1, width):
            eyh_ref[0 if i < 0 else 1] = e[1]

    round_body(planes, meta, coef_ref, coefh_ref, a_ref, b_ref, True,
               lambda level, i: src_ref[i + 1] * wavelet[level - 1], None,
               scratch_dest(es_ref, hs_ref, ps_ref, hist_ref, width), (oa_ref, ob_ref), seen)


def state_planes(e_ref, hs_ref, ps_ref, level=None):
    planes = Planes()
    width = e_ref.shape[-3]
    planes.last = width - 1
    for c in range(3):
        for i in range(width):
            if level is None:
                planes.put(("E", c, i), e_ref, c, i + 0)
            else:
                planes.put(("E", c, i), e_ref, level, c, i)
        for i in range(-1, width):
            planes.put(("H", c, i), hs_ref, c, i + 2)
        for i in range(-1, width + 1):
            planes.put(("P", c, i), ps_ref, c, i + 1)
    return planes


def forward_two_kernel(meta, wavelet, hist_in, hs_in, ps_in, coef_ref, coefh_ref, src_ref, maps_ref, a_ref, b_ref,
                       hist_ref, eyh_ref, oa_ref, ob_ref, es_ref, hs_ref, ps_ref):
    even = meta[1] == 0
    width = hist_in.shape[2]
    planes = state_planes(hist_in, hs_in, ps_in, 2)
    eyh_ref[0] = pick(even, a_ref, b_ref, 1, True)
    eyh_ref[1] = pick(even, a_ref, b_ref, 1, False)

    def seen(level, i, e):
        if level == 2 and i in (-1, width):
            eyh_ref[2 if i < 0 else 3] = e[1]

    round_body(planes, meta, coef_ref, coefh_ref, a_ref, b_ref, False,
               lambda level, i: src_ref[i + 1] * wavelet[ROUND + level - 1], None,
               scratch_dest(es_ref, hs_ref, ps_ref, hist_ref, width), None, seen)
    steps = 2 * ROUND

    def resid(i):
        return maps_ref[0, i + 1] * hist_ref[2, 1, i] - maps_ref[steps, i + 1]

    last = width - 1
    emit(even, oa_ref, ob_ref, 0, resid(last), resid(0))
    emit(even, oa_ref, ob_ref, 1, resid(last - 1), resid(1))


def correlate(corr_ref, i, b, now, prev, add):
    eps = b[0] * (now[0] - prev[0]) + b[1] * (now[1] - prev[1]) + b[2] * (now[2] - prev[2])
    sig = b[0] * now[0] + b[1] * now[1] + b[2] * now[2]
    if add is not None:
        eps, sig = eps + add[0, i], sig + add[1, i]
    corr_ref[0, i] = eps
    corr_ref[1, i] = sig


def adjoint_one_kernel(meta, e_ref, h_ref, p_ref, coef_ref, coefh_ref, maps_ref, hist1_ref, hist2_ref, eyh_ref,
                       a_ref, b_ref, ra_ref, rb_ref, e_out, hs_ref, ps_ref, corr_ref, oa_ref, ob_ref, es_ref):
    even = meta[1] == 0
    width = e_ref.shape[1]
    steps = 2 * ROUND
    planes = own_planes(e_ref, h_ref, p_ref)

    def ey(n, i):
        if 0 <= i < width:
            return hist1_ref[n - 1, 1, i] if n <= ROUND else hist2_ref[n - 1 - ROUND, 1, i]
        at = {3: 0, 5: 2}[n]
        return eyh_ref[at if i < 0 else at + 1]

    def extra(i):
        if i < 0:
            return pick(even, ra_ref, rb_ref, -1 - i, True)
        return pick(even, ra_ref, rb_ref, i - width, False)

    def inject(level, i):
        n = steps + 1 - level
        if n == steps and not 0 <= i < width:
            return extra(i)
        return maps_ref[0, i + 1] * ey(n, i) - maps_ref[n, i + 1]

    def seen(level, i, e):
        if not 0 <= i < width:
            return
        n = steps + 1 - level
        now = [hist2_ref[n - 1 - ROUND, c, i] for c in range(3)]
        prev = [hist2_ref[n - 2 - ROUND, c, i] if n - 1 > ROUND else hist1_ref[n - 2, c, i] for c in range(3)]
        correlate(corr_ref, i, e, now, prev, corr_ref if level > 1 else None)

    def dest(kind, c, i, level):
        if kind == "E":
            if 0 <= i < width:
                return e_out, (c, i)
            return es_ref, (c, i + 1)
        if kind == "H":
            return hs_ref, (c, i + 2)
        return ps_ref, (c, i + 1)

    round_body(planes, meta, coef_ref, coefh_ref, a_ref, b_ref, True, inject, extra, dest, (oa_ref, ob_ref), seen)


def adjoint_two_kernel(meta, e_ref, hs_in, ps_in, coef_ref, coefh_ref, maps_ref, e0_ref, hist1_ref, ey2_ref, eyh_ref,
                       corr_in, a_ref, b_ref, corr_ref, es_ref, hs_ref, ps_ref):
    width = e_ref.shape[1]
    steps = 2 * ROUND
    planes = state_planes(e_ref, hs_in, ps_in)

    def ey(n, i):
        if 0 <= i < width:
            return hist1_ref[n - 1, 1, i]
        if n == 3:
            return eyh_ref[0 if i < 0 else 1]
        return ey2_ref[0 if i < 0 else 1]

    def inject(level, i):
        n = steps + 1 - ROUND - level
        return maps_ref[0, i + 1] * ey(n, i) - maps_ref[n, i + 1]

    def seen(level, i, e):
        if not 0 <= i < width:
            return
        n = steps + 1 - ROUND - level
        now = [hist1_ref[n - 1, c, i] for c in range(3)]
        prev = [hist1_ref[n - 2, c, i] if n > 1 else e0_ref[c, i] for c in range(3)]
        correlate(corr_ref, i, e, now, prev, corr_ref if level > 1 else corr_in)

    round_body(planes, meta, coef_ref, coefh_ref, a_ref, b_ref, False, inject, None,
               scratch_dest(es_ref, hs_ref, ps_ref), None, seen)


def call(body, name, inputs, scalars, outs, scratch=(), remote=0, work=10**10):
    smem = pl.BlockSpec(memory_space=pltpu.SMEM)
    vmem = pl.BlockSpec(memory_space=pltpu.VMEM)
    stay = pl.BlockSpec(memory_space=pltpu.HBM)
    return pl.pallas_call(
        body,
        name=name,
        out_shape=[jax.ShapeDtypeStruct(s, F32) for s in outs],
        in_specs=[smem] * len(scalars) + [stay] * remote + [vmem] * (len(inputs) - remote),
        out_specs=[vmem] * len(outs),
        scratch_shapes=[s if not isinstance(s, tuple) else pltpu.VMEM(s, F32) for s in scratch],
        cost_estimate=pl.CostEstimate(flops=work, transcendentals=0, bytes_accessed=0),
        compiler_params=pltpu.CompilerParams(vmem_limit_bytes=48 * 1024 * 1024),
    )(*scalars, *[pltpu.with_memory_space_constraint(x, pltpu.HBM) for x in inputs[:remote]], *inputs[remote:])


def per_device(
    electric,
    magnetic,
    polar,
    adj_electric,
    adj_magnetic,
    adj_polar,
    permittivity,
    conductivity,
    debye_class,
    debye_rate,
    debye_strength,
    wavelet,
    src_cell,
    src_sign,
    rec_owner,
    rec_pos,
    observed,
):
    width, depth, span = permittivity.shape
    steps = wavelet.shape[0]
    nsub = lax.axis_size("sub")
    nshot = lax.axis_size("shot")
    mine = lax.axis_index("sub")
    meta = jnp.stack([mine, mine % 2]).astype(jnp.int32)
    plane = (depth, span)

    in_x, rest = split_index(rec_pos[0], width)
    rec_y, rec_z = split_index(rest, span)
    rec_row = (rec_owner[0, :, 0] * width + in_x) * depth + rec_z
    listed = jnp.concatenate([rec_row[None].astype(F32), rec_y[None].astype(F32), observed[0]], axis=0)
    fields = (electric[0], magnetic[0], polar[0])
    adjoint = (adj_electric[0], adj_magnetic[0], adj_polar[0])

    own = (3, width, *plane)
    *fields, coef, src, a1, b1 = call(
        lambda *refs: first_kernel(width * nsub, *refs),
        "first",
        [*fields, permittivity, conductivity, debye_class, src_cell, src_sign],
        [meta, debye_rate, debye_strength, wavelet],
        [own, own, own, (4, width, *plane), (width + 2, *plane), (17, *plane), (17, *plane)],
        [
            (width, *plane),
            (width, *plane),
            pltpu.VMEM((width, *plane), jnp.int32),
            pltpu.SemaphoreType.DMA((6,)),
        ],
        remote=6,
    )
    got_a1, got_b1 = exchange(a1, b1)
    listed, b1 = lax.optimization_barrier((listed, b1))
    got = lax.all_to_all(jnp.broadcast_to(listed[None], (nsub, *listed.shape)), "sub", 0, 0)
    got, got_a1, got_b1 = lax.optimization_barrier((got, got_a1, got_b1))
    e_sh, h_sh, p_sh = (3, width + 2, *plane), (3, width + 3, *plane), (3, width + 2, *plane)
    hist1, hs, ps, coefh, ey2, a2, b2 = call(
        forward_one_kernel,
        "forward_one",
        [*fields, coef, src, got_a1, got_b1],
        [meta, debye_rate, debye_strength, wavelet],
        [(ROUND, 3, width, *plane), h_sh, p_sh, (2, 4, *plane), (2, *plane), (8, *plane), (8, *plane)],
        [e_sh],
    )
    got, a2, b2 = lax.optimization_barrier((got, a2, b2))
    got_a2, got_b2 = exchange(a2, b2)
    (maps,) = call(
        lambda *refs: receiver_kernel(width, depth, *refs),
        "receivers",
        [got],
        [meta],
        [(steps + 1, width + 2, *plane)],
        [((steps + 1) * (width + 2) * depth, span)],
    )
    coef_later, maps = lax.optimization_barrier((coef, maps))
    a3, b3 = call(adjoint_first_kernel, "adjoint_first", [*adjoint, coef_later], [meta], [(14, *plane), (14, *plane)])
    got_a3, got_b3 = exchange(a3, b3)
    hist2, eyh, a4, b4 = call(
        forward_two_kernel,
        "forward_two",
        [hist1, hs, ps, coef, coefh, src, maps, got_a2, got_b2],
        [meta, wavelet],
        [(ROUND, 3, width, *plane), (4, *plane), (2, *plane), (2, *plane)],
        [e_sh, h_sh, p_sh],
    )
    got_a4, got_b4 = exchange(a4, b4)
    e_adj, hs, ps, corr, a5, b5 = call(
        adjoint_one_kernel,
        "adjoint_one",
        [*adjoint, coef, coefh, maps, hist1, hist2, eyh, got_a3, got_b3, got_a4, got_b4],
        [meta],
        [(3, width, *plane), h_sh, p_sh, (2, width, *plane), (8, *plane), (8, *plane)],
        [e_sh],
    )
    got_a5, got_b5 = exchange(a5, b5)
    (corr,) = call(
        adjoint_two_kernel,
        "adjoint_two",
        [e_adj, hs, ps, coef, coefh, maps, fields[0], hist1, ey2, eyh, corr, got_a5, got_b5],
        [meta],
        [(2, width, *plane)],
        [e_sh, h_sh, p_sh],
    )
    total = shot_sum(corr)
    return (-(total[0] / (steps * nshot)), -(total[1] / (steps * nshot)))


def solution(mesh):
    in_specs = (
        P("shot", None, "sub", None, None),
        P("shot", None, "sub", None, None),
        P("shot", None, "sub", None, None),
        P("shot", None, "sub", None, None),
        P("shot", None, "sub", None, None),
        P("shot", None, "sub", None, None),
        P("sub", None, None),
        P("sub", None, None),
        P("sub", None, None),
        P(),
        P(),
        P(),
        P("shot", None),
        P("shot", None),
        P("shot", "sub", None),
        P("shot", "sub"),
        P("shot", None, "sub"),
    )
    out_specs = (P("sub", None, None), P("sub", None, None))
    return jax.shard_map(
        per_device, mesh=mesh, in_specs=in_specs, out_specs=out_specs, check_vma=False
    )
```

```python
import jax
import jax.numpy as jnp
from jax import lax
from jax.experimental import pallas as pl
from jax.experimental.pallas import tpu as pltpu
from jax.sharding import PartitionSpec as P

ROUND = 3
F32 = jnp.float32


def pair_swap(block, axis, first):
    route = []
    for i in range(first, lax.axis_size(axis) - 1, 2):
        route += [(i, i + 1), (i + 1, i)]
    return lax.ppermute(block, axis, route)


def exchange(inner, outer):
    got_outer = pair_swap(outer, "sub", 1)
    got_inner = pair_swap(inner, "sub", 0)
    return got_inner, got_outer


def shot_sum(x):
    n = lax.axis_size("shot")
    if n & (n - 1):
        return lax.psum(x, "shot")
    flip = 1
    while flip < n:
        x = x + lax.ppermute(x, "shot", [(i, i ^ flip) for i in range(n)])
        flip = 2 * flip + 1
    return x


def split_index(v, n):
    if n & (n - 1) == 0:
        return v & (n - 1), v >> (n.bit_length() - 1)
    return v % n, v // n


def ahead(u, axis):
    n = u.shape[axis]
    edge = lax.broadcasted_iota(jnp.int32, u.shape, axis) == n - 1
    return jnp.where(edge, 0.0, pltpu.roll(u, n - 1, axis))


def behind(u, axis):
    edge = lax.broadcasted_iota(jnp.int32, u.shape, axis) == 0
    return jnp.where(edge, 0.0, pltpu.roll(u, 1, axis))


def dfy(u):
    return ahead(u, 1) - u


def dfz(u):
    return ahead(u, 0) - u


def dby(u):
    return u - behind(u, 1)


def dbz(u):
    return u - behind(u, 0)


def h_step(h, e, e_next, keep=None, parts=(0, 1, 2)):
    ex, ey, ez = e
    new = {}
    if 0 in parts:
        new[0] = h[0] - 0.5 * (dfy(ez) - dfz(ey))
    ny, nz = e_next[1], e_next[2]
    if keep is not None:
        ny, nz = ny * keep, nz * keep
    new[1] = h[1] - 0.5 * (dfz(ex) - (nz - ez))
    new[2] = h[2] - 0.5 * ((ny - ey) - dfy(ex))
    return new


def e_step(e, h, h_prev, p, coef, inject, parts=(0, 1, 2)):
    ca, cb = coef[0], coef[1]
    new = {}
    for c in parts:
        if c == 0:
            curl = dby(h[2]) - dbz(h[1])
        elif c == 1:
            curl = dbz(h[0]) - (h[2] - h_prev[2])
        else:
            curl = (h[1] - h_prev[1]) - dby(h[0])
        new[c] = ca * e[c] + cb * (curl - p[c])
        if c == 1:
            new[c] = new[c] + inject
    return new


def p_step(p, e_new, coef):
    return {c: coef[2] * p[c] + coef[3] * e_new[c] for c in e_new}


class Planes:
    def __init__(self):
        self.at = {}

    def put(self, key, ref, *idx):
        self.at[key] = (ref, idx)

    def get(self, kind, c, i):
        ref, idx = self.at[kind, c, i]
        return ref[idx]

    def triple(self, kind, i, parts=(0, 1, 2)):
        return {c: self.get(kind, c, i) for c in parts}


def pick(even, a_ref, b_ref, k, low):
    a, b = a_ref[k], b_ref[k]
    return jnp.where(even, b, a) if low else jnp.where(even, a, b)


def emit(even, a_ref, b_ref, k, right, left):
    if right is None:
        right = left
    if left is None:
        left = right
    a_ref[k] = jnp.where(even, right, left)
    b_ref[k] = jnp.where(even, left, right)


def pre_steps(planes, coef_of, inject):
    h1, e1 = {}, {}
    last = planes.last
    sides = (0, 1, 2) if last <= 3 else (0, 1, last - 2, last - 1)
    for i in sides:
        e = [planes.get("E", c, i) for c in range(3)]
        nxt = {c: planes.get("E", c, i + 1) for c in (1, 2)}
        h1[i] = h_step(planes.triple("H", i), e, nxt)
    for i in (1, last - 1):
        parts = (0, 1, 2) if i == last - 1 else (1, 2)
        e1[i] = e_step(planes.triple("E", i), h1[i], h1[i - 1], planes.triple("P", i), coef_of(i), inject(i), parts)
    return h1, e1


def emit_state(even, planes, h1, e1, a_ref, b_ref, full):
    last = planes.last
    right = [planes.get("E", c, last) for c in range(3)]
    right += [h1[last - 1][1], h1[last - 1][2]] + [e1[last - 1][c] for c in range(3)]
    left = [planes.get("E", c, 0) for c in range(3)]
    left += [h1[0][c] for c in range(3)] + [e1[1][1], e1[1][2]]
    if full:
        right += [planes.get("P", c, last) for c in range(3)] + [planes.get("H", c, last) for c in range(3)]
        left += [planes.get("P", c, 0) for c in range(3)] + [None] * 3
    for k, (r, l) in enumerate(zip(right, left)):
        emit(even, a_ref, b_ref, k, r, l)


def own_planes(e_ref, h_ref, p_ref, h_at=0, p_at=0):
    planes = Planes()
    width = e_ref.shape[1]
    planes.last = width - 1
    for i in range(width):
        for c in range(3):
            planes.put(("E", c, i), e_ref, c, i)
            planes.put(("H", c, i), h_ref, c, i + h_at)
            planes.put(("P", c, i), p_ref, c, i + p_at)
    return planes


def source_map(cell_ref, sign_ref, mine, width, depth, span, full_x):
    flat = cell_ref[...]
    x, rest = split_index(flat, full_x)
    y, z = split_index(rest, span)
    row = (x - (mine * width - 1)) * depth + z
    rows = (width + 2) * depth
    n = flat.shape[1]
    hot = lax.broadcasted_iota(jnp.int32, (rows, n), 0) == row
    amp = (2 * sign_ref[...] - 1).astype(F32)
    where_y = lax.broadcasted_iota(jnp.int32, (span, n), 0) == y
    left = jnp.where(hot, 1.0, 0.0).astype(jnp.bfloat16)
    right = jnp.where(where_y, amp, 0.0).astype(jnp.bfloat16)
    return lax.dot_general(left, right, (((1,), (1,)), ((), ())), preferred_element_type=F32)


def first_kernel(full_x, meta, e_in, h_in, p_in, perm_in, cond_in, cls_in, cells_in, signs_in, rate_in, strength_in,
                 wavelet_in, e_ref, h_ref, p_ref, coef_ref, src_ref, tab_ref, a_ref, b_ref, perm, cond, cls, cells, signs,
                 rate_t, strength_t, wavelet, sems):
    even = meta[1] == 0
    width, depth, span = perm.shape
    moves = [(cells_in, cells), (signs_in, signs), (wavelet_in, wavelet), (rate_in, rate_t), (strength_in, strength_t)]
    moves += [(perm_in, perm), (cond_in, cond), (cls_in, cls), (e_in, e_ref), (h_in, h_ref), (p_in, p_ref)]
    copies = [pltpu.make_async_copy(a, b, sems.at[k]) for k, (a, b) in enumerate(moves)]
    for copy in copies:
        copy.start()
    for copy in copies[:5]:
        copy.wait()
    listed = [rate_t[k] for k in range(rate_t.shape[0])]
    listed += [(1.0 - rate_t[k]) * strength_t[k] for k in range(rate_t.shape[0])]
    listed += [wavelet[k] for k in range(wavelet.shape[0])]
    for k, value in enumerate(listed):
        tab_ref[k:k + 1, :] = jnp.full((1, span), value, F32)
    src = source_map(cells, signs, meta[0], width, depth, span, full_x)
    src_ref[...] = src.reshape(width + 2, depth, span)
    for copy in copies[5:8]:
        copy.wait()
    for i in range(width):
        ratio = cond[i] / (2.0 * perm[i])
        coef_ref[0, i] = (1.0 - ratio) / (1.0 + ratio)
        coef_ref[1, i] = 0.5 / (perm[i] * (1.0 + ratio))
        kind = cls[i]
        rate = jnp.zeros((depth, span), F32)
        gain = jnp.zeros((depth, span), F32)
        for k in range(rate_t.shape[0]):
            rate = jnp.where(kind == k, rate_t[k], rate)
            gain = jnp.where(kind == k, (1.0 - rate_t[k]) * strength_t[k], gain)
        coef_ref[2, i] = rate
        coef_ref[3, i] = gain
    for copy in copies[8:]:
        copy.wait()
    planes = own_planes(e_ref, h_ref, p_ref)
    h1, e1 = pre_steps(planes, lambda i: [coef_ref[k, i] for k in range(4)], lambda i: src_ref[i + 1] * wavelet[0])
    emit_state(even, planes, h1, e1, a_ref, b_ref, True)
    last = width - 1
    emit(even, a_ref, b_ref, 14, coef_ref[0, last], coef_ref[0, 0])
    emit(even, a_ref, b_ref, 15, coef_ref[1, last], coef_ref[1, 0])
    emit(even, a_ref, b_ref, 16, cls[last].astype(F32), cls[0].astype(F32))


def adjoint_first_kernel(meta, e_ref, h_ref, p_ref, coef_ref, a_ref, b_ref):
    planes = own_planes(e_ref, h_ref, p_ref)
    h1, e1 = pre_steps(planes, lambda i: [coef_ref[k, i] for k in range(4)], lambda i: 0.0)
    emit_state(meta[1] == 0, planes, h1, e1, a_ref, b_ref, True)


def receiver_kernel(width, depth, which, meta, got, maps_ref, acc):
    mine = meta[0]
    rows = (width + 4) * depth
    span = acc.shape[1]
    blocks, _, n = got.shape
    acc[...] = jnp.zeros(acc.shape, F32)
    first_row = ((mine * width - 2) * depth).astype(F32)
    row_at = lax.broadcasted_iota(jnp.int32, (rows, n), 0).astype(F32)
    y_at = lax.broadcasted_iota(jnp.int32, (span, n), 0).astype(F32)
    group = max(g for g in (1, 2, 4, 8) if blocks % g == 0)
    zero = jnp.zeros((rows, n), jnp.bfloat16)

    def block(k, carry):
        left = [[] for _ in which]
        right = []
        for b in range(group):
            at = k * group + b
            hot = row_at == got[at, 0:1, :] - first_row
            at_y = jnp.where(y_at == got[at, 1:2, :], 1.0, 0.0).astype(jnp.bfloat16)
            right += [at_y] * 3
            for part, s in zip(left, which):
                if s == 0:
                    part += [jnp.where(hot, 1.0, 0.0).astype(jnp.bfloat16), zero, zero]
                    continue
                v = got[at, 1 + s:2 + s, :]
                high = v.astype(jnp.bfloat16).astype(F32)
                mid = (v - high).astype(jnp.bfloat16).astype(F32)
                low = (v - high) - mid
                part += [jnp.where(hot, u, 0.0).astype(jnp.bfloat16) for u in (high, mid, low)]
        acc[...] += lax.dot_general(
            jnp.concatenate([jnp.concatenate(part, axis=1) for part in left], axis=0) if len(left) > 1 else jnp.concatenate(left[0], axis=1),
            jnp.concatenate(right, axis=1),
            (((1,), (1,)), ((), ())),
            preferred_element_type=F32,
        )
        return carry

    lax.fori_loop(0, blocks // group, block, 0)
    maps_ref[...] = acc[...].reshape(maps_ref.shape)


def round_body(planes, meta, coef_ref, coefh_ref, a_ref, b_ref, full, inject, first_extra, dest, prestep, seen):
    even = meta[1] == 0
    keep = jnp.where(meta[0] > 0, 1.0, 0.0).astype(F32)
    last = planes.last
    w = last + 1

    def low(k):
        return pick(even, a_ref, b_ref, k, True)

    def high(k):
        return pick(even, a_ref, b_ref, k, False)

    def coef_of(i):
        if i == -1:
            return [coefh_ref[0, k] for k in range(4)]
        if i == w:
            return [coefh_ref[1, k] for k in range(4)]
        return [coef_ref[k, i] for k in range(4)]

    held = {}
    for c in range(3):
        held["E", c, -1] = low(c)
        held["E", c, w] = high(c)
        held["H", c, w] = high(3 + c)
    held["H", 1, -2], held["H", 2, -2] = low(3), low(4)
    if full:
        for c in range(3):
            held["P", c, -1] = low(8 + c)
            held["H", c, -1] = low(11 + c)
            held["P", c, w] = high(8 + c)
    else:
        for i in (-1, w):
            cf = coef_of(i)
            for c in range(3):
                held["P", c, i] = cf[2] * planes.get("P", c, i) + cf[3] * held["E", c, i]

    def get(kind, c, i):
        if (kind, c, i) in held:
            return held[kind, c, i]
        return planes.get(kind, c, i)

    def store(kind, c, i, level, value):
        held.pop((kind, c, i), None)
        ref, idx = dest(kind, c, i, level)
        ref[idx] = value
        planes.put((kind, c, i), ref, *idx)

    for level in (1, 2, 3):
        if level == 2:
            for c in range(3):
                v = low(5 + c)
                if c == 1 and first_extra is not None:
                    v = v + first_extra(-2)
                held["E", c, -2] = v
            for c in (1, 2):
                v = high(5 + c)
                if c == 1 and first_extra is not None:
                    v = v + first_extra(w + 1)
                held["E", c, w + 1] = v
        h_lo = {1: -1, 2: -2, 3: -1}[level]
        h_hi = {1: last, 2: w, 3: last}[level]
        e_lo, e_hi = (0, last) if level == 3 else (-1, w)
        h_prev = None
        if h_lo > e_lo - 1:
            h_prev = {c: get("H", c, e_lo - 1) for c in (1, 2)}
        for i in range(h_lo, max(h_hi, e_hi) + 1):
            e = [get("E", c, i) for c in range(3)]
            if i <= h_hi:
                parts = (1, 2) if i == -2 else (0, 1, 2)
                h = h_step({c: get("H", c, i) for c in parts}, e, {c: get("E", c, i + 1) for c in (1, 2)},
                           keep if i == -1 else None, parts)
                for c in parts:
                    store("H", c, i, level, h[c])
            else:
                h = {c: get("H", c, i) for c in range(3)}
            if e_lo <= i <= e_hi:
                p = {c: get("P", c, i) for c in range(3)}
                cf = coef_of(i)
                new = e_step(e, h, h_prev, p, cf, inject(level, i))
                pn = p_step(p, new, cf)
                for c in range(3):
                    store("E", c, i, level, new[c])
                    store("P", c, i, level, pn[c])
                if seen is not None:
                    seen(level, i, new)
            h_prev = h
    if prestep is None:
        return
    h1, e1 = pre_steps(planes, coef_of, lambda i: inject(4, i))
    emit_state(even, planes, h1, e1, prestep[0], prestep[1], False)


def scratch_dest(es, hs, ps, own_e=None, width=4):
    def dest(kind, c, i, level):
        if kind == "E":
            if own_e is not None and 0 <= i < width:
                return own_e, (level - 1, c, i)
            return es, (c, i + 1)
        if kind == "H":
            return hs, (c, i + 2)
        return ps, (c, i + 1)

    return dest


def forward_one_kernel(meta, tab_ref, e_ref, h_ref, p_ref, coef_ref, src_ref, b_ref, a_ref,
                       hist_ref, hs_ref, ps_ref, coefh_ref, eyh_ref, oa_ref, ob_ref, es_ref):
    even = meta[1] == 0
    width = e_ref.shape[1]
    classes = (tab_ref.shape[0] - 2 * ROUND) // 2
    wavelet = 2 * classes
    for side in (0, 1):
        coefh_ref[side, 0] = pick(even, a_ref, b_ref, 14, side == 0)
        coefh_ref[side, 1] = pick(even, a_ref, b_ref, 15, side == 0)
        kind = pick(even, a_ref, b_ref, 16, side == 0)
        rate = jnp.zeros(kind.shape, F32)
        gain = jnp.zeros(kind.shape, F32)
        for k in range(classes):
            rate = jnp.where(kind == float(k), tab_ref[k:k + 1, :], rate)
            gain = jnp.where(kind == float(k), tab_ref[classes + k:classes + k + 1, :], gain)
        coefh_ref[side, 2] = rate
        coefh_ref[side, 3] = gain
    planes = own_planes(e_ref, h_ref, p_ref)

    def seen(level, i, e):
        if level == 2 and i in (-1, width):
            eyh_ref[0 if i < 0 else 1] = e[1]

    round_body(planes, meta, coef_ref, coefh_ref, a_ref, b_ref, True,
               lambda level, i: src_ref[i + 1] * tab_ref[wavelet + level - 1:wavelet + level, :], None,
               scratch_dest(es_ref, hs_ref, ps_ref, hist_ref, width), (oa_ref, ob_ref), seen)


def state_planes(e_ref, hs_ref, ps_ref, level=None):
    planes = Planes()
    width = e_ref.shape[-3]
    planes.last = width - 1
    for c in range(3):
        for i in range(width):
            if level is None:
                planes.put(("E", c, i), e_ref, c, i + 0)
            else:
                planes.put(("E", c, i), e_ref, level, c, i)
        for i in range(-1, width):
            planes.put(("H", c, i), hs_ref, c, i + 2)
        for i in range(-1, width + 1):
            planes.put(("P", c, i), ps_ref, c, i + 1)
    return planes


def forward_two_kernel(meta, tab_ref, hist_in, hs_in, ps_in, coef_ref, coefh_ref, src_ref, b_ref, a_ref,
                       hist_ref, eyh_ref, oa_ref, ob_ref, es_ref, hs_ref, ps_ref):
    even = meta[1] == 0
    width = hist_in.shape[2]
    wavelet = tab_ref.shape[0] - ROUND
    planes = state_planes(hist_in, hs_in, ps_in, 2)
    eyh_ref[0] = pick(even, a_ref, b_ref, 1, True)
    eyh_ref[1] = pick(even, a_ref, b_ref, 1, False)

    def seen(level, i, e):
        if level == 2 and i in (-1, width):
            eyh_ref[2 if i < 0 else 3] = e[1]

    round_body(planes, meta, coef_ref, coefh_ref, a_ref, b_ref, False,
               lambda level, i: src_ref[i + 1] * tab_ref[wavelet + level - 1:wavelet + level, :], None,
               scratch_dest(es_ref, hs_ref, ps_ref, hist_ref, width), None, seen)
    last = width - 1
    emit(even, oa_ref, ob_ref, 0, hist_ref[2, 1, last], hist_ref[2, 1, 0])
    emit(even, oa_ref, ob_ref, 1, hist_ref[2, 1, last - 1], hist_ref[2, 1, 1])


def correlate(corr_ref, i, b, now, prev, add):
    eps = b[0] * (now[0] - prev[0]) + b[1] * (now[1] - prev[1]) + b[2] * (now[2] - prev[2])
    sig = b[0] * now[0] + b[1] * now[1] + b[2] * now[2]
    if add is not None:
        eps, sig = eps + add[0, i], sig + add[1, i]
    corr_ref[0, i] = eps
    corr_ref[1, i] = sig


def adjoint_one_kernel(meta, e_ref, h_ref, p_ref, coef_ref, coefh_ref, maps6_ref, maps5_ref, hist1_ref, hist2_ref, eyh_ref,
                       b_ref, a_ref, rb_ref, ra_ref, e_out, hs_ref, ps_ref, corr_ref, oa_ref, ob_ref, es_ref):
    even = meta[1] == 0
    width = e_ref.shape[1]
    steps = 2 * ROUND
    planes = own_planes(e_ref, h_ref, p_ref)

    def ey(n, i):
        if 0 <= i < width:
            return hist1_ref[n - 1, 1, i] if n <= ROUND else hist2_ref[n - 1 - ROUND, 1, i]
        at = {3: 0, 5: 2}[n]
        return eyh_ref[at if i < 0 else at + 1]

    def extra(i):
        if i < 0:
            ey_last = pick(even, ra_ref, rb_ref, -1 - i, True)
        else:
            ey_last = pick(even, ra_ref, rb_ref, i - width, False)
        return maps6_ref[0, i + 2] * ey_last - maps6_ref[1, i + 2]

    def inject(level, i):
        n = steps + 1 - level
        if n == steps and not 0 <= i < width:
            return extra(i)
        seen_at = maps6_ref[1, i + 2] if n == steps else maps5_ref[steps - 1 - n, i + 2]
        return maps6_ref[0, i + 2] * ey(n, i) - seen_at

    def seen(level, i, e):
        if not 0 <= i < width:
            return
        n = steps + 1 - level
        now = [hist2_ref[n - 1 - ROUND, c, i] for c in range(3)]
        prev = [hist2_ref[n - 2 - ROUND, c, i] if n - 1 > ROUND else hist1_ref[n - 2, c, i] for c in range(3)]
        correlate(corr_ref, i, e, now, prev, corr_ref if level > 1 else None)

    def dest(kind, c, i, level):
        if kind == "E":
            if 0 <= i < width:
                return e_out, (c, i)
            return es_ref, (c, i + 1)
        if kind == "H":
            return hs_ref, (c, i + 2)
        return ps_ref, (c, i + 1)

    round_body(planes, meta, coef_ref, coefh_ref, a_ref, b_ref, True, inject, extra, dest, (oa_ref, ob_ref), seen)


def adjoint_two_kernel(meta, e_ref, hs_in, ps_in, coef_ref, coefh_ref, maps6_ref, maps5_ref, maps2_ref, e0_ref, hist1_ref, ey2_ref, eyh_ref,
                       corr_in, b_ref, a_ref, corr_ref, es_ref, hs_ref, ps_ref):
    width = e_ref.shape[1]
    steps = 2 * ROUND
    planes = state_planes(e_ref, hs_in, ps_in)

    def ey(n, i):
        if 0 <= i < width:
            return hist1_ref[n - 1, 1, i]
        if n == 3:
            return eyh_ref[0 if i < 0 else 1]
        return ey2_ref[0 if i < 0 else 1]

    def inject(level, i):
        n = steps + 1 - ROUND - level
        seen_at = maps5_ref[ROUND - 1, i + 2] if n == ROUND else maps2_ref[ROUND - 1 - n, i + 2]
        return maps6_ref[0, i + 2] * ey(n, i) - seen_at

    def seen(level, i, e):
        if not 0 <= i < width:
            return
        n = steps + 1 - ROUND - level
        now = [hist1_ref[n - 1, c, i] for c in range(3)]
        prev = [hist1_ref[n - 2, c, i] if n > 1 else e0_ref[c, i] for c in range(3)]
        correlate(corr_ref, i, e, now, prev, corr_ref if level > 1 else corr_in)

    round_body(planes, meta, coef_ref, coefh_ref, a_ref, b_ref, False, inject, None,
               scratch_dest(es_ref, hs_ref, ps_ref), None, seen)


def call(body, name, inputs, scalars, outs, scratch=(), remote=0, work=10**10):
    smem = pl.BlockSpec(memory_space=pltpu.SMEM)
    vmem = pl.BlockSpec(memory_space=pltpu.VMEM)
    stay = pl.BlockSpec(memory_space=pltpu.HBM)
    return pl.pallas_call(
        body,
        name=name,
        out_shape=[jax.ShapeDtypeStruct(s, F32) for s in outs],
        in_specs=[smem] * len(scalars) + [stay] * remote + [vmem] * (len(inputs) - remote),
        out_specs=[vmem] * len(outs),
        scratch_shapes=[s if not isinstance(s, tuple) else pltpu.VMEM(s, F32) for s in scratch],
        cost_estimate=pl.CostEstimate(flops=work, transcendentals=0, bytes_accessed=0),
        compiler_params=pltpu.CompilerParams(vmem_limit_bytes=48 * 1024 * 1024),
    )(*scalars, *[pltpu.with_memory_space_constraint(x, pltpu.HBM) for x in inputs[:remote]], *inputs[remote:])


def per_device(
    electric,
    magnetic,
    polar,
    adj_electric,
    adj_magnetic,
    adj_polar,
    permittivity,
    conductivity,
    debye_class,
    debye_rate,
    debye_strength,
    wavelet,
    src_cell,
    src_sign,
    rec_owner,
    rec_pos,
    observed,
):
    width, depth, span = permittivity.shape
    steps = wavelet.shape[0]
    nsub = lax.axis_size("sub")
    nshot = lax.axis_size("shot")
    mine = lax.axis_index("sub")
    meta = jnp.stack([mine, mine % 2]).astype(jnp.int32)
    plane = (depth, span)

    in_x, rest = split_index(rec_pos[0], width)
    rec_y, rec_z = split_index(rest, span)
    rec_row = (rec_owner[0, :, 0] * width + in_x) * depth + rec_z
    listed = jnp.concatenate([rec_row[None].astype(F32), rec_y[None].astype(F32), observed[0]], axis=0)
    fields = (electric[0], magnetic[0], polar[0])
    adjoint = (adj_electric[0], adj_magnetic[0], adj_polar[0])

    own = (3, width, *plane)
    classes = debye_rate.shape[0]
    tab_rows = 2 * classes + steps
    *fields, coef, src, tab, a1, b1 = call(
        lambda *refs: first_kernel(width * nsub, *refs),
        "first",
        [*fields, permittivity, conductivity, debye_class, src_cell, src_sign, debye_rate, debye_strength, wavelet],
        [meta],
        [own, own, own, (4, width, *plane), (width + 2, *plane), (tab_rows, span), (17, *plane), (17, *plane)],
        [
            (width, *plane),
            (width, *plane),
            pltpu.VMEM((width, *plane), jnp.int32),
            pltpu.VMEM(src_cell.shape, jnp.int32),
            pltpu.VMEM(src_sign.shape, jnp.int32),
            pltpu.SMEM(debye_rate.shape, F32),
            pltpu.SMEM(debye_strength.shape, F32),
            pltpu.SMEM(wavelet.shape, F32),
            pltpu.SemaphoreType.DMA((11,)),
        ],
        remote=11,
    )
    got_a1, got_b1 = exchange(a1, b1)
    listed, b1 = lax.optimization_barrier((listed, b1))
    got = lax.all_to_all(jnp.broadcast_to(listed[None], (nsub, *listed.shape)), "sub", 0, 0)
    got, got_a1, got_b1 = lax.optimization_barrier((got, got_a1, got_b1))
    e_sh, h_sh, p_sh = (3, width + 2, *plane), (3, width + 3, *plane), (3, width + 2, *plane)
    hist1, hs, ps, coefh, ey2, a2, b2 = call(
        forward_one_kernel,
        "forward_one",
        [tab, *fields, coef, src, got_b1, got_a1],
        [meta],
        [(ROUND, 3, width, *plane), h_sh, p_sh, (2, 4, *plane), (2, *plane), (8, *plane), (8, *plane)],
        [e_sh],
    )
    got, coef, a2, b2 = lax.optimization_barrier((got, coef, a2, b2))
    got_a2, got_b2 = exchange(a2, b2)
    a3, b3 = call(adjoint_first_kernel, "adjoint_first", [*adjoint, coef], [meta], [(14, *plane), (14, *plane)])
    got_a3, got_b3 = exchange(a3, b3)

    def receivers(name, which):
        (maps,) = call(
            lambda *refs: receiver_kernel(width, depth, which, *refs),
            name,
            [got],
            [meta],
            [(len(which), width + 4, *plane)],
            [(len(which) * (width + 4) * depth, span)],
        )
        return maps

    maps6 = receivers("receivers_last", (0, steps))
    hist2, eyh, a4, b4 = call(
        forward_two_kernel,
        "forward_two",
        [tab, hist1, hs, ps, coef, coefh, src, got_b2, got_a2],
        [meta],
        [(ROUND, 3, width, *plane), (4, *plane), (2, *plane), (2, *plane)],
        [e_sh, h_sh, p_sh],
    )
    got, a4, b4 = lax.optimization_barrier((got, a4, b4))
    got_a4, got_b4 = exchange(a4, b4)
    maps5 = receivers("receivers_middle", tuple(range(steps - 1, ROUND - 1, -1)))
    e_adj, hs, ps, corr, a5, b5 = call(
        adjoint_one_kernel,
        "adjoint_one",
        [*adjoint, coef, coefh, maps6, maps5, hist1, hist2, eyh, got_b3, got_a3, got_b4, got_a4],
        [meta],
        [(3, width, *plane), h_sh, p_sh, (2, width, *plane), (8, *plane), (8, *plane)],
        [e_sh],
    )
    got, a5, b5 = lax.optimization_barrier((got, a5, b5))
    got_a5, got_b5 = exchange(a5, b5)
    maps2 = receivers("receivers_first", tuple(range(ROUND - 1, 0, -1)))
    (corr,) = call(
        adjoint_two_kernel,
        "adjoint_two",
        [e_adj, hs, ps, coef, coefh, maps6, maps5, maps2, fields[0], hist1, ey2, eyh, corr, got_b5, got_a5],
        [meta],
        [(2, width, *plane)],
        [e_sh, h_sh, p_sh],
    )
    total = shot_sum(corr)
    return (-(total[0] / (steps * nshot)), -(total[1] / (steps * nshot)))


def solution(mesh):
    in_specs = (
        P("shot", None, "sub", None, None),
        P("shot", None, "sub", None, None),
        P("shot", None, "sub", None, None),
        P("shot", None, "sub", None, None),
        P("shot", None, "sub", None, None),
        P("shot", None, "sub", None, None),
        P("sub", None, None),
        P("sub", None, None),
        P("sub", None, None),
        P(),
        P(),
        P(),
        P("shot", None),
        P("shot", None),
        P("shot", "sub", None),
        P("shot", "sub"),
        P("shot", None, "sub"),
    )
    out_specs = (P("sub", None, None), P("sub", None, None))
    return jax.shard_map(
        per_device, mesh=mesh, in_specs=in_specs, out_specs=out_specs, check_vma=False
    )
```

```python
import jax
import jax.numpy as jnp
from jax import lax
from jax.experimental import pallas as pl
from jax.experimental.pallas import tpu as pltpu
from jax.sharding import PartitionSpec as P

ROUND = 3
F32 = jnp.float32


def pair_swap(block, axis, first):
    route = []
    for i in range(first, lax.axis_size(axis) - 1, 2):
        route += [(i, i + 1), (i + 1, i)]
    return lax.ppermute(block, axis, route)


def exchange(inner, outer):
    got_outer = pair_swap(outer, "sub", 1)
    got_inner = pair_swap(inner, "sub", 0)
    return got_inner, got_outer


def shot_sum(x):
    n = lax.axis_size("shot")
    if n & (n - 1):
        return lax.psum(x, "shot")
    flip = 1
    while flip < n:
        x = x + lax.ppermute(x, "shot", [(i, i ^ flip) for i in range(n)])
        flip = 2 * flip + 1
    return x


def split_index(v, n):
    if n & (n - 1) == 0:
        return v & (n - 1), v >> (n.bit_length() - 1)
    return v % n, v // n


def ahead(u, axis):
    n = u.shape[axis]
    edge = lax.broadcasted_iota(jnp.int32, u.shape, axis) == n - 1
    return jnp.where(edge, 0.0, pltpu.roll(u, n - 1, axis))


def behind(u, axis):
    edge = lax.broadcasted_iota(jnp.int32, u.shape, axis) == 0
    return jnp.where(edge, 0.0, pltpu.roll(u, 1, axis))


def dfy(u):
    return ahead(u, 1) - u


def dfz(u):
    return ahead(u, 0) - u


def dby(u):
    return u - behind(u, 1)


def dbz(u):
    return u - behind(u, 0)


def h_step(h, e, e_next, keep=None, parts=(0, 1, 2)):
    ex, ey, ez = e
    new = {}
    if 0 in parts:
        new[0] = h[0] - 0.5 * (dfy(ez) - dfz(ey))
    ny, nz = e_next[1], e_next[2]
    if keep is not None:
        ny, nz = ny * keep, nz * keep
    new[1] = h[1] - 0.5 * (dfz(ex) - (nz - ez))
    new[2] = h[2] - 0.5 * ((ny - ey) - dfy(ex))
    return new


def e_step(e, h, h_prev, p, coef, inject, parts=(0, 1, 2)):
    ca, cb = coef[0], coef[1]
    new = {}
    for c in parts:
        if c == 0:
            curl = dby(h[2]) - dbz(h[1])
        elif c == 1:
            curl = dbz(h[0]) - (h[2] - h_prev[2])
        else:
            curl = (h[1] - h_prev[1]) - dby(h[0])
        new[c] = ca * e[c] + cb * (curl - p[c])
        if c == 1:
            new[c] = new[c] + inject
    return new


def p_step(p, e_new, coef):
    return {c: coef[2] * p[c] + coef[3] * e_new[c] for c in e_new}


class Planes:
    def __init__(self):
        self.at = {}

    def put(self, key, ref, *idx):
        self.at[key] = (ref, idx)

    def get(self, kind, c, i):
        ref, idx = self.at[kind, c, i]
        return ref[idx]

    def triple(self, kind, i, parts=(0, 1, 2)):
        return {c: self.get(kind, c, i) for c in parts}


def is_even(meta, shape):
    return jnp.broadcast_to(meta[1:2, :], shape) > 0.5


def pick(even, a_ref, b_ref, k, low):
    a, b = a_ref[k], b_ref[k]
    return jnp.where(even, b, a) if low else jnp.where(even, a, b)


def emit(even, a_ref, b_ref, k, right, left):
    if right is None:
        right = left
    if left is None:
        left = right
    a_ref[k] = jnp.where(even, right, left)
    b_ref[k] = jnp.where(even, left, right)


def pre_steps(planes, coef_of, inject):
    h1, e1 = {}, {}
    last = planes.last
    sides = (0, 1, 2) if last <= 3 else (0, 1, last - 2, last - 1)
    for i in sides:
        e = [planes.get("E", c, i) for c in range(3)]
        nxt = {c: planes.get("E", c, i + 1) for c in (1, 2)}
        h1[i] = h_step(planes.triple("H", i), e, nxt)
    for i in (1, last - 1):
        parts = (0, 1, 2) if i == last - 1 else (1, 2)
        e1[i] = e_step(planes.triple("E", i), h1[i], h1[i - 1], planes.triple("P", i), coef_of(i), inject(i), parts)
    return h1, e1


def emit_state(even, planes, h1, e1, a_ref, b_ref, full):
    last = planes.last
    right = [planes.get("E", c, last) for c in range(3)]
    right += [h1[last - 1][1], h1[last - 1][2]] + [e1[last - 1][c] for c in range(3)]
    left = [planes.get("E", c, 0) for c in range(3)]
    left += [h1[0][c] for c in range(3)] + [e1[1][1], e1[1][2]]
    if full:
        right += [planes.get("P", c, last) for c in range(3)] + [planes.get("H", c, last) for c in range(3)]
        left += [planes.get("P", c, 0) for c in range(3)] + [None] * 3
    for k, (r, l) in enumerate(zip(right, left)):
        emit(even, a_ref, b_ref, k, r, l)


def own_planes(e_ref, h_ref, p_ref, h_at=0, p_at=0):
    planes = Planes()
    width = e_ref.shape[1]
    planes.last = width - 1
    for i in range(width):
        for c in range(3):
            planes.put(("E", c, i), e_ref, c, i)
            planes.put(("H", c, i), h_ref, c, i + h_at)
            planes.put(("P", c, i), p_ref, c, i + p_at)
    return planes


def source_map(cell_ref, sign_ref, mine, width, depth, span, full_x):
    flat = cell_ref[...]
    x, rest = split_index(flat, full_x)
    y, z = split_index(rest, span)
    n = flat.shape[1]
    row = (x - (jnp.broadcast_to(mine, (1, n)) * width - 1)) * depth + z
    rows = (width + 2) * depth
    hot = lax.broadcasted_iota(jnp.int32, (rows, n), 0) == row
    amp = (2 * sign_ref[...] - 1).astype(F32)
    where_y = lax.broadcasted_iota(jnp.int32, (span, n), 0) == y
    left = jnp.where(hot, 1.0, 0.0).astype(jnp.bfloat16)
    right = jnp.where(where_y, amp, 0.0).astype(jnp.bfloat16)
    return lax.dot_general(left, right, (((1,), (1,)), ((), ())), preferred_element_type=F32)


def first_kernel(full_x, meta, e_in, h_in, p_in, perm_in, cond_in, cls_in, cells_in, signs_in, rate_in, strength_in,
                 wavelet_in, e_ref, h_ref, p_ref, coef_ref, src_ref, tab_ref, a_ref, b_ref, perm, cond, cls, cells, signs,
                 rate_t, strength_t, wavelet, sems):
    width, depth, span = perm.shape
    even = is_even(meta, (depth, span))
    moves = [(cells_in, cells), (signs_in, signs), (wavelet_in, wavelet), (rate_in, rate_t), (strength_in, strength_t)]
    moves += [(perm_in, perm), (cond_in, cond), (cls_in, cls), (e_in, e_ref), (h_in, h_ref), (p_in, p_ref)]
    copies = [pltpu.make_async_copy(a, b, sems.at[k]) for k, (a, b) in enumerate(moves)]
    for copy in copies:
        copy.start()
    for copy in copies[:5]:
        copy.wait()
    listed = [rate_t[k] for k in range(rate_t.shape[0])]
    listed += [(1.0 - rate_t[k]) * strength_t[k] for k in range(rate_t.shape[0])]
    listed += [wavelet[k] for k in range(wavelet.shape[0])]
    for k, value in enumerate(listed):
        tab_ref[k:k + 1, :] = jnp.full((1, span), value, F32)
    src = source_map(cells, signs, meta[0:1, 0:1].astype(jnp.int32), width, depth, span, full_x)
    src_ref[...] = src.reshape(width + 2, depth, span)
    for copy in copies[5:8]:
        copy.wait()
    for i in range(width):
        ratio = cond[i] / (2.0 * perm[i])
        coef_ref[0, i] = (1.0 - ratio) / (1.0 + ratio)
        coef_ref[1, i] = 0.5 / (perm[i] * (1.0 + ratio))
        kind = cls[i]
        rate = jnp.zeros((depth, span), F32)
        gain = jnp.zeros((depth, span), F32)
        for k in range(rate_t.shape[0]):
            rate = jnp.where(kind == k, rate_t[k], rate)
            gain = jnp.where(kind == k, (1.0 - rate_t[k]) * strength_t[k], gain)
        coef_ref[2, i] = rate
        coef_ref[3, i] = gain
    for copy in copies[8:]:
        copy.wait()
    planes = own_planes(e_ref, h_ref, p_ref)
    h1, e1 = pre_steps(planes, lambda i: [coef_ref[k, i] for k in range(4)], lambda i: src_ref[i + 1] * wavelet[0])
    emit_state(even, planes, h1, e1, a_ref, b_ref, True)
    last = width - 1
    emit(even, a_ref, b_ref, 14, coef_ref[0, last], coef_ref[0, 0])
    emit(even, a_ref, b_ref, 15, coef_ref[1, last], coef_ref[1, 0])
    emit(even, a_ref, b_ref, 16, cls[last].astype(F32), cls[0].astype(F32))


def adjoint_first_kernel(meta, e_ref, h_ref, p_ref, coef_ref, a_ref, b_ref):
    planes = own_planes(e_ref, h_ref, p_ref)
    h1, e1 = pre_steps(planes, lambda i: [coef_ref[k, i] for k in range(4)], lambda i: 0.0)
    emit_state(is_even(meta, e_ref.shape[2:]), planes, h1, e1, a_ref, b_ref, True)


def receiver_kernel(width, depth, which, meta, got, maps_ref, acc):
    rows = (width + 4) * depth
    span = acc.shape[1]
    blocks, _, n = got.shape
    acc[...] = jnp.zeros(acc.shape, F32)
    first_row = (meta[0:1, :] * width - 2.0) * depth
    row_at = lax.broadcasted_iota(jnp.int32, (rows, n), 0).astype(F32)
    y_at = lax.broadcasted_iota(jnp.int32, (span, n), 0).astype(F32)
    group = max(g for g in (1, 2, 4, 8) if blocks % g == 0)
    zero = jnp.zeros((rows, n), jnp.bfloat16)

    def block(k, carry):
        left = [[] for _ in which]
        right = []
        for b in range(group):
            at = k * group + b
            hot = row_at == got[at, 0:1, :] - first_row[:, :n]
            at_y = jnp.where(y_at == got[at, 1:2, :], 1.0, 0.0).astype(jnp.bfloat16)
            right += [at_y] * 3
            for part, s in zip(left, which):
                if s == 0:
                    part += [jnp.where(hot, 1.0, 0.0).astype(jnp.bfloat16), zero, zero]
                    continue
                v = got[at, 1 + s:2 + s, :]
                high = v.astype(jnp.bfloat16).astype(F32)
                mid = (v - high).astype(jnp.bfloat16).astype(F32)
                low = (v - high) - mid
                part += [jnp.where(hot, u, 0.0).astype(jnp.bfloat16) for u in (high, mid, low)]
        acc[...] += lax.dot_general(
            jnp.concatenate([jnp.concatenate(part, axis=1) for part in left], axis=0) if len(left) > 1 else jnp.concatenate(left[0], axis=1),
            jnp.concatenate(right, axis=1),
            (((1,), (1,)), ((), ())),
            preferred_element_type=F32,
        )
        return carry

    lax.fori_loop(0, blocks // group, block, 0)
    maps_ref[...] = acc[...].reshape(maps_ref.shape)


def round_body(planes, meta, coef_ref, coefh_ref, a_ref, b_ref, full, inject, first_extra, dest, prestep, seen):
    even = is_even(meta, coef_ref.shape[2:])
    keep = meta[2:3, :]
    last = planes.last
    w = last + 1

    def low(k):
        return pick(even, a_ref, b_ref, k, True)

    def high(k):
        return pick(even, a_ref, b_ref, k, False)

    def coef_of(i):
        if i == -1:
            return [coefh_ref[0, k] for k in range(4)]
        if i == w:
            return [coefh_ref[1, k] for k in range(4)]
        return [coef_ref[k, i] for k in range(4)]

    held = {}
    for c in range(3):
        held["E", c, -1] = low(c)
        held["E", c, w] = high(c)
        held["H", c, w] = high(3 + c)
    held["H", 1, -2], held["H", 2, -2] = low(3), low(4)
    if full:
        for c in range(3):
            held["P", c, -1] = low(8 + c)
            held["H", c, -1] = low(11 + c)
            held["P", c, w] = high(8 + c)
    else:
        for i in (-1, w):
            cf = coef_of(i)
            for c in range(3):
                held["P", c, i] = cf[2] * planes.get("P", c, i) + cf[3] * held["E", c, i]

    def get(kind, c, i):
        if (kind, c, i) in held:
            return held[kind, c, i]
        return planes.get(kind, c, i)

    def store(kind, c, i, level, value):
        held.pop((kind, c, i), None)
        ref, idx = dest(kind, c, i, level)
        ref[idx] = value
        planes.put((kind, c, i), ref, *idx)

    for level in (1, 2, 3):
        if level == 2:
            for c in range(3):
                v = low(5 + c)
                if c == 1 and first_extra is not None:
                    v = v + first_extra(-2)
                held["E", c, -2] = v
            for c in (1, 2):
                v = high(5 + c)
                if c == 1 and first_extra is not None:
                    v = v + first_extra(w + 1)
                held["E", c, w + 1] = v
        h_lo = {1: -1, 2: -2, 3: -1}[level]
        h_hi = {1: last, 2: w, 3: last}[level]
        e_lo, e_hi = (0, last) if level == 3 else (-1, w)
        h_prev = None
        if h_lo > e_lo - 1:
            h_prev = {c: get("H", c, e_lo - 1) for c in (1, 2)}
        for i in range(h_lo, max(h_hi, e_hi) + 1):
            e = [get("E", c, i) for c in range(3)]
            if i <= h_hi:
                parts = (1, 2) if i == -2 else (0, 1, 2)
                h = h_step({c: get("H", c, i) for c in parts}, e, {c: get("E", c, i + 1) for c in (1, 2)},
                           keep if i == -1 else None, parts)
                for c in parts:
                    store("H", c, i, level, h[c])
            else:
                h = {c: get("H", c, i) for c in range(3)}
            if e_lo <= i <= e_hi:
                p = {c: get("P", c, i) for c in range(3)}
                cf = coef_of(i)
                new = e_step(e, h, h_prev, p, cf, inject(level, i))
                pn = p_step(p, new, cf)
                for c in range(3):
                    store("E", c, i, level, new[c])
                    store("P", c, i, level, pn[c])
                if seen is not None:
                    seen(level, i, new)
            h_prev = h
    if prestep is None:
        return
    h1, e1 = pre_steps(planes, coef_of, lambda i: inject(4, i))
    emit_state(even, planes, h1, e1, prestep[0], prestep[1], False)


def scratch_dest(es, hs, ps, own_e=None, width=4):
    def dest(kind, c, i, level):
        if kind == "E":
            if own_e is not None and 0 <= i < width:
                return own_e, (level - 1, c, i)
            return es, (c, i + 1)
        if kind == "H":
            return hs, (c, i + 2)
        return ps, (c, i + 1)

    return dest


def forward_one_kernel(meta, tab_ref, e_ref, h_ref, p_ref, coef_ref, src_ref, b_ref, a_ref,
                       hist_ref, hs_ref, ps_ref, coefh_ref, eyh_ref, oa_ref, ob_ref, es_ref):
    even = is_even(meta, e_ref.shape[2:])
    width = e_ref.shape[1]
    classes = (tab_ref.shape[0] - 2 * ROUND) // 2
    wavelet = 2 * classes
    for side in (0, 1):
        coefh_ref[side, 0] = pick(even, a_ref, b_ref, 14, side == 0)
        coefh_ref[side, 1] = pick(even, a_ref, b_ref, 15, side == 0)
        kind = pick(even, a_ref, b_ref, 16, side == 0)
        rate = jnp.zeros(kind.shape, F32)
        gain = jnp.zeros(kind.shape, F32)
        for k in range(classes):
            rate = jnp.where(kind == float(k), tab_ref[k:k + 1, :], rate)
            gain = jnp.where(kind == float(k), tab_ref[classes + k:classes + k + 1, :], gain)
        coefh_ref[side, 2] = rate
        coefh_ref[side, 3] = gain
    planes = own_planes(e_ref, h_ref, p_ref)

    def seen(level, i, e):
        if level == 2 and i in (-1, width):
            eyh_ref[0 if i < 0 else 1] = e[1]

    round_body(planes, meta, coef_ref, coefh_ref, a_ref, b_ref, True,
               lambda level, i: src_ref[i + 1] * tab_ref[wavelet + level - 1:wavelet + level, :], None,
               scratch_dest(es_ref, hs_ref, ps_ref, hist_ref, width), (oa_ref, ob_ref), seen)


def state_planes(e_ref, hs_ref, ps_ref, level=None):
    planes = Planes()
    width = e_ref.shape[-3]
    planes.last = width - 1
    for c in range(3):
        for i in range(width):
            if level is None:
                planes.put(("E", c, i), e_ref, c, i + 0)
            else:
                planes.put(("E", c, i), e_ref, level, c, i)
        for i in range(-1, width):
            planes.put(("H", c, i), hs_ref, c, i + 2)
        for i in range(-1, width + 1):
            planes.put(("P", c, i), ps_ref, c, i + 1)
    return planes


def forward_two_kernel(meta, tab_ref, hist_in, hs_in, ps_in, coef_ref, coefh_ref, src_ref, b_ref, a_ref,
                       hist_ref, eyh_ref, oa_ref, ob_ref, es_ref, hs_ref, ps_ref):
    even = is_even(meta, hist_in.shape[3:])
    width = hist_in.shape[2]
    wavelet = tab_ref.shape[0] - ROUND
    planes = state_planes(hist_in, hs_in, ps_in, 2)
    eyh_ref[0] = pick(even, a_ref, b_ref, 1, True)
    eyh_ref[1] = pick(even, a_ref, b_ref, 1, False)

    def seen(level, i, e):
        if level == 2 and i in (-1, width):
            eyh_ref[2 if i < 0 else 3] = e[1]

    round_body(planes, meta, coef_ref, coefh_ref, a_ref, b_ref, False,
               lambda level, i: src_ref[i + 1] * tab_ref[wavelet + level - 1:wavelet + level, :], None,
               scratch_dest(es_ref, hs_ref, ps_ref, hist_ref, width), None, seen)
    last = width - 1
    emit(even, oa_ref, ob_ref, 0, hist_ref[2, 1, last], hist_ref[2, 1, 0])
    emit(even, oa_ref, ob_ref, 1, hist_ref[2, 1, last - 1], hist_ref[2, 1, 1])


def correlate(corr_ref, i, b, now, prev, add):
    eps = b[0] * (now[0] - prev[0]) + b[1] * (now[1] - prev[1]) + b[2] * (now[2] - prev[2])
    sig = b[0] * now[0] + b[1] * now[1] + b[2] * now[2]
    if add is not None:
        eps, sig = eps + add[0, i], sig + add[1, i]
    corr_ref[0, i] = eps
    corr_ref[1, i] = sig


def adjoint_one_kernel(meta, e_ref, h_ref, p_ref, coef_ref, coefh_ref, maps_ref, hist1_ref, hist2_ref, eyh_ref,
                       b_ref, a_ref, rb_ref, ra_ref, e_out, hs_ref, ps_ref, corr_ref, oa_ref, ob_ref, es_ref):
    even = is_even(meta, e_ref.shape[2:])
    width = e_ref.shape[1]
    steps = 2 * ROUND
    planes = own_planes(e_ref, h_ref, p_ref)

    def ey(n, i):
        if 0 <= i < width:
            return hist1_ref[n - 1, 1, i] if n <= ROUND else hist2_ref[n - 1 - ROUND, 1, i]
        at = {3: 0, 5: 2}[n]
        return eyh_ref[at if i < 0 else at + 1]

    def extra(i):
        if i < 0:
            ey_last = pick(even, ra_ref, rb_ref, -1 - i, True)
        else:
            ey_last = pick(even, ra_ref, rb_ref, i - width, False)
        return maps_ref[0, i + 2] * ey_last - maps_ref[1, i + 2]

    def inject(level, i):
        n = steps + 1 - level
        if n == steps and not 0 <= i < width:
            return extra(i)
        return maps_ref[0, i + 2] * ey(n, i) - maps_ref[steps + 1 - n, i + 2]

    def seen(level, i, e):
        if not 0 <= i < width:
            return
        n = steps + 1 - level
        now = [hist2_ref[n - 1 - ROUND, c, i] for c in range(3)]
        prev = [hist2_ref[n - 2 - ROUND, c, i] if n - 1 > ROUND else hist1_ref[n - 2, c, i] for c in range(3)]
        correlate(corr_ref, i, e, now, prev, corr_ref if level > 1 else None)

    def dest(kind, c, i, level):
        if kind == "E":
            if 0 <= i < width:
                return e_out, (c, i)
            return es_ref, (c, i + 1)
        if kind == "H":
            return hs_ref, (c, i + 2)
        return ps_ref, (c, i + 1)

    round_body(planes, meta, coef_ref, coefh_ref, a_ref, b_ref, True, inject, extra, dest, (oa_ref, ob_ref), seen)


def adjoint_two_kernel(meta, e_ref, hs_in, ps_in, coef_ref, coefh_ref, maps_ref, maps2_ref, e0_ref, hist1_ref, ey2_ref, eyh_ref,
                       corr_in, b_ref, a_ref, corr_ref, es_ref, hs_ref, ps_ref):
    width = e_ref.shape[1]
    steps = 2 * ROUND
    planes = state_planes(e_ref, hs_in, ps_in)

    def ey(n, i):
        if 0 <= i < width:
            return hist1_ref[n - 1, 1, i]
        if n == 3:
            return eyh_ref[0 if i < 0 else 1]
        return ey2_ref[0 if i < 0 else 1]

    def inject(level, i):
        n = steps + 1 - ROUND - level
        seen_at = maps_ref[ROUND + 1, i + 2] if n == ROUND else maps2_ref[ROUND - 1 - n, i + 2]
        return maps_ref[0, i + 2] * ey(n, i) - seen_at

    def seen(level, i, e):
        if not 0 <= i < width:
            return
        n = steps + 1 - ROUND - level
        now = [hist1_ref[n - 1, c, i] for c in range(3)]
        prev = [hist1_ref[n - 2, c, i] if n > 1 else e0_ref[c, i] for c in range(3)]
        correlate(corr_ref, i, e, now, prev, corr_ref if level > 1 else corr_in)

    round_body(planes, meta, coef_ref, coefh_ref, a_ref, b_ref, False, inject, None,
               scratch_dest(es_ref, hs_ref, ps_ref), None, seen)


def call(body, name, inputs, outs, scratch=(), remote=(), work=10**10):
    vmem = pl.BlockSpec(memory_space=pltpu.VMEM)
    stay = pl.BlockSpec(memory_space=pltpu.HBM)
    return pl.pallas_call(
        body,
        name=name,
        out_shape=[jax.ShapeDtypeStruct(s, F32) for s in outs],
        in_specs=[vmem] * len(inputs) + [stay] * len(remote),
        out_specs=[vmem] * len(outs),
        scratch_shapes=[s if not isinstance(s, tuple) else pltpu.VMEM(s, F32) for s in scratch],
        cost_estimate=pl.CostEstimate(flops=work, transcendentals=0, bytes_accessed=0),
        compiler_params=pltpu.CompilerParams(vmem_limit_bytes=48 * 1024 * 1024),
    )(*inputs, *[pltpu.with_memory_space_constraint(x, pltpu.HBM) for x in remote])


def per_device(
    electric,
    magnetic,
    polar,
    adj_electric,
    adj_magnetic,
    adj_polar,
    permittivity,
    conductivity,
    debye_class,
    debye_rate,
    debye_strength,
    wavelet,
    src_cell,
    src_sign,
    rec_owner,
    rec_pos,
    observed,
):
    width, depth, span = permittivity.shape
    steps = wavelet.shape[0]
    nsub = lax.axis_size("sub")
    nshot = lax.axis_size("shot")
    mine = lax.axis_index("sub")
    facts = jnp.stack([mine, 1 - mine % 2, jnp.minimum(mine, 1)]).astype(F32)
    meta = jnp.broadcast_to(jnp.pad(facts, (0, 5))[:, None], (8, 128))
    plane = (depth, span)

    in_x, rest = split_index(rec_pos[0], width)
    rec_y, rec_z = split_index(rest, span)
    rec_row = (rec_owner[0, :, 0] * width + in_x) * depth + rec_z
    listed = jnp.concatenate([rec_row[None].astype(F32), rec_y[None].astype(F32), observed[0]], axis=0)
    def receivers(name, which):
        (maps,) = call(
            lambda *refs: receiver_kernel(width, depth, which, *refs),
            name,
            [meta, got],
            [(len(which), width + 4, *plane)],
            [(len(which) * (width + 4) * depth, span)],
        )
        return maps

    fields = (electric[0], magnetic[0], polar[0])
    adjoint = (adj_electric[0], adj_magnetic[0], adj_polar[0])

    own = (3, width, *plane)
    classes = debye_rate.shape[0]
    tab_rows = 2 * classes + steps
    *fields, coef, src, tab, a1, b1 = call(
        lambda *refs: first_kernel(width * nsub, *refs),
        "first",
        [meta],
        [own, own, own, (4, width, *plane), (width + 2, *plane), (tab_rows, span), (17, *plane), (17, *plane)],
        [
            (width, *plane),
            (width, *plane),
            pltpu.VMEM((width, *plane), jnp.int32),
            pltpu.VMEM(src_cell.shape, jnp.int32),
            pltpu.VMEM(src_sign.shape, jnp.int32),
            pltpu.SMEM(debye_rate.shape, F32),
            pltpu.SMEM(debye_strength.shape, F32),
            pltpu.SMEM(wavelet.shape, F32),
            pltpu.SemaphoreType.DMA((11,)),
        ],
        [*fields, permittivity, conductivity, debye_class, src_cell, src_sign, debye_rate, debye_strength, wavelet],
    )
    got_a1, got_b1 = exchange(a1, b1)
    listed, b1 = lax.optimization_barrier((listed, b1))
    got = lax.all_to_all(jnp.broadcast_to(listed[None], (nsub, *listed.shape)), "sub", 0, 0)
    got, got_a1, got_b1 = lax.optimization_barrier((got, got_a1, got_b1))
    e_sh, h_sh, p_sh = (3, width + 2, *plane), (3, width + 3, *plane), (3, width + 2, *plane)
    hist1, hs, ps, coefh, ey2, a2, b2 = call(
        forward_one_kernel,
        "forward_one",
        [meta, tab, *fields, coef, src, got_b1, got_a1],
        [(ROUND, 3, width, *plane), h_sh, p_sh, (2, 4, *plane), (2, *plane), (8, *plane), (8, *plane)],
        [e_sh],
    )
    got, coef, a2, b2 = lax.optimization_barrier((got, coef, a2, b2))
    got_a2, got_b2 = exchange(a2, b2)
    a3, b3 = call(adjoint_first_kernel, "adjoint_first", [meta, *adjoint, coef], [(14, *plane), (14, *plane)])
    got_a3, got_b3 = exchange(a3, b3)
    hist2, eyh, a4, b4 = call(
        forward_two_kernel,
        "forward_two",
        [meta, tab, hist1, hs, ps, coef, coefh, src, got_b2, got_a2],
        [(ROUND, 3, width, *plane), (4, *plane), (2, *plane), (2, *plane)],
        [e_sh, h_sh, p_sh],
    )
    got, a4, b4 = lax.optimization_barrier((got, a4, b4))
    got_a4, got_b4 = exchange(a4, b4)
    maps = receivers("receivers_late", (0, *range(steps, ROUND - 1, -1)))
    e_adj, hs, ps, corr, a5, b5 = call(
        adjoint_one_kernel,
        "adjoint_one",
        [meta, *adjoint, coef, coefh, maps, hist1, hist2, eyh, got_b3, got_a3, got_b4, got_a4],
        [(3, width, *plane), h_sh, p_sh, (2, width, *plane), (8, *plane), (8, *plane)],
        [e_sh],
    )
    got, a5, b5 = lax.optimization_barrier((got, a5, b5))
    got_a5, got_b5 = exchange(a5, b5)
    maps2 = receivers("receivers_early", tuple(range(ROUND - 1, 0, -1)))
    (corr,) = call(
        adjoint_two_kernel,
        "adjoint_two",
        [meta, e_adj, hs, ps, coef, coefh, maps, maps2, fields[0], hist1, ey2, eyh, corr, got_b5, got_a5],
        [(2, width, *plane)],
        [e_sh, h_sh, p_sh],
    )
    total = shot_sum(corr)
    return (-(total[0] / (steps * nshot)), -(total[1] / (steps * nshot)))


def solution(mesh):
    in_specs = (
        P("shot", None, "sub", None, None),
        P("shot", None, "sub", None, None),
        P("shot", None, "sub", None, None),
        P("shot", None, "sub", None, None),
        P("shot", None, "sub", None, None),
        P("shot", None, "sub", None, None),
        P("sub", None, None),
        P("sub", None, None),
        P("sub", None, None),
        P(),
        P(),
        P(),
        P("shot", None),
        P("shot", None),
        P("shot", "sub", None),
        P("shot", "sub"),
        P("shot", None, "sub"),
    )
    out_specs = (P("sub", None, None), P("sub", None, None))
    return jax.shard_map(
        per_device, mesh=mesh, in_specs=in_specs, out_specs=out_specs, check_vma=False
    )
```

```python
import jax
import jax.numpy as jnp
from jax import lax
from jax.experimental import pallas as pl
from jax.experimental.pallas import tpu as pltpu
from jax.sharding import PartitionSpec as P

ROUND = 3
F32 = jnp.float32


def pair_swap(block, axis, first):
    route = []
    for i in range(first, lax.axis_size(axis) - 1, 2):
        route += [(i, i + 1), (i + 1, i)]
    return lax.ppermute(block, axis, route)


def exchange(inner, outer):
    got_outer = pair_swap(outer, "sub", 1)
    got_inner = pair_swap(inner, "sub", 0)
    return got_inner, got_outer


def shot_sum(x):
    n = lax.axis_size("shot")
    if n & (n - 1):
        return lax.psum(x, "shot")
    flip = 1
    while flip < n:
        x = x + lax.ppermute(x, "shot", [(i, i ^ flip) for i in range(n)])
        flip = 2 * flip + 1
    return x


def split_index(v, n):
    if n & (n - 1) == 0:
        return v & (n - 1), v >> (n.bit_length() - 1)
    return v % n, v // n


def ahead(u, axis):
    n = u.shape[axis]
    edge = lax.broadcasted_iota(jnp.int32, u.shape, axis) == n - 1
    return jnp.where(edge, 0.0, pltpu.roll(u, n - 1, axis))


def behind(u, axis):
    edge = lax.broadcasted_iota(jnp.int32, u.shape, axis) == 0
    return jnp.where(edge, 0.0, pltpu.roll(u, 1, axis))


def dfy(u):
    return ahead(u, 1) - u


def dfz(u):
    return ahead(u, 0) - u


def dby(u):
    return u - behind(u, 1)


def dbz(u):
    return u - behind(u, 0)


def h_step(h, e, e_next, keep=None, parts=(0, 1, 2)):
    ex, ey, ez = e[0], e[1], e[2]
    new = {}
    if 0 in parts:
        new[0] = h[0] - 0.5 * (dfy(ez) - dfz(ey))
    if 1 in parts:
        ahead_z = -ez if e_next is None else (e_next[2] if keep is None else e_next[2] * keep) - ez
        new[1] = h[1] - 0.5 * (dfz(ex) - ahead_z)
    if 2 in parts:
        ahead_y = -ey if e_next is None else (e_next[1] if keep is None else e_next[1] * keep) - ey
        new[2] = h[2] - 0.5 * (ahead_y - dfy(ex))
    return new


def e_step(e, h, h_prev, p, coef, inject, parts=(0, 1, 2)):
    ca, cb = coef[0], coef[1]
    new = {}
    for c in parts:
        if c == 0:
            curl = dby(h[2]) - dbz(h[1])
        elif c == 1:
            curl = dbz(h[0]) - (h[2] if h_prev is None else h[2] - h_prev[2])
        else:
            curl = (h[1] if h_prev is None else h[1] - h_prev[1]) - dby(h[0])
        new[c] = ca * e[c] + cb * (curl - p[c])
        if c == 1:
            new[c] = new[c] + inject
    return new


def p_step(p, e_new, coef):
    return {c: coef[2] * p[c] + coef[3] * e_new[c] for c in e_new}


class Planes:
    def __init__(self):
        self.at = {}

    def put(self, key, ref, *idx):
        self.at[key] = (ref, idx)

    def get(self, kind, c, i):
        ref, idx = self.at[kind, c, i]
        return ref[idx]

    def triple(self, kind, i, parts=(0, 1, 2)):
        return {c: self.get(kind, c, i) for c in parts}


def is_even(meta, shape):
    return jnp.broadcast_to(meta[1:2, :], shape) > 0.5


def pick(even, a_ref, b_ref, k, low):
    a, b = a_ref[k], b_ref[k]
    return jnp.where(even, b, a) if low else jnp.where(even, a, b)


def emit(even, a_ref, b_ref, k, right, left):
    a_ref[k] = jnp.where(even, right, left)
    b_ref[k] = jnp.where(even, left, right)


def edge_values(planes, coef_of, inject):
    last = planes.last
    lo = last - ROUND + 1
    e, h, p = ({i: planes.triple(kind, i) for i in range(lo, last + 1)} for kind in "EHP")
    right = []
    for step in range(1, ROUND + 1):
        parts = (1, 2) if step == ROUND else (0, 1, 2)
        for i in range(lo + step - 1, last + 1):
            h[i].update(h_step(h[i], e[i], e[i + 1] if i < last else None, parts=parts))
        right += [h[last][1], h[last][2]]
        if step < ROUND:
            for i in range(lo + step, last + 1):
                e[i] = e_step(e[i], h[i], h[i - 1], p[i], coef_of(i), inject(step, i))
                p[i] = p_step(p[i], e[i], coef_of(i))
    e, h, p = ({i: planes.triple(kind, i) for i in range(ROUND)} for kind in "EHP")
    left = [e[0][1], e[0][2]]
    for step in range(1, ROUND):
        for i in range(ROUND - step):
            h[i] = h_step(h[i], e[i], e[i + 1])
        for i in range(ROUND - step):
            parts = (0, 1, 2) if i < ROUND - step - 1 else (1, 2)
            e[i] = e_step(e[i], h[i], h[i - 1] if i > 0 else None, p[i], coef_of(i), inject(step, i), parts)
            p[i] = p_step(p[i], e[i], coef_of(i))
        left += [e[0][1], e[0][2]]
    return right, left


def emit_all(even, a_ref, b_ref, right, left, first=0):
    for k, (r, l) in enumerate(zip(right, left)):
        emit(even, a_ref, b_ref, first + k, r, l)


def own_planes(e_ref, h_ref, p_ref, level=None):
    planes = Planes()
    width = h_ref.shape[1]
    planes.last = width - 1
    for i in range(width):
        for c in range(3):
            planes.put(("E", c, i), e_ref, *((c, i) if level is None else (level, c, i)))
            planes.put(("H", c, i), h_ref, c, i)
            planes.put(("P", c, i), p_ref, c, i)
    return planes


def source_map(cell_ref, sign_ref, mine, width, depth, span, full_x):
    flat = cell_ref[...]
    x, rest = split_index(flat, full_x)
    y, z = split_index(rest, span)
    n = flat.shape[1]
    row = (x - jnp.broadcast_to(mine, (1, n)) * width) * depth + z
    rows = width * depth
    hot = lax.broadcasted_iota(jnp.int32, (rows, n), 0) == row
    amp = (2 * sign_ref[...] - 1).astype(F32)
    where_y = lax.broadcasted_iota(jnp.int32, (span, n), 0) == y
    left = jnp.where(hot, 1.0, 0.0).astype(jnp.bfloat16)
    right = jnp.where(where_y, amp, 0.0).astype(jnp.bfloat16)
    return lax.dot_general(left, right, (((1,), (1,)), ((), ())), preferred_element_type=F32)


def first_kernel(full_x, meta, e_in, h_in, p_in, perm_in, cond_in, cls_in, cells_in, signs_in, rate_in, strength_in,
                 wavelet_in, e_ref, h_ref, p_ref, coef_ref, src_ref, tab_ref, a_ref, b_ref, perm, cond, cls, cells, signs,
                 rate_t, strength_t, wavelet, sems):
    width, depth, span = perm.shape
    even = is_even(meta, (depth, span))
    moves = [(cells_in, cells), (signs_in, signs), (wavelet_in, wavelet), (rate_in, rate_t), (strength_in, strength_t)]
    moves += [(perm_in, perm), (cond_in, cond), (cls_in, cls), (e_in, e_ref), (h_in, h_ref), (p_in, p_ref)]
    copies = [pltpu.make_async_copy(a, b, sems.at[k]) for k, (a, b) in enumerate(moves)]
    for copy in copies:
        copy.start()
    for copy in copies[:5]:
        copy.wait()
    listed = [rate_t[k] for k in range(rate_t.shape[0])]
    listed += [(1.0 - rate_t[k]) * strength_t[k] for k in range(rate_t.shape[0])]
    listed += [wavelet[k] for k in range(wavelet.shape[0])]
    for k, value in enumerate(listed):
        tab_ref[k:k + 1, :] = jnp.full((1, span), value, F32)
    src = source_map(cells, signs, meta[0:1, 0:1].astype(jnp.int32), width, depth, span, full_x)
    src_ref[...] = src.reshape(width, depth, span)
    for copy in copies[5:8]:
        copy.wait()
    for i in range(width):
        ratio = cond[i] / (2.0 * perm[i])
        coef_ref[0, i] = (1.0 - ratio) / (1.0 + ratio)
        coef_ref[1, i] = 0.5 / (perm[i] * (1.0 + ratio))
        kind = cls[i]
        rate = jnp.zeros((depth, span), F32)
        gain = jnp.zeros((depth, span), F32)
        for k in range(rate_t.shape[0]):
            rate = jnp.where(kind == k, rate_t[k], rate)
            gain = jnp.where(kind == k, (1.0 - rate_t[k]) * strength_t[k], gain)
        coef_ref[2, i] = rate
        coef_ref[3, i] = gain
    for copy in copies[8:]:
        copy.wait()
    planes = own_planes(e_ref, h_ref, p_ref)
    right, left = edge_values(planes, lambda i: [coef_ref[k, i] for k in range(4)],
                              lambda step, i: src_ref[i] * wavelet[step - 1])
    last = width - 1
    right += [coef_ref[0, last], coef_ref[1, last], cls[last].astype(F32)]
    left += [coef_ref[0, 0], coef_ref[1, 0], cls[0].astype(F32)]
    emit_all(even, a_ref, b_ref, right, left)


def receiver_kernel(width, depth, which, meta, got, maps_ref, acc):
    rows = width * depth
    span = acc.shape[1]
    blocks, _, n = got.shape
    acc[...] = jnp.zeros(acc.shape, F32)
    first_row = meta[0:1, :] * (width * depth)
    row_at = lax.broadcasted_iota(jnp.int32, (rows, n), 0).astype(F32)
    y_at = lax.broadcasted_iota(jnp.int32, (span, n), 0).astype(F32)
    group = max(g for g in (1, 2, 4, 8) if blocks % g == 0)
    zero = jnp.zeros((rows, n), jnp.bfloat16)

    def block(k, carry):
        left = [[] for _ in which]
        right = []
        for b in range(group):
            at = k * group + b
            hot = row_at == got[at, 0:1, :] - first_row[:, :n]
            at_y = jnp.where(y_at == got[at, 1:2, :], 1.0, 0.0).astype(jnp.bfloat16)
            right += [at_y] * 3
            for part, s in zip(left, which):
                if s == 0:
                    part += [jnp.where(hot, 1.0, 0.0).astype(jnp.bfloat16), zero, zero]
                    continue
                v = got[at, 1 + s:2 + s, :]
                high = v.astype(jnp.bfloat16).astype(F32)
                mid = (v - high).astype(jnp.bfloat16).astype(F32)
                low = (v - high) - mid
                part += [jnp.where(hot, u, 0.0).astype(jnp.bfloat16) for u in (high, mid, low)]
        acc[...] += lax.dot_general(
            jnp.concatenate([jnp.concatenate(part, axis=1) for part in left], axis=0) if len(left) > 1 else jnp.concatenate(left[0], axis=1),
            jnp.concatenate(right, axis=1),
            (((1,), (1,)), ((), ())),
            preferred_element_type=F32,
        )
        return carry

    lax.fori_loop(0, blocks // group, block, 0)
    maps_ref[...] = acc[...].reshape(maps_ref.shape)


def round_body(planes, meta, coef_ref, coefh_ref, a_ref, b_ref, inject, dest, seen=None):
    even = is_even(meta, coef_ref.shape[2:])
    keep = meta[2:3, :]
    last = planes.last

    def coef_of(i):
        return [coef_ref[k, i] for k in range(4)]

    before, after = ([coefh_ref[side, k] for k in range(4)] for side in (0, 1))
    zero = jnp.zeros(coef_ref.shape[2:], F32)
    none = {c: zero for c in range(3)}

    def store(kind, c, i, level, value):
        ref, idx = dest(kind, c, i, level)
        ref[idx] = value
        planes.put((kind, c, i), ref, *idx)

    low_e = low_h = low_p = high_e = high_p = None
    for level in range(1, ROUND + 1):
        sent = 2 * (level - 1)
        edge = {c: planes.get("E", c, 0) * keep for c in (1, 2)}
        if level == 1:
            low_h = {0: zero, 1: 0.5 * edge[2], 2: -0.5 * edge[1]}
            far = None
        else:
            far = {1: 0.5 * low_e[2], 2: -0.5 * low_e[1]}
            low_h.update(h_step(low_h, low_e, edge, parts=(0, 1, 2) if level < ROUND else (1, 2)))
        if level == 1:
            low_e = {0: before[1] * (dby(low_h[2]) - dbz(low_h[1])), 1: -(before[1] * low_h[2]), 2: before[1] * low_h[1]}
            low_p = {c: before[3] * low_e[c] for c in range(3)}
        elif level < ROUND:
            low_e = e_step(low_e, low_h, far, low_p, before, 0.0)
            low_p = p_step(low_p, low_e, before)
        h_prev = {c: low_h[c] + pick(even, a_ref, b_ref, sent + c - 1, True) for c in (1, 2)}
        for i in range(last + 1):
            e = planes.triple("E", i)
            if i < last:
                e_next = planes.triple("E", i + 1, (1, 2))
            else:
                e_next = {c: pick(even, a_ref, b_ref, sent + c - 1, False) for c in (1, 2)}
                if level > 1:
                    e_next = {c: e_next[c] + high_e[c] for c in (1, 2)}
            h = h_step(planes.triple("H", i), e, e_next)
            cf = coef_of(i)
            new = e_step(e, h, h_prev, planes.triple("P", i), cf, inject(level, i))
            pn = p_step(planes.triple("P", i), new, cf)
            for c in range(3):
                store("H", c, i, level, h[c])
                store("E", c, i, level, new[c])
                store("P", c, i, level, pn[c])
            if seen is not None:
                seen(level, i, new)
            h_prev = h
        if level == 1:
            high_e = {0: zero, 1: after[1] * h_prev[2], 2: -(after[1] * h_prev[1])}
            high_p = {c: after[3] * high_e[c] for c in range(3)}
            high_h = none
        elif level < ROUND:
            high_h = h_step(high_h, high_e, None)
            high_e = e_step(high_e, high_h, h_prev, high_p, after, 0.0)
            high_p = p_step(high_p, high_e, after)


def store_in(e_ref, h_ref, p_ref, by_level=False):
    refs = {"E": e_ref, "H": h_ref, "P": p_ref}

    def dest(kind, c, i, level):
        return refs[kind], ((level - 1, c, i) if kind == "E" and by_level else (c, i))

    return dest


def forward_one_kernel(meta, tab_ref, e_ref, h_ref, p_ref, coef_ref, src_ref, b_ref, a_ref,
                       hist_ref, hs_ref, ps_ref, coefh_ref, oa_ref, ob_ref):
    even = is_even(meta, e_ref.shape[2:])
    classes = (tab_ref.shape[0] - 2 * ROUND) // 2
    wavelet = 2 * classes
    for side in (0, 1):
        coefh_ref[side, 0] = pick(even, a_ref, b_ref, 2 * ROUND, side == 0)
        coefh_ref[side, 1] = pick(even, a_ref, b_ref, 2 * ROUND + 1, side == 0)
        kind = pick(even, a_ref, b_ref, 2 * ROUND + 2, side == 0)
        rate = jnp.zeros(kind.shape, F32)
        gain = jnp.zeros(kind.shape, F32)
        for k in range(classes):
            rate = jnp.where(kind == float(k), tab_ref[k:k + 1, :], rate)
            gain = jnp.where(kind == float(k), tab_ref[classes + k:classes + k + 1, :], gain)
        coefh_ref[side, 2] = rate
        coefh_ref[side, 3] = gain
    planes = own_planes(e_ref, h_ref, p_ref)

    def inject(level, i):
        return src_ref[i] * tab_ref[wavelet + level - 1:wavelet + level, :]

    round_body(planes, meta, coef_ref, coefh_ref, a_ref, b_ref, inject, store_in(hist_ref, hs_ref, ps_ref, True))
    right, left = edge_values(planes, lambda i: [coef_ref[k, i] for k in range(4)], lambda step, i: inject(ROUND + step, i))
    emit_all(even, oa_ref, ob_ref, right, left)


def forward_two_kernel(meta, tab_ref, hist_in, hs_in, ps_in, coef_ref, coefh_ref, src_ref, maps_ref, e_ref, h_ref, p_ref,
                       b_ref, a_ref, hist_ref, oa_ref, ob_ref, hs_ref, ps_ref):
    wavelet = tab_ref.shape[0] - ROUND
    round_body(own_planes(hist_in, hs_in, ps_in, ROUND - 1), meta, coef_ref, coefh_ref, a_ref, b_ref,
               lambda level, i: src_ref[i] * tab_ref[wavelet + level - 1:wavelet + level, :],
               store_in(hist_ref, hs_ref, ps_ref, True))

    def inject(step, i):
        return maps_ref[0, i] * hist_ref[ROUND - step, 1, i] - maps_ref[step, i]

    right, left = edge_values(own_planes(e_ref, h_ref, p_ref), lambda i: [coef_ref[k, i] for k in range(4)], inject)
    emit_all(is_even(meta, e_ref.shape[2:]), oa_ref, ob_ref, right, left)


def correlate(corr_ref, i, b, now, prev, add):
    eps = b[0] * (now[0] - prev[0]) + b[1] * (now[1] - prev[1]) + b[2] * (now[2] - prev[2])
    sig = b[0] * now[0] + b[1] * now[1] + b[2] * now[2]
    if add is not None:
        eps, sig = eps + add[0, i], sig + add[1, i]
    corr_ref[0, i] = eps
    corr_ref[1, i] = sig


def adjoint_one_kernel(meta, e_ref, h_ref, p_ref, coef_ref, coefh_ref, maps_ref, maps2_ref, hist1_ref, hist2_ref,
                       b_ref, a_ref, e_out, hs_ref, ps_ref, corr_ref, oa_ref, ob_ref):
    planes = own_planes(e_ref, h_ref, p_ref)

    def seen(level, i, e):
        n = ROUND - level
        now = [hist2_ref[n, c, i] for c in range(3)]
        prev = [hist2_ref[n - 1, c, i] if n > 0 else hist1_ref[ROUND - 1, c, i] for c in range(3)]
        correlate(corr_ref, i, e, now, prev, corr_ref if level > 1 else None)

    def inject(level, i):
        return maps_ref[0, i] * hist2_ref[ROUND - level, 1, i] - maps_ref[level, i]

    def inject_next(step, i):
        return maps_ref[0, i] * hist1_ref[ROUND - step, 1, i] - maps2_ref[step - 1, i]

    round_body(planes, meta, coef_ref, coefh_ref, a_ref, b_ref, inject, store_in(e_out, hs_ref, ps_ref), seen)
    right, left = edge_values(planes, lambda i: [coef_ref[k, i] for k in range(4)], inject_next)
    emit_all(is_even(meta, e_ref.shape[2:]), oa_ref, ob_ref, right, left)


def adjoint_two_kernel(meta, e_ref, hs_in, ps_in, coef_ref, coefh_ref, maps_ref, maps2_ref, e0_ref, hist1_ref,
                       corr_in, b_ref, a_ref, corr_ref, es_ref, hs_ref, ps_ref):
    def seen(level, i, e):
        n = ROUND - level
        now = [hist1_ref[n, c, i] for c in range(3)]
        prev = [hist1_ref[n - 1, c, i] if n > 0 else e0_ref[c, i] for c in range(3)]
        correlate(corr_ref, i, e, now, prev, corr_ref if level > 1 else corr_in)

    def inject(level, i):
        return maps_ref[0, i] * hist1_ref[ROUND - level, 1, i] - maps2_ref[level - 1, i]

    round_body(own_planes(e_ref, hs_in, ps_in), meta, coef_ref, coefh_ref, a_ref, b_ref, inject,
               store_in(es_ref, hs_ref, ps_ref), seen)


def call(body, name, inputs, outs, scratch=(), remote=(), work=10**10):
    vmem = pl.BlockSpec(memory_space=pltpu.VMEM)
    stay = pl.BlockSpec(memory_space=pltpu.HBM)
    return pl.pallas_call(
        body,
        name=name,
        out_shape=[jax.ShapeDtypeStruct(s, F32) for s in outs],
        in_specs=[vmem] * len(inputs) + [stay] * len(remote),
        out_specs=[vmem] * len(outs),
        scratch_shapes=[s if not isinstance(s, tuple) else pltpu.VMEM(s, F32) for s in scratch],
        cost_estimate=pl.CostEstimate(flops=work, transcendentals=0, bytes_accessed=0),
        compiler_params=pltpu.CompilerParams(vmem_limit_bytes=48 * 1024 * 1024),
    )(*inputs, *[pltpu.with_memory_space_constraint(x, pltpu.HBM) for x in remote])


def per_device(
    electric,
    magnetic,
    polar,
    adj_electric,
    adj_magnetic,
    adj_polar,
    permittivity,
    conductivity,
    debye_class,
    debye_rate,
    debye_strength,
    wavelet,
    src_cell,
    src_sign,
    rec_owner,
    rec_pos,
    observed,
):
    width, depth, span = permittivity.shape
    steps = wavelet.shape[0]
    nsub = lax.axis_size("sub")
    nshot = lax.axis_size("shot")
    mine = lax.axis_index("sub")
    facts = jnp.stack([mine, 1 - mine % 2, jnp.minimum(mine, 1)]).astype(F32)
    meta = jnp.broadcast_to(jnp.pad(facts, (0, 5))[:, None], (8, 128))
    plane = (depth, span)

    in_x, rest = split_index(rec_pos[0], width)
    rec_y, rec_z = split_index(rest, span)
    rec_row = (rec_owner[0, :, 0] * width + in_x) * depth + rec_z
    listed = jnp.concatenate([rec_row[None].astype(F32), rec_y[None].astype(F32), observed[0]], axis=0)
    def receivers(name, which):
        (maps,) = call(
            lambda *refs: receiver_kernel(width, depth, which, *refs),
            name,
            [meta, got],
            [(len(which), width, *plane)],
            [(len(which) * width * depth, span)],
            work=10**9,
        )
        return maps

    fields = (electric[0], magnetic[0], polar[0])
    adjoint = (adj_electric[0], adj_magnetic[0], adj_polar[0])

    own = (3, width, *plane)
    classes = debye_rate.shape[0]
    tab_rows = 2 * classes + steps
    *fields, coef, src, tab, a1, b1 = call(
        lambda *refs: first_kernel(width * nsub, *refs),
        "first",
        [meta],
        [own, own, own, (4, width, *plane), (width, *plane), (tab_rows, span), *[(2 * ROUND + 3, *plane)] * 2],
        [
            (width, *plane),
            (width, *plane),
            pltpu.VMEM((width, *plane), jnp.int32),
            pltpu.VMEM(src_cell.shape, jnp.int32),
            pltpu.VMEM(src_sign.shape, jnp.int32),
            pltpu.SMEM(debye_rate.shape, F32),
            pltpu.SMEM(debye_strength.shape, F32),
            pltpu.SMEM(wavelet.shape, F32),
            pltpu.SemaphoreType.DMA((11,)),
        ],
        [*fields, permittivity, conductivity, debye_class, src_cell, src_sign, debye_rate, debye_strength, wavelet],
    )
    got_a1, got_b1 = exchange(a1, b1)
    listed, b1 = lax.optimization_barrier((listed, b1))
    got = lax.all_to_all(jnp.broadcast_to(listed[None], (nsub, *listed.shape)), "sub", 0, 0)
    edges = [(2 * ROUND, *plane)] * 2
    hist1, hs, ps, coefh, a2, b2 = call(
        forward_one_kernel,
        "forward_one",
        [meta, tab, *fields, coef, src, got_b1, got_a1],
        [(ROUND, *own), own, own, (2, 4, *plane), *edges],
    )
    got, hs = lax.optimization_barrier((got, hs))
    got_a2, got_b2 = exchange(a2, b2)
    maps = receivers("receivers_late", (0, *range(steps, ROUND, -1)))
    hist2, a3, b3 = call(
        forward_two_kernel,
        "forward_two",
        [meta, tab, hist1, hs, ps, coef, coefh, src, maps, *adjoint, got_b2, got_a2],
        [(ROUND, *own), *edges],
        [own, own],
    )
    got, hist2 = lax.optimization_barrier((got, hist2))
    got_a3, got_b3 = exchange(a3, b3)
    maps2 = receivers("receivers_early", tuple(range(ROUND, 0, -1)))
    e_adj, hs, ps, corr, a4, b4 = call(
        adjoint_one_kernel,
        "adjoint_one",
        [meta, *adjoint, coef, coefh, maps, maps2, hist1, hist2, got_b3, got_a3],
        [own, own, own, (2, width, *plane), *edges],
    )
    got_a4, got_b4 = exchange(a4, b4)
    (corr,) = call(
        adjoint_two_kernel,
        "adjoint_two",
        [meta, e_adj, hs, ps, coef, coefh, maps, maps2, fields[0], hist1, corr, got_b4, got_a4],
        [(2, width, *plane)],
        [own, own, own],
    )
    total = shot_sum(corr)
    return (-(total[0] / (steps * nshot)), -(total[1] / (steps * nshot)))


def solution(mesh):
    in_specs = (
        P("shot", None, "sub", None, None),
        P("shot", None, "sub", None, None),
        P("shot", None, "sub", None, None),
        P("shot", None, "sub", None, None),
        P("shot", None, "sub", None, None),
        P("shot", None, "sub", None, None),
        P("sub", None, None),
        P("sub", None, None),
        P("sub", None, None),
        P(),
        P(),
        P(),
        P("shot", None),
        P("shot", None),
        P("shot", "sub", None),
        P("shot", "sub"),
        P("shot", None, "sub"),
    )
    out_specs = (P("sub", None, None), P("sub", None, None))
    return jax.shard_map(
        per_device, mesh=mesh, in_specs=in_specs, out_specs=out_specs, check_vma=False
    )
```

```python
import jax
import jax.numpy as jnp
from jax import lax
from jax.experimental import pallas as pl
from jax.experimental.pallas import tpu as pltpu
from jax.sharding import PartitionSpec as P

ROUND = 3
F32 = jnp.float32


def pair_swap(block, axis, first):
    route = []
    for i in range(first, lax.axis_size(axis) - 1, 2):
        route += [(i, i + 1), (i + 1, i)]
    return lax.ppermute(block, axis, route)


def exchange(inner, outer):
    got_outer = pair_swap(outer, "sub", 1)
    got_inner = pair_swap(inner, "sub", 0)
    return got_inner, got_outer


def shot_sum(x):
    n = lax.axis_size("shot")
    if n & (n - 1):
        return lax.psum(x, "shot")
    flip = 1
    while flip < n:
        x = x + lax.ppermute(x, "shot", [(i, i ^ flip) for i in range(n)])
        flip = 2 * flip + 1
    return x


def split_index(v, n):
    if n & (n - 1) == 0:
        return v & (n - 1), v >> (n.bit_length() - 1)
    return v % n, v // n


def ahead(u, axis):
    n = u.shape[axis]
    edge = lax.broadcasted_iota(jnp.int32, u.shape, axis) == n - 1
    return jnp.where(edge, 0.0, pltpu.roll(u, n - 1, axis))


def behind(u, axis):
    edge = lax.broadcasted_iota(jnp.int32, u.shape, axis) == 0
    return jnp.where(edge, 0.0, pltpu.roll(u, 1, axis))


def dfy(u):
    return ahead(u, 1) - u


def dfz(u):
    return ahead(u, 0) - u


def dby(u):
    return u - behind(u, 1)


def dbz(u):
    return u - behind(u, 0)


def h_step(h, e, e_next, keep=None, parts=(0, 1, 2)):
    ex, ey, ez = e[0], e[1], e[2]
    new = {}
    if 0 in parts:
        new[0] = h[0] - 0.5 * (dfy(ez) - dfz(ey))
    if 1 in parts:
        ahead_z = -ez if e_next is None else (e_next[2] if keep is None else e_next[2] * keep) - ez
        new[1] = h[1] - 0.5 * (dfz(ex) - ahead_z)
    if 2 in parts:
        ahead_y = -ey if e_next is None else (e_next[1] if keep is None else e_next[1] * keep) - ey
        new[2] = h[2] - 0.5 * (ahead_y - dfy(ex))
    return new


def e_step(e, h, h_prev, p, coef, inject, parts=(0, 1, 2)):
    ca, cb = coef[0], coef[1]
    new = {}
    for c in parts:
        if c == 0:
            curl = dby(h[2]) - dbz(h[1])
        elif c == 1:
            curl = dbz(h[0]) - (h[2] if h_prev is None else h[2] - h_prev[2])
        else:
            curl = (h[1] if h_prev is None else h[1] - h_prev[1]) - dby(h[0])
        new[c] = ca * e[c] + cb * (curl - p[c])
        if c == 1:
            new[c] = new[c] + inject
    return new


def p_step(p, e_new, coef):
    return {c: coef[2] * p[c] + coef[3] * e_new[c] for c in e_new}


class Planes:
    def __init__(self):
        self.at = {}

    def put(self, key, ref, *idx):
        self.at[key] = (ref, idx)

    def get(self, kind, c, i):
        ref, idx = self.at[kind, c, i]
        return ref[idx]

    def triple(self, kind, i, parts=(0, 1, 2)):
        return {c: self.get(kind, c, i) for c in parts}


def is_even(meta, shape):
    return jnp.broadcast_to(meta[1:2, :], shape) > 0.5


def pick(even, a_ref, b_ref, k, low):
    a, b = a_ref[k], b_ref[k]
    return jnp.where(even, b, a) if low else jnp.where(even, a, b)


def emit(even, a_ref, b_ref, k, right, left):
    a_ref[k] = jnp.where(even, right, left)
    b_ref[k] = jnp.where(even, left, right)


def edge_values(planes, coef_of, inject, h_out):
    last = planes.last
    lo = last - ROUND + 1
    e0 = {i: planes.triple("E", i) for i in range(last + 1)}
    h1 = {i: h_step(planes.triple("H", i), e0[i], e0[i + 1] if i < last else None) for i in range(last + 1)}
    p0 = {i: planes.triple("P", i) for i in range(last + 1)}
    raw = planes.triple("H", last)
    for c in range(3):
        for i in range(last):
            h_out[c, i] = h1[i][c]
        h_out[c, last] = raw[c]
    e, h, p = dict(e0), dict(h1), dict(p0)
    right = []
    for step in range(1, ROUND + 1):
        if step > 1:
            parts = (1, 2) if step == ROUND else (0, 1, 2)
            for i in range(lo + step - 1, last + 1):
                h[i] = {**h[i], **h_step(h[i], e[i], e[i + 1] if i < last else None, parts=parts)}
        right += [h[last][1], h[last][2]]
        if step < ROUND:
            for i in range(lo + step, last + 1):
                e[i] = e_step(e[i], h[i], h[i - 1], p[i], coef_of(i), inject(step, i))
                p[i] = p_step(p[i], e[i], coef_of(i))
    e, h, p = dict(e0), dict(h1), dict(p0)
    left = [e[0][1], e[0][2]]
    for step in range(1, ROUND):
        if step > 1:
            for i in range(ROUND - step):
                h[i] = h_step(h[i], e[i], e[i + 1])
        for i in range(ROUND - step):
            parts = (0, 1, 2) if i < ROUND - step - 1 else (1, 2)
            e[i] = e_step(e[i], h[i], h[i - 1] if i > 0 else None, p[i], coef_of(i), inject(step, i), parts)
            p[i] = p_step(p[i], e[i], coef_of(i))
        left += [e[0][1], e[0][2]]
    return right, left


def emit_all(even, a_ref, b_ref, right, left, first=0):
    for k, (r, l) in enumerate(zip(right, left)):
        emit(even, a_ref, b_ref, first + k, r, l)


def own_planes(e_ref, h_ref, p_ref, level=None):
    planes = Planes()
    width = h_ref.shape[1]
    planes.last = width - 1
    for i in range(width):
        for c in range(3):
            planes.put(("E", c, i), e_ref, *((c, i) if level is None else (level, c, i)))
            planes.put(("H", c, i), h_ref, c, i)
            planes.put(("P", c, i), p_ref, c, i)
    return planes


def source_map(cell_ref, sign_ref, mine, width, depth, span, full_x):
    flat = cell_ref[...]
    x, rest = split_index(flat, full_x)
    y, z = split_index(rest, span)
    n = flat.shape[1]
    row = (x - jnp.broadcast_to(mine, (1, n)) * width) * depth + z
    rows = width * depth
    hot = lax.broadcasted_iota(jnp.int32, (rows, n), 0) == row
    amp = (2 * sign_ref[...] - 1).astype(F32)
    where_y = lax.broadcasted_iota(jnp.int32, (span, n), 0) == y
    left = jnp.where(hot, 1.0, 0.0).astype(jnp.bfloat16)
    right = jnp.where(where_y, amp, 0.0).astype(jnp.bfloat16)
    return lax.dot_general(left, right, (((1,), (1,)), ((), ())), preferred_element_type=F32)


def first_kernel(full_x, meta, e_in, h_in, p_in, perm_in, cond_in, cls_in, cells_in, signs_in, rate_in, strength_in,
                 wavelet_in, e_ref, h_ref, p_ref, coef_ref, src_ref, tab_ref, a_ref, b_ref, perm, cond, cls, cells, signs,
                 rate_t, strength_t, wavelet, sems):
    width, depth, span = perm.shape
    even = is_even(meta, (depth, span))
    moves = [(cells_in, cells), (signs_in, signs), (wavelet_in, wavelet), (rate_in, rate_t), (strength_in, strength_t)]
    moves += [(perm_in, perm), (cond_in, cond), (cls_in, cls), (e_in, e_ref), (h_in, h_ref), (p_in, p_ref)]
    copies = [pltpu.make_async_copy(a, b, sems.at[k]) for k, (a, b) in enumerate(moves)]
    for copy in copies:
        copy.start()
    for copy in copies[:5]:
        copy.wait()
    for k in range(wavelet.shape[0]):
        tab_ref[k:k + 1, :] = jnp.full((1, span), wavelet[k], F32)
    src = source_map(cells, signs, meta[0:1, 0:1].astype(jnp.int32), width, depth, span, full_x)
    src_ref[...] = src.reshape(width, depth, span)
    for copy in copies[5:8]:
        copy.wait()
    for i in range(width):
        ratio = cond[i] / (2.0 * perm[i])
        coef_ref[0, i] = (1.0 - ratio) / (1.0 + ratio)
        coef_ref[1, i] = 0.5 / (perm[i] * (1.0 + ratio))
        kind = cls[i]
        rate = jnp.zeros((depth, span), F32)
        gain = jnp.zeros((depth, span), F32)
        for k in range(rate_t.shape[0]):
            rate = jnp.where(kind == k, rate_t[k], rate)
            gain = jnp.where(kind == k, (1.0 - rate_t[k]) * strength_t[k], gain)
        coef_ref[2, i] = rate
        coef_ref[3, i] = gain
    for copy in copies[8:]:
        copy.wait()
    planes = own_planes(e_ref, h_ref, p_ref)
    right, left = edge_values(planes, lambda i: [coef_ref[k, i] for k in range(4)],
                              lambda step, i: src_ref[i] * wavelet[step - 1], h_ref)
    last = width - 1
    right += [coef_ref[k, last] for k in (0, 1, 3)]
    left += [coef_ref[k, 0] for k in (0, 1, 3)]
    emit_all(even, a_ref, b_ref, right, left)


def receiver_kernel(width, depth, which, meta, got, maps_ref, acc):
    rows = width * depth
    span = acc.shape[1]
    blocks, _, n = got.shape
    acc[...] = jnp.zeros(acc.shape, F32)
    first_row = meta[0:1, :] * (width * depth)
    row_at = lax.broadcasted_iota(jnp.int32, (rows, n), 0).astype(F32)
    y_at = lax.broadcasted_iota(jnp.int32, (span, n), 0).astype(F32)
    group = max(g for g in (1, 2, 4, 8) if blocks % g == 0)
    zero = jnp.zeros((rows, n), jnp.bfloat16)

    def block(k, carry):
        left = [[] for _ in which]
        right = []
        for b in range(group):
            at = k * group + b
            hot = row_at == got[at, 0:1, :] - first_row[:, :n]
            at_y = jnp.where(y_at == got[at, 1:2, :], 1.0, 0.0).astype(jnp.bfloat16)
            right += [at_y] * 3
            for part, s in zip(left, which):
                if s == 0:
                    part += [jnp.where(hot, 1.0, 0.0).astype(jnp.bfloat16), zero, zero]
                    continue
                v = got[at, 1 + s:2 + s, :]
                high = v.astype(jnp.bfloat16).astype(F32)
                mid = (v - high).astype(jnp.bfloat16).astype(F32)
                low = (v - high) - mid
                part += [jnp.where(hot, u, 0.0).astype(jnp.bfloat16) for u in (high, mid, low)]
        acc[...] += lax.dot_general(
            jnp.concatenate([jnp.concatenate(part, axis=1) for part in left], axis=0) if len(left) > 1 else jnp.concatenate(left[0], axis=1),
            jnp.concatenate(right, axis=1),
            (((1,), (1,)), ((), ())),
            preferred_element_type=F32,
        )
        return carry

    lax.fori_loop(0, blocks // group, block, 0)
    maps_ref[...] = acc[...].reshape(maps_ref.shape)


def round_body(planes, meta, coef_ref, coefh_ref, a_ref, b_ref, inject, dest, seen=None):
    even = is_even(meta, coef_ref.shape[2:])
    keep = meta[2:3, :]
    last = planes.last

    def coef_of(i):
        return [coef_ref[k, i] for k in range(4)]

    before, after = ([coefh_ref[side, k] for k in range(3)] for side in (0, 1))
    zero = jnp.zeros(coef_ref.shape[2:], F32)
    none = {c: zero for c in range(3)}

    def store(kind, c, i, level, value):
        ref, idx = dest(kind, c, i, level)
        ref[idx] = value
        planes.put((kind, c, i), ref, *idx)

    low_e = low_h = low_p = high_e = high_p = None
    for level in range(1, ROUND + 1):
        sent = 2 * (level - 1)
        edge = {c: planes.get("E", c, 0) * keep for c in (1, 2)}
        if level == 1:
            low_h = {0: zero, 1: 0.5 * edge[2], 2: -0.5 * edge[1]}
            far = None
        else:
            far = {1: 0.5 * low_e[2], 2: -0.5 * low_e[1]}
            low_h.update(h_step(low_h, low_e, edge, parts=(0, 1, 2) if level < ROUND else (1, 2)))
        if level == 1:
            low_e = {0: before[1] * (dby(low_h[2]) - dbz(low_h[1])), 1: -(before[1] * low_h[2]), 2: before[1] * low_h[1]}
            low_p = {c: before[2] * low_e[c] for c in range(3)}
        elif level < ROUND:
            low_e = e_step(low_e, low_h, far, low_p, before, 0.0)
        h_prev = {c: low_h[c] + pick(even, a_ref, b_ref, sent + c - 1, True) for c in (1, 2)}
        for i in range(last + 1):
            e = planes.triple("E", i)
            if i < last:
                e_next = planes.triple("E", i + 1, (1, 2))
            else:
                e_next = {c: pick(even, a_ref, b_ref, sent + c - 1, False) for c in (1, 2)}
                if level > 1:
                    e_next = {c: e_next[c] + high_e[c] for c in (1, 2)}
            h = planes.triple("H", i)
            if level > 1 or i == last:
                h = h_step(h, e, e_next)
            cf = coef_of(i)
            new = e_step(e, h, h_prev, planes.triple("P", i), cf, inject(level, i))
            pn = p_step(planes.triple("P", i), new, cf)
            for c in range(3):
                if level > 1 or i == last:
                    store("H", c, i, level, h[c])
                store("E", c, i, level, new[c])
                store("P", c, i, level, pn[c])
            if seen is not None:
                seen(level, i, new)
            h_prev = h
        if level == 1:
            high_e = {0: zero, 1: after[1] * h_prev[2], 2: -(after[1] * h_prev[1])}
            high_p = {c: after[2] * high_e[c] for c in range(3)}
            high_h = none
        elif level < ROUND:
            high_h = h_step(high_h, high_e, None)
            high_e = e_step(high_e, high_h, h_prev, high_p, after, 0.0)


def store_in(e_ref, h_ref, p_ref, by_level=False):
    refs = {"E": e_ref, "H": h_ref, "P": p_ref}

    def dest(kind, c, i, level):
        return refs[kind], ((level - 1, c, i) if kind == "E" and by_level else (c, i))

    return dest


def forward_one_kernel(meta, tab_ref, e_ref, h_ref, p_ref, coef_ref, src_ref, b_ref, a_ref,
                       hist_ref, hs_ref, ps_ref, coefh_ref, oa_ref, ob_ref):
    even = is_even(meta, e_ref.shape[2:])
    wavelet = 0
    for side in (0, 1):
        for k in range(3):
            coefh_ref[side, k] = pick(even, a_ref, b_ref, 2 * ROUND + k, side == 0)
    planes = own_planes(e_ref, h_ref, p_ref)

    def inject(level, i):
        return src_ref[i] * tab_ref[wavelet + level - 1:wavelet + level, :]

    round_body(planes, meta, coef_ref, coefh_ref, a_ref, b_ref, inject, store_in(hist_ref, hs_ref, ps_ref, True))
    right, left = edge_values(planes, lambda i: [coef_ref[k, i] for k in range(4)], lambda step, i: inject(ROUND + step, i), hs_ref)
    emit_all(even, oa_ref, ob_ref, right, left)


def forward_two_kernel(meta, tab_ref, hist_in, hs_in, ps_in, coef_ref, coefh_ref, src_ref, maps_ref, e_ref, h_ref, p_ref,
                       b_ref, a_ref, hist_ref, h_out, oa_ref, ob_ref, hs_ref, ps_ref):
    wavelet = ROUND
    round_body(own_planes(hist_in, hs_in, ps_in, ROUND - 1), meta, coef_ref, coefh_ref, a_ref, b_ref,
               lambda level, i: src_ref[i] * tab_ref[wavelet + level - 1:wavelet + level, :],
               store_in(hist_ref, hs_ref, ps_ref, True))

    def inject(step, i):
        return maps_ref[0, i] * hist_ref[ROUND - step, 1, i] - maps_ref[step, i]

    right, left = edge_values(own_planes(e_ref, h_ref, p_ref), lambda i: [coef_ref[k, i] for k in range(4)], inject, h_out)
    emit_all(is_even(meta, e_ref.shape[2:]), oa_ref, ob_ref, right, left)


def correlate(corr_ref, i, b, now, prev, add):
    eps = b[0] * (now[0] - prev[0]) + b[1] * (now[1] - prev[1]) + b[2] * (now[2] - prev[2])
    sig = b[0] * now[0] + b[1] * now[1] + b[2] * now[2]
    if add is not None:
        eps, sig = eps + add[0, i], sig + add[1, i]
    corr_ref[0, i] = eps
    corr_ref[1, i] = sig


def adjoint_one_kernel(meta, e_ref, h_ref, p_ref, coef_ref, coefh_ref, maps_ref, maps2_ref, hist1_ref, hist2_ref,
                       b_ref, a_ref, e_out, hs_ref, ps_ref, oa_ref, ob_ref):
    planes = own_planes(e_ref, h_ref, p_ref)

    def inject(level, i):
        return maps_ref[0, i] * hist2_ref[ROUND - level, 1, i] - maps_ref[level, i]

    def inject_next(step, i):
        return maps_ref[0, i] * hist1_ref[ROUND - step, 1, i] - maps2_ref[step - 1, i]

    round_body(planes, meta, coef_ref, coefh_ref, a_ref, b_ref, inject, store_in(e_out, hs_ref, ps_ref, True))
    right, left = edge_values(planes, lambda i: [coef_ref[k, i] for k in range(4)], inject_next, hs_ref)
    emit_all(is_even(meta, e_ref.shape[2:]), oa_ref, ob_ref, right, left)


def correlation_kernel(adj_ref, hist1_ref, hist2_ref, corr_ref):
    for i in range(corr_ref.shape[1]):
        for level in range(1, ROUND + 1):
            n = ROUND - level
            e = [adj_ref[level - 1, c, i] for c in range(3)]
            now = [hist2_ref[n, c, i] for c in range(3)]
            prev = [hist2_ref[n - 1, c, i] if n > 0 else hist1_ref[ROUND - 1, c, i] for c in range(3)]
            correlate(corr_ref, i, e, now, prev, corr_ref if level > 1 else None)


def adjoint_two_kernel(meta, e_ref, hs_in, ps_in, coef_ref, coefh_ref, maps_ref, maps2_ref, e0_ref, hist1_ref,
                       corr_in, b_ref, a_ref, corr_ref, es_ref, hs_ref, ps_ref):
    def seen(level, i, e):
        n = ROUND - level
        now = [hist1_ref[n, c, i] for c in range(3)]
        prev = [hist1_ref[n - 1, c, i] if n > 0 else e0_ref[c, i] for c in range(3)]
        correlate(corr_ref, i, e, now, prev, corr_ref if level > 1 else corr_in)

    def inject(level, i):
        return maps_ref[0, i] * hist1_ref[ROUND - level, 1, i] - maps2_ref[level - 1, i]

    round_body(own_planes(e_ref, hs_in, ps_in, ROUND - 1), meta, coef_ref, coefh_ref, a_ref, b_ref, inject,
               store_in(es_ref, hs_ref, ps_ref), seen)


def call(body, name, inputs, outs, scratch=(), remote=(), work=10**10):
    vmem = pl.BlockSpec(memory_space=pltpu.VMEM)
    stay = pl.BlockSpec(memory_space=pltpu.HBM)
    return pl.pallas_call(
        body,
        name=name,
        out_shape=[jax.ShapeDtypeStruct(s, F32) for s in outs],
        in_specs=[vmem] * len(inputs) + [stay] * len(remote),
        out_specs=[vmem] * len(outs),
        scratch_shapes=[s if not isinstance(s, tuple) else pltpu.VMEM(s, F32) for s in scratch],
        cost_estimate=pl.CostEstimate(flops=work, transcendentals=0, bytes_accessed=0),
        compiler_params=pltpu.CompilerParams(vmem_limit_bytes=48 * 1024 * 1024),
    )(*inputs, *[pltpu.with_memory_space_constraint(x, pltpu.HBM) for x in remote])


def per_device(
    electric,
    magnetic,
    polar,
    adj_electric,
    adj_magnetic,
    adj_polar,
    permittivity,
    conductivity,
    debye_class,
    debye_rate,
    debye_strength,
    wavelet,
    src_cell,
    src_sign,
    rec_owner,
    rec_pos,
    observed,
):
    width, depth, span = permittivity.shape
    steps = wavelet.shape[0]
    nsub = lax.axis_size("sub")
    nshot = lax.axis_size("shot")
    mine = lax.axis_index("sub")
    facts = jnp.stack([mine, 1 - mine % 2, jnp.minimum(mine, 1)]).astype(F32)
    meta = jnp.broadcast_to(jnp.pad(facts, (0, 5))[:, None], (8, 128))
    plane = (depth, span)

    in_x, rest = split_index(rec_pos[0], width)
    rec_y, rec_z = split_index(rest, span)
    rec_row = (rec_owner[0, :, 0] * width + in_x) * depth + rec_z
    listed = jnp.concatenate([rec_row[None].astype(F32), rec_y[None].astype(F32), observed[0]], axis=0)
    def receivers(name, which):
        (maps,) = call(
            lambda *refs: receiver_kernel(width, depth, which, *refs),
            name,
            [meta, got],
            [(len(which), width, *plane)],
            [(len(which) * width * depth, span)],
            work=10**9,
        )
        return maps

    fields = (electric[0], magnetic[0], polar[0])
    adjoint = (adj_electric[0], adj_magnetic[0], adj_polar[0])

    own = (3, width, *plane)
    *fields, coef, src, tab, a1, b1 = call(
        lambda *refs: first_kernel(width * nsub, *refs),
        "first",
        [meta],
        [own, own, own, (4, width, *plane), (width, *plane), (steps, span), *[(2 * ROUND + 3, *plane)] * 2],
        [
            (width, *plane),
            (width, *plane),
            pltpu.VMEM((width, *plane), jnp.int32),
            pltpu.VMEM(src_cell.shape, jnp.int32),
            pltpu.VMEM(src_sign.shape, jnp.int32),
            pltpu.SMEM(debye_rate.shape, F32),
            pltpu.SMEM(debye_strength.shape, F32),
            pltpu.SMEM(wavelet.shape, F32),
            pltpu.SemaphoreType.DMA((11,)),
        ],
        [*fields, permittivity, conductivity, debye_class, src_cell, src_sign, debye_rate, debye_strength, wavelet],
    )
    got_a1, got_b1 = exchange(a1, b1)
    listed, b1 = lax.optimization_barrier((listed, b1))
    got = lax.all_to_all(jnp.broadcast_to(listed[None], (nsub, *listed.shape)), "sub", 0, 0)
    edges = [(2 * ROUND, *plane)] * 2
    hist1, hs, ps, coefh, a2, b2 = call(
        forward_one_kernel,
        "forward_one",
        [meta, tab, *fields, coef, src, got_b1, got_a1],
        [(ROUND, *own), own, own, (2, 3, *plane), *edges],
    )
    got, hs = lax.optimization_barrier((got, hs))
    got_a2, got_b2 = exchange(a2, b2)
    maps = receivers("receivers_late", (0, *range(steps, ROUND, -1)))
    hist2, adj_h, a3, b3 = call(
        forward_two_kernel,
        "forward_two",
        [meta, tab, hist1, hs, ps, coef, coefh, src, maps, *adjoint, got_b2, got_a2],
        [(ROUND, *own), own, *edges],
        [own, own],
    )
    got, hist2 = lax.optimization_barrier((got, hist2))
    got_a3, got_b3 = exchange(a3, b3)
    maps2 = receivers("receivers_early", tuple(range(ROUND, 0, -1)))
    adj, hs, ps, a4, b4 = call(
        adjoint_one_kernel,
        "adjoint_one",
        [meta, adjoint[0], adj_h, adjoint[2], coef, coefh, maps, maps2, hist1, hist2, got_b3, got_a3],
        [(ROUND, *own), own, own, *edges],
    )
    got_a4, got_b4 = exchange(a4, b4)
    (corr,) = call(correlation_kernel, "correlation", [adj, hist1, hist2], [(2, width, *plane)], work=10**9)
    (corr,) = call(
        adjoint_two_kernel,
        "adjoint_two",
        [meta, adj, hs, ps, coef, coefh, maps, maps2, fields[0], hist1, corr, got_b4, got_a4],
        [(2, width, *plane)],
        [own, own, own],
    )
    total = shot_sum(corr)
    return (-(total[0] / (steps * nshot)), -(total[1] / (steps * nshot)))


def solution(mesh):
    in_specs = (
        P("shot", None, "sub", None, None),
        P("shot", None, "sub", None, None),
        P("shot", None, "sub", None, None),
        P("shot", None, "sub", None, None),
        P("shot", None, "sub", None, None),
        P("shot", None, "sub", None, None),
        P("sub", None, None),
        P("sub", None, None),
        P("sub", None, None),
        P(),
        P(),
        P(),
        P("shot", None),
        P("shot", None),
        P("shot", "sub", None),
        P("shot", "sub"),
        P("shot", None, "sub"),
    )
    out_specs = (P("sub", None, None), P("sub", None, None))
    return jax.shard_map(
        per_device, mesh=mesh, in_specs=in_specs, out_specs=out_specs, check_vma=False
    )
```

```python
import jax
import jax.numpy as jnp
from jax import lax
from jax.experimental import pallas as pl
from jax.experimental.pallas import tpu as pltpu
from jax.sharding import PartitionSpec as P

ROUND = 3
F32 = jnp.float32


def pair_swap(block, axis, first):
    route = []
    for i in range(first, lax.axis_size(axis) - 1, 2):
        route += [(i, i + 1), (i + 1, i)]
    return lax.ppermute(block, axis, route)


def exchange(inner, outer):
    got_outer = pair_swap(outer, "sub", 1)
    got_inner = pair_swap(inner, "sub", 0)
    return got_inner, got_outer


def shot_sum(x):
    n = lax.axis_size("shot")
    if n & (n - 1):
        return lax.psum(x, "shot")
    flip = 1
    while flip < n:
        x = x + lax.ppermute(x, "shot", [(i, i ^ flip) for i in range(n)])
        flip = 2 * flip + 1
    return x


def split_index(v, n):
    if n & (n - 1) == 0:
        return v & (n - 1), v >> (n.bit_length() - 1)
    return v % n, v // n


def ahead(u, axis):
    n = u.shape[axis]
    edge = lax.broadcasted_iota(jnp.int32, u.shape, axis) == n - 1
    return jnp.where(edge, 0.0, pltpu.roll(u, n - 1, axis))


def behind(u, axis):
    edge = lax.broadcasted_iota(jnp.int32, u.shape, axis) == 0
    return jnp.where(edge, 0.0, pltpu.roll(u, 1, axis))


def dfy(u):
    return ahead(u, 1) - u


def dfz(u):
    return ahead(u, 0) - u


def dby(u):
    return u - behind(u, 1)


def dbz(u):
    return u - behind(u, 0)


def h_step(h, e, e_next, keep=None, parts=(0, 1, 2)):
    ex, ey, ez = e[0], e[1], e[2]
    new = {}
    if 0 in parts:
        new[0] = h[0] - 0.5 * (dfy(ez) - dfz(ey))
    if 1 in parts:
        ahead_z = -ez if e_next is None else (e_next[2] if keep is None else e_next[2] * keep) - ez
        new[1] = h[1] - 0.5 * (dfz(ex) - ahead_z)
    if 2 in parts:
        ahead_y = -ey if e_next is None else (e_next[1] if keep is None else e_next[1] * keep) - ey
        new[2] = h[2] - 0.5 * (ahead_y - dfy(ex))
    return new


def e_step(e, h, h_prev, p, coef, inject, parts=(0, 1, 2)):
    ca, cb = coef[0], coef[1]
    new = {}
    for c in parts:
        if c == 0:
            curl = dby(h[2]) - dbz(h[1])
        elif c == 1:
            curl = dbz(h[0]) - (h[2] if h_prev is None else h[2] - h_prev[2])
        else:
            curl = (h[1] if h_prev is None else h[1] - h_prev[1]) - dby(h[0])
        new[c] = ca * e[c] + cb * (curl - p[c])
        if c == 1:
            new[c] = new[c] + inject
    return new


def p_step(p, e_new, coef):
    return {c: coef[2] * p[c] + coef[3] * e_new[c] for c in e_new}


class Planes:
    def __init__(self):
        self.at = {}

    def put(self, key, ref, *idx):
        self.at[key] = (ref, idx)

    def get(self, kind, c, i):
        ref, idx = self.at[kind, c, i]
        return ref[idx]

    def triple(self, kind, i, parts=(0, 1, 2)):
        return {c: self.get(kind, c, i) for c in parts}


def is_even(meta, shape):
    return jnp.broadcast_to(meta[1:2, :], shape) > 0.5


def pick(even, a_ref, b_ref, k, low):
    a, b = a_ref[k], b_ref[k]
    return jnp.where(even, b, a) if low else jnp.where(even, a, b)


def emit(even, a_ref, b_ref, k, right, left):
    a_ref[k] = jnp.where(even, right, left)
    b_ref[k] = jnp.where(even, left, right)


def edge_values(planes, coef_of, inject, h_out):
    last = planes.last
    lo = last - ROUND + 1
    e0 = {i: planes.triple("E", i) for i in range(last + 1)}
    h1 = {i: h_step(planes.triple("H", i), e0[i], e0[i + 1] if i < last else None) for i in range(last + 1)}
    p0 = {i: planes.triple("P", i) for i in range(last + 1)}
    raw = planes.triple("H", last)
    for c in range(3):
        for i in range(last):
            h_out[c, i] = h1[i][c]
        h_out[c, last] = raw[c]
    e, h, p = dict(e0), dict(h1), dict(p0)
    right = []
    for step in range(1, ROUND + 1):
        if step > 1:
            parts = (1, 2) if step == ROUND else (0, 1, 2)
            for i in range(lo + step - 1, last + 1):
                h[i] = {**h[i], **h_step(h[i], e[i], e[i + 1] if i < last else None, parts=parts)}
        right += [h[last][1], h[last][2]]
        if step < ROUND:
            for i in range(lo + step, last + 1):
                e[i] = e_step(e[i], h[i], h[i - 1], p[i], coef_of(i), inject(step, i))
                p[i] = p_step(p[i], e[i], coef_of(i))
    e, h, p = dict(e0), dict(h1), dict(p0)
    left = [e[0][1], e[0][2]]
    for step in range(1, ROUND):
        if step > 1:
            for i in range(ROUND - step):
                h[i] = h_step(h[i], e[i], e[i + 1])
        for i in range(ROUND - step):
            parts = (0, 1, 2) if i < ROUND - step - 1 else (1, 2)
            e[i] = e_step(e[i], h[i], h[i - 1] if i > 0 else None, p[i], coef_of(i), inject(step, i), parts)
            p[i] = p_step(p[i], e[i], coef_of(i))
        left += [e[0][1], e[0][2]]
    return right, left


def emit_all(even, a_ref, b_ref, right, left, first=0):
    for k, (r, l) in enumerate(zip(right, left)):
        emit(even, a_ref, b_ref, first + k, r, l)


def own_planes(e_ref, h_ref, p_ref, level=None):
    planes = Planes()
    width = h_ref.shape[1]
    planes.last = width - 1
    for i in range(width):
        for c in range(3):
            planes.put(("E", c, i), e_ref, *((c, i) if level is None else (level, c, i)))
            planes.put(("H", c, i), h_ref, c, i)
            planes.put(("P", c, i), p_ref, c, i)
    return planes


def source_map(cell_ref, sign_ref, mine, width, depth, span, full_x):
    flat = cell_ref[...]
    x, rest = split_index(flat, full_x)
    y, z = split_index(rest, span)
    n = flat.shape[1]
    row = (x - jnp.broadcast_to(mine, (1, n)) * width) * depth + z
    rows = width * depth
    hot = lax.broadcasted_iota(jnp.int32, (rows, n), 0) == row
    amp = (2 * sign_ref[...] - 1).astype(F32)
    where_y = lax.broadcasted_iota(jnp.int32, (span, n), 0) == y
    left = jnp.where(hot, 1.0, 0.0).astype(jnp.bfloat16)
    right = jnp.where(where_y, amp, 0.0).astype(jnp.bfloat16)
    return lax.dot_general(left, right, (((1,), (1,)), ((), ())), preferred_element_type=F32)


def first_kernel(full_x, meta, e_in, h_in, p_in, perm_in, cond_in, cls_in, cells_in, signs_in, rate_in, strength_in,
                 wavelet_in, e_ref, h_ref, p_ref, coef_ref, src_ref, tab_ref, a_ref, b_ref, perm, cond, cls, cells, signs,
                 rate_t, strength_t, wavelet, sems):
    width, depth, span = perm.shape
    even = is_even(meta, (depth, span))
    moves = [(cells_in, cells), (signs_in, signs), (wavelet_in, wavelet), (rate_in, rate_t), (strength_in, strength_t)]
    moves += [(perm_in, perm), (cond_in, cond), (cls_in, cls), (e_in, e_ref), (h_in, h_ref), (p_in, p_ref)]
    copies = [pltpu.make_async_copy(a, b, sems.at[k]) for k, (a, b) in enumerate(moves)]
    for copy in copies:
        copy.start()
    for copy in copies[:5]:
        copy.wait()
    for k in range(wavelet.shape[0]):
        tab_ref[k:k + 1, :] = jnp.full((1, span), wavelet[k], F32)
    src = source_map(cells, signs, meta[0:1, 0:1].astype(jnp.int32), width, depth, span, full_x)
    src_ref[...] = src.reshape(width, depth, span)
    for copy in copies[5:8]:
        copy.wait()
    for i in range(width):
        ratio = cond[i] / (2.0 * perm[i])
        coef_ref[0, i] = (1.0 - ratio) / (1.0 + ratio)
        coef_ref[1, i] = 0.5 / (perm[i] * (1.0 + ratio))
        kind = cls[i]
        rate = jnp.zeros((depth, span), F32)
        gain = jnp.zeros((depth, span), F32)
        for k in range(rate_t.shape[0]):
            rate = jnp.where(kind == k, rate_t[k], rate)
            gain = jnp.where(kind == k, (1.0 - rate_t[k]) * strength_t[k], gain)
        coef_ref[2, i] = rate
        coef_ref[3, i] = gain
    for copy in copies[8:]:
        copy.wait()
    planes = own_planes(e_ref, h_ref, p_ref)
    right, left = edge_values(planes, lambda i: [coef_ref[k, i] for k in range(4)],
                              lambda step, i: src_ref[i] * wavelet[step - 1], h_ref)
    last = width - 1
    right += [coef_ref[k, last] for k in (0, 1, 3)]
    left += [coef_ref[k, 0] for k in (0, 1, 3)]
    emit_all(even, a_ref, b_ref, right, left)


def receiver_kernel(width, depth, which, meta, got, maps_ref, acc):
    rows = width * depth
    span = acc.shape[1]
    blocks, _, n = got.shape
    acc[...] = jnp.zeros(acc.shape, F32)
    first_row = meta[0:1, :] * (width * depth)
    row_at = lax.broadcasted_iota(jnp.int32, (rows, n), 0).astype(F32)
    y_at = lax.broadcasted_iota(jnp.int32, (span, n), 0).astype(F32)
    group = max(g for g in (1, 2, 4, 8) if blocks % g == 0)
    zero = jnp.zeros((rows, n), jnp.bfloat16)

    def block(k, carry):
        left = [[] for _ in which]
        right = []
        for b in range(group):
            at = k * group + b
            hot = row_at == got[at, 0:1, :] - first_row[:, :n]
            at_y = jnp.where(y_at == got[at, 1:2, :], 1.0, 0.0).astype(jnp.bfloat16)
            right += [at_y] * 3
            for part, s in zip(left, which):
                if s == 0:
                    part += [jnp.where(hot, 1.0, 0.0).astype(jnp.bfloat16), zero, zero]
                    continue
                v = got[at, 1 + s:2 + s, :]
                high = v.astype(jnp.bfloat16).astype(F32)
                mid = (v - high).astype(jnp.bfloat16).astype(F32)
                low = (v - high) - mid
                part += [jnp.where(hot, u, 0.0).astype(jnp.bfloat16) for u in (high, mid, low)]
        acc[...] += lax.dot_general(
            jnp.concatenate([jnp.concatenate(part, axis=1) for part in left], axis=0) if len(left) > 1 else jnp.concatenate(left[0], axis=1),
            jnp.concatenate(right, axis=1),
            (((1,), (1,)), ((), ())),
            preferred_element_type=F32,
        )
        return carry

    lax.fori_loop(0, blocks // group, block, 0)
    maps_ref[...] = acc[...].reshape(maps_ref.shape)


def round_body(planes, meta, coef_ref, coefh_ref, a_ref, b_ref, inject, dest, seen=None):
    even = is_even(meta, coef_ref.shape[2:])
    keep = meta[2:3, :]
    last = planes.last

    def coef_of(i):
        return [coef_ref[k, i] for k in range(4)]

    before, after = ([coefh_ref[side, k] for k in range(3)] for side in (0, 1))
    zero = jnp.zeros(coef_ref.shape[2:], F32)
    none = {c: zero for c in range(3)}

    def store(kind, c, i, level, value):
        ref, idx = dest(kind, c, i, level)
        ref[idx] = value
        planes.put((kind, c, i), ref, *idx)

    low_e = low_h = low_p = high_e = high_p = None
    for level in range(1, ROUND + 1):
        sent = 2 * (level - 1)
        edge = {c: planes.get("E", c, 0) * keep for c in (1, 2)}
        if level == 1:
            low_h = {0: zero, 1: 0.5 * edge[2], 2: -0.5 * edge[1]}
            far = None
        else:
            far = {1: 0.5 * low_e[2], 2: -0.5 * low_e[1]}
            low_h.update(h_step(low_h, low_e, edge, parts=(0, 1, 2) if level < ROUND else (1, 2)))
        if level == 1:
            low_e = {0: before[1] * (dby(low_h[2]) - dbz(low_h[1])), 1: -(before[1] * low_h[2]), 2: before[1] * low_h[1]}
            low_p = {c: before[2] * low_e[c] for c in range(3)}
        elif level < ROUND:
            low_e = e_step(low_e, low_h, far, low_p, before, 0.0)
        h_prev = {c: low_h[c] + pick(even, a_ref, b_ref, sent + c - 1, True) for c in (1, 2)}
        now_h = {}
        for i in range(last + 1):
            h = planes.triple("H", i)
            if level > 1 or i == last:
                if i < last:
                    e_next = planes.triple("E", i + 1, (1, 2))
                else:
                    e_next = {c: pick(even, a_ref, b_ref, sent + c - 1, False) for c in (1, 2)}
                    if level > 1:
                        e_next = {c: e_next[c] + high_e[c] for c in (1, 2)}
                h = h_step(h, planes.triple("E", i), e_next)
                for c in range(3):
                    store("H", c, i, level, h[c])
            now_h[i] = h
        for i in range(last + 1):
            h = now_h[i]
            cf = coef_of(i)
            new = e_step(planes.triple("E", i), h, h_prev, planes.triple("P", i), cf, inject(level, i))
            pn = p_step(planes.triple("P", i), new, cf)
            for c in range(3):
                store("E", c, i, level, new[c])
                store("P", c, i, level, pn[c])
            if seen is not None:
                seen(level, i, new)
            h_prev = h
        if level == 1:
            high_e = {0: zero, 1: after[1] * h_prev[2], 2: -(after[1] * h_prev[1])}
            high_p = {c: after[2] * high_e[c] for c in range(3)}
            high_h = none
        elif level < ROUND:
            high_h = h_step(high_h, high_e, None)
            high_e = e_step(high_e, high_h, h_prev, high_p, after, 0.0)


def store_in(e_ref, h_ref, p_ref, by_level=False):
    refs = {"E": e_ref, "H": h_ref, "P": p_ref}

    def dest(kind, c, i, level):
        return refs[kind], ((level - 1, c, i) if kind == "E" and by_level else (c, i))

    return dest


def forward_one_kernel(meta, tab_ref, e_ref, h_ref, p_ref, coef_ref, src_ref, b_ref, a_ref,
                       hist_ref, hs_ref, ps_ref, coefh_ref, oa_ref, ob_ref):
    even = is_even(meta, e_ref.shape[2:])
    wavelet = 0
    for side in (0, 1):
        for k in range(3):
            coefh_ref[side, k] = pick(even, a_ref, b_ref, 2 * ROUND + k, side == 0)
    planes = own_planes(e_ref, h_ref, p_ref)

    def inject(level, i):
        return src_ref[i] * tab_ref[wavelet + level - 1:wavelet + level, :]

    round_body(planes, meta, coef_ref, coefh_ref, a_ref, b_ref, inject, store_in(hist_ref, hs_ref, ps_ref, True))
    right, left = edge_values(planes, lambda i: [coef_ref[k, i] for k in range(4)], lambda step, i: inject(ROUND + step, i), hs_ref)
    emit_all(even, oa_ref, ob_ref, right, left)


def forward_two_kernel(meta, tab_ref, hist_in, hs_in, ps_in, coef_ref, coefh_ref, src_ref, maps_ref, e_ref, h_ref, p_ref,
                       b_ref, a_ref, hist_ref, h_out, oa_ref, ob_ref, hs_ref, ps_ref):
    wavelet = ROUND
    round_body(own_planes(hist_in, hs_in, ps_in, ROUND - 1), meta, coef_ref, coefh_ref, a_ref, b_ref,
               lambda level, i: src_ref[i] * tab_ref[wavelet + level - 1:wavelet + level, :],
               store_in(hist_ref, hs_ref, ps_ref, True))

    def inject(step, i):
        return maps_ref[0, i] * hist_ref[ROUND - step, 1, i] - maps_ref[step, i]

    right, left = edge_values(own_planes(e_ref, h_ref, p_ref), lambda i: [coef_ref[k, i] for k in range(4)], inject, h_out)
    emit_all(is_even(meta, e_ref.shape[2:]), oa_ref, ob_ref, right, left)


def correlate(corr_ref, i, b, now, prev, add):
    eps = b[0] * (now[0] - prev[0]) + b[1] * (now[1] - prev[1]) + b[2] * (now[2] - prev[2])
    sig = b[0] * now[0] + b[1] * now[1] + b[2] * now[2]
    if add is not None:
        eps, sig = eps + add[0, i], sig + add[1, i]
    corr_ref[0, i] = eps
    corr_ref[1, i] = sig


def adjoint_one_kernel(meta, e_ref, h_ref, p_ref, coef_ref, coefh_ref, maps_ref, maps2_ref, hist1_ref, hist2_ref,
                       b_ref, a_ref, e_out, hs_ref, ps_ref, oa_ref, ob_ref):
    planes = own_planes(e_ref, h_ref, p_ref)

    def inject(level, i):
        return maps_ref[0, i] * hist2_ref[ROUND - level, 1, i] - maps_ref[level, i]

    def inject_next(step, i):
        return maps_ref[0, i] * hist1_ref[ROUND - step, 1, i] - maps2_ref[step - 1, i]

    round_body(planes, meta, coef_ref, coefh_ref, a_ref, b_ref, inject, store_in(e_out, hs_ref, ps_ref, True))
    right, left = edge_values(planes, lambda i: [coef_ref[k, i] for k in range(4)], inject_next, hs_ref)
    emit_all(is_even(meta, e_ref.shape[2:]), oa_ref, ob_ref, right, left)


def correlation_kernel(adj_ref, hist1_ref, hist2_ref, corr_ref):
    for i in range(corr_ref.shape[1]):
        for level in range(1, ROUND + 1):
            n = ROUND - level
            e = [adj_ref[level - 1, c, i] for c in range(3)]
            now = [hist2_ref[n, c, i] for c in range(3)]
            prev = [hist2_ref[n - 1, c, i] if n > 0 else hist1_ref[ROUND - 1, c, i] for c in range(3)]
            correlate(corr_ref, i, e, now, prev, corr_ref if level > 1 else None)


def adjoint_two_kernel(meta, e_ref, hs_in, ps_in, coef_ref, coefh_ref, maps_ref, maps2_ref, e0_ref, hist1_ref,
                       corr_in, b_ref, a_ref, corr_ref, es_ref, hs_ref, ps_ref):
    def seen(level, i, e):
        n = ROUND - level
        now = [hist1_ref[n, c, i] for c in range(3)]
        prev = [hist1_ref[n - 1, c, i] if n > 0 else e0_ref[c, i] for c in range(3)]
        correlate(corr_ref, i, e, now, prev, corr_ref if level > 1 else corr_in)

    def inject(level, i):
        return maps_ref[0, i] * hist1_ref[ROUND - level, 1, i] - maps2_ref[level - 1, i]

    round_body(own_planes(e_ref, hs_in, ps_in, ROUND - 1), meta, coef_ref, coefh_ref, a_ref, b_ref, inject,
               store_in(es_ref, hs_ref, ps_ref), seen)


def call(body, name, inputs, outs, scratch=(), remote=(), work=10**10):
    vmem = pl.BlockSpec(memory_space=pltpu.VMEM)
    stay = pl.BlockSpec(memory_space=pltpu.HBM)
    return pl.pallas_call(
        body,
        name=name,
        out_shape=[jax.ShapeDtypeStruct(s, F32) for s in outs],
        in_specs=[vmem] * len(inputs) + [stay] * len(remote),
        out_specs=[vmem] * len(outs),
        scratch_shapes=[s if not isinstance(s, tuple) else pltpu.VMEM(s, F32) for s in scratch],
        cost_estimate=pl.CostEstimate(flops=work, transcendentals=0, bytes_accessed=0),
        compiler_params=pltpu.CompilerParams(vmem_limit_bytes=48 * 1024 * 1024),
    )(*inputs, *[pltpu.with_memory_space_constraint(x, pltpu.HBM) for x in remote])


def per_device(
    electric,
    magnetic,
    polar,
    adj_electric,
    adj_magnetic,
    adj_polar,
    permittivity,
    conductivity,
    debye_class,
    debye_rate,
    debye_strength,
    wavelet,
    src_cell,
    src_sign,
    rec_owner,
    rec_pos,
    observed,
):
    width, depth, span = permittivity.shape
    steps = wavelet.shape[0]
    nsub = lax.axis_size("sub")
    nshot = lax.axis_size("shot")
    mine = lax.axis_index("sub")
    facts = jnp.stack([mine, 1 - mine % 2, jnp.minimum(mine, 1)]).astype(F32)
    meta = jnp.broadcast_to(jnp.pad(facts, (0, 5))[:, None], (8, 128))
    plane = (depth, span)

    in_x, rest = split_index(rec_pos[0], width)
    rec_y, rec_z = split_index(rest, span)
    rec_row = (rec_owner[0, :, 0] * width + in_x) * depth + rec_z
    listed = jnp.concatenate([rec_row[None].astype(F32), rec_y[None].astype(F32), observed[0]], axis=0)
    def receivers(name, which):
        (maps,) = call(
            lambda *refs: receiver_kernel(width, depth, which, *refs),
            name,
            [meta, got],
            [(len(which), width, *plane)],
            [(len(which) * width * depth, span)],
            work=10**9,
        )
        return maps

    fields = (electric[0], magnetic[0], polar[0])
    adjoint = (adj_electric[0], adj_magnetic[0], adj_polar[0])

    own = (3, width, *plane)
    *fields, coef, src, tab, a1, b1 = call(
        lambda *refs: first_kernel(width * nsub, *refs),
        "first",
        [meta],
        [own, own, own, (4, width, *plane), (width, *plane), (steps, span), *[(2 * ROUND + 3, *plane)] * 2],
        [
            (width, *plane),
            (width, *plane),
            pltpu.VMEM((width, *plane), jnp.int32),
            pltpu.VMEM(src_cell.shape, jnp.int32),
            pltpu.VMEM(src_sign.shape, jnp.int32),
            pltpu.SMEM(debye_rate.shape, F32),
            pltpu.SMEM(debye_strength.shape, F32),
            pltpu.SMEM(wavelet.shape, F32),
            pltpu.SemaphoreType.DMA((11,)),
        ],
        [*fields, permittivity, conductivity, debye_class, src_cell, src_sign, debye_rate, debye_strength, wavelet],
    )
    got_a1, got_b1 = exchange(a1, b1)
    listed, a1 = lax.optimization_barrier((listed, a1))
    got = lax.all_to_all(jnp.broadcast_to(listed[None], (nsub, *listed.shape)), "sub", 0, 0)
    edges = [(2 * ROUND, *plane)] * 2
    hist1, hs, ps, coefh, a2, b2 = call(
        forward_one_kernel,
        "forward_one",
        [meta, tab, *fields, coef, src, got_b1, got_a1],
        [(ROUND, *own), own, own, (2, 3, *plane), *edges],
    )
    got, hs = lax.optimization_barrier((got, hs))
    got_a2, got_b2 = exchange(a2, b2)
    maps = receivers("receivers_late", (0, *range(steps, ROUND, -1)))
    hist2, adj_h, a3, b3 = call(
        forward_two_kernel,
        "forward_two",
        [meta, tab, hist1, hs, ps, coef, coefh, src, maps, *adjoint, got_b2, got_a2],
        [(ROUND, *own), own, *edges],
        [own, own],
    )
    got, hist2 = lax.optimization_barrier((got, hist2))
    got_a3, got_b3 = exchange(a3, b3)
    maps2 = receivers("receivers_early", tuple(range(ROUND, 0, -1)))
    adj, hs, ps, a4, b4 = call(
        adjoint_one_kernel,
        "adjoint_one",
        [meta, adjoint[0], adj_h, adjoint[2], coef, coefh, maps, maps2, hist1, hist2, got_b3, got_a3],
        [(ROUND, *own), own, own, *edges],
    )
    got_a4, got_b4 = exchange(a4, b4)
    (corr,) = call(correlation_kernel, "correlation", [adj, hist1, hist2], [(2, width, *plane)], work=10**9)
    (corr,) = call(
        adjoint_two_kernel,
        "adjoint_two",
        [meta, adj, hs, ps, coef, coefh, maps, maps2, fields[0], hist1, corr, got_b4, got_a4],
        [(2, width, *plane)],
        [own, own, own],
    )
    total = shot_sum(corr)
    return (-(total[0] / (steps * nshot)), -(total[1] / (steps * nshot)))


def solution(mesh):
    in_specs = (
        P("shot", None, "sub", None, None),
        P("shot", None, "sub", None, None),
        P("shot", None, "sub", None, None),
        P("shot", None, "sub", None, None),
        P("shot", None, "sub", None, None),
        P("shot", None, "sub", None, None),
        P("sub", None, None),
        P("sub", None, None),
        P("sub", None, None),
        P(),
        P(),
        P(),
        P("shot", None),
        P("shot", None),
        P("shot", "sub", None),
        P("shot", "sub"),
        P("shot", None, "sub"),
    )
    out_specs = (P("sub", None, None), P("sub", None, None))
    return jax.shard_map(
        per_device, mesh=mesh, in_specs=in_specs, out_specs=out_specs, check_vma=False
    )
```

```python
import jax
import jax.numpy as jnp
from jax import lax
from jax.experimental import pallas as pl
from jax.experimental.pallas import tpu as pltpu
from jax.sharding import PartitionSpec as P

ROUND = 3
F32 = jnp.float32


def pair_swap(block, axis, first):
    route = []
    for i in range(first, lax.axis_size(axis) - 1, 2):
        route += [(i, i + 1), (i + 1, i)]
    return lax.ppermute(block, axis, route)


def exchange(inner, outer):
    got_outer = pair_swap(outer, "sub", 1)
    got_inner = pair_swap(inner, "sub", 0)
    return got_inner, got_outer


def shot_sum(x):
    n = lax.axis_size("shot")
    if n & (n - 1):
        return lax.psum(x, "shot")
    flip = 1
    while flip < n:
        x = x + lax.ppermute(x, "shot", [(i, i ^ flip) for i in range(n)])
        flip = 2 * flip + 1
    return x


def split_index(v, n):
    if n & (n - 1) == 0:
        return v & (n - 1), v >> (n.bit_length() - 1)
    return v % n, v // n


def ahead(u, axis):
    n = u.shape[axis]
    edge = lax.broadcasted_iota(jnp.int32, u.shape, axis) == n - 1
    return jnp.where(edge, 0.0, pltpu.roll(u, n - 1, axis))


def behind(u, axis):
    edge = lax.broadcasted_iota(jnp.int32, u.shape, axis) == 0
    return jnp.where(edge, 0.0, pltpu.roll(u, 1, axis))


def dfy(u):
    return ahead(u, 1) - u


def dfz(u):
    return ahead(u, 0) - u


def dby(u):
    return u - behind(u, 1)


def dbz(u):
    return u - behind(u, 0)


def h_step(h, e, e_next, keep=None, parts=(0, 1, 2)):
    ex, ey, ez = e[0], e[1], e[2]
    new = {}
    if 0 in parts:
        new[0] = h[0] - 0.5 * (dfy(ez) - dfz(ey))
    if 1 in parts:
        ahead_z = -ez if e_next is None else (e_next[2] if keep is None else e_next[2] * keep) - ez
        new[1] = h[1] - 0.5 * (dfz(ex) - ahead_z)
    if 2 in parts:
        ahead_y = -ey if e_next is None else (e_next[1] if keep is None else e_next[1] * keep) - ey
        new[2] = h[2] - 0.5 * (ahead_y - dfy(ex))
    return new


def e_step(e, h, h_prev, p, coef, inject, parts=(0, 1, 2)):
    ca, cb = coef[0], coef[1]
    new = {}
    for c in parts:
        if c == 0:
            curl = dby(h[2]) - dbz(h[1])
        elif c == 1:
            curl = dbz(h[0]) - (h[2] if h_prev is None else h[2] - h_prev[2])
        else:
            curl = (h[1] if h_prev is None else h[1] - h_prev[1]) - dby(h[0])
        new[c] = ca * e[c] + cb * (curl - p[c])
        if c == 1:
            new[c] = new[c] + inject
    return new


def p_step(p, e_new, coef):
    return {c: coef[2] * p[c] + coef[3] * e_new[c] for c in e_new}


class Planes:
    def __init__(self):
        self.at = {}

    def put(self, key, ref, *idx):
        self.at[key] = (ref, idx)

    def get(self, kind, c, i):
        ref, idx = self.at[kind, c, i]
        return ref[idx]

    def triple(self, kind, i, parts=(0, 1, 2)):
        return {c: self.get(kind, c, i) for c in parts}


def is_even(meta, shape):
    return jnp.broadcast_to(meta[1:2, :], shape) > 0.5


def pick(even, a_ref, b_ref, k, low):
    a, b = a_ref[k], b_ref[k]
    return jnp.where(even, b, a) if low else jnp.where(even, a, b)


def emit(even, a_ref, b_ref, k, right, left):
    a_ref[k] = jnp.where(even, right, left)
    b_ref[k] = jnp.where(even, left, right)


def edge_values(planes, coef_of, inject, h_out):
    last = planes.last
    lo = last - ROUND + 1
    e0 = {i: planes.triple("E", i) for i in range(last + 1)}
    h1 = {i: h_step(planes.triple("H", i), e0[i], e0[i + 1] if i < last else None) for i in range(last + 1)}
    p0 = {i: planes.triple("P", i) for i in range(last + 1)}
    raw = planes.triple("H", last)
    for c in range(3):
        for i in range(last):
            h_out[c, i] = h1[i][c]
        h_out[c, last] = raw[c]
    e, h, p = dict(e0), dict(h1), dict(p0)
    right = []
    for step in range(1, ROUND + 1):
        if step > 1:
            parts = (1, 2) if step == ROUND else (0, 1, 2)
            for i in range(lo + step - 1, last + 1):
                h[i] = {**h[i], **h_step(h[i], e[i], e[i + 1] if i < last else None, parts=parts)}
        right += [h[last][1], h[last][2]]
        if step < ROUND:
            for i in range(lo + step, last + 1):
                e[i] = e_step(e[i], h[i], h[i - 1], p[i], coef_of(i), inject(step, i))
                p[i] = p_step(p[i], e[i], coef_of(i))
    e, h, p = dict(e0), dict(h1), dict(p0)
    left = [e[0][1], e[0][2]]
    for step in range(1, ROUND):
        if step > 1:
            for i in range(ROUND - step):
                h[i] = h_step(h[i], e[i], e[i + 1])
        for i in range(ROUND - step):
            parts = (0, 1, 2) if i < ROUND - step - 1 else (1, 2)
            e[i] = e_step(e[i], h[i], h[i - 1] if i > 0 else None, p[i], coef_of(i), inject(step, i), parts)
            p[i] = p_step(p[i], e[i], coef_of(i))
        left += [e[0][1], e[0][2]]
    return right, left


def emit_all(even, a_ref, b_ref, right, left, first=0):
    for k, (r, l) in enumerate(zip(right, left)):
        emit(even, a_ref, b_ref, first + k, r, l)


def own_planes(e_ref, h_ref, p_ref, level=None):
    planes = Planes()
    width = h_ref.shape[1]
    planes.last = width - 1
    for i in range(width):
        for c in range(3):
            planes.put(("E", c, i), e_ref, *((c, i) if level is None else (level, c, i)))
            planes.put(("H", c, i), h_ref, c, i)
            planes.put(("P", c, i), p_ref, c, i)
    return planes


def source_map(cell_ref, sign_ref, mine, width, depth, span, full_x):
    flat = cell_ref[...]
    x, rest = split_index(flat, full_x)
    y, z = split_index(rest, span)
    n = flat.shape[1]
    row = (x - jnp.broadcast_to(mine, (1, n)) * width) * depth + z
    rows = width * depth
    hot = lax.broadcasted_iota(jnp.int32, (rows, n), 0) == row
    amp = (2 * sign_ref[...] - 1).astype(F32)
    where_y = lax.broadcasted_iota(jnp.int32, (span, n), 0) == y
    left = jnp.where(hot, 1.0, 0.0).astype(jnp.bfloat16)
    right = jnp.where(where_y, amp, 0.0).astype(jnp.bfloat16)
    return lax.dot_general(left, right, (((1,), (1,)), ((), ())), preferred_element_type=F32)


def first_kernel(full_x, meta, e_in, h_in, p_in, perm_in, cond_in, cls_in, cells_in, signs_in, rate_in, strength_in,
                 wavelet_in, e_ref, h_ref, p_ref, coef_ref, src_ref, tab_ref, a_ref, b_ref, perm, cond, cls, cells, signs,
                 rate_t, strength_t, wavelet, sems):
    width, depth, span = perm.shape
    even = is_even(meta, (depth, span))
    moves = [(cells_in, cells), (signs_in, signs), (wavelet_in, wavelet), (rate_in, rate_t), (strength_in, strength_t)]
    moves += [(perm_in, perm), (cond_in, cond), (cls_in, cls), (e_in, e_ref), (h_in, h_ref), (p_in, p_ref)]
    copies = [pltpu.make_async_copy(a, b, sems.at[k]) for k, (a, b) in enumerate(moves)]
    for copy in copies:
        copy.start()
    for copy in copies[:5]:
        copy.wait()
    for k in range(wavelet.shape[0]):
        tab_ref[k:k + 1, :] = jnp.full((1, span), wavelet[k], F32)
    src = source_map(cells, signs, meta[0:1, 0:1].astype(jnp.int32), width, depth, span, full_x)
    src_ref[...] = src.reshape(width, depth, span)
    for copy in copies[5:8]:
        copy.wait()
    for i in range(width):
        double = 2.0 * perm[i]
        share = 1.0 / (double + cond[i])
        coef_ref[0, i] = (double - cond[i]) * share
        coef_ref[1, i] = share
        kind = cls[i]
        rate = jnp.zeros((depth, span), F32)
        gain = jnp.zeros((depth, span), F32)
        for k in range(rate_t.shape[0]):
            rate = jnp.where(kind == k, rate_t[k], rate)
            gain = jnp.where(kind == k, (1.0 - rate_t[k]) * strength_t[k], gain)
        coef_ref[2, i] = rate
        coef_ref[3, i] = gain
    for copy in copies[8:]:
        copy.wait()
    planes = own_planes(e_ref, h_ref, p_ref)
    right, left = edge_values(planes, lambda i: [coef_ref[k, i] for k in range(4)],
                              lambda step, i: src_ref[i] * wavelet[step - 1], h_ref)
    last = width - 1
    right += [coef_ref[0, last] - coef_ref[1, last] * coef_ref[3, last], coef_ref[1, last]]
    left += [coef_ref[0, 0] - coef_ref[1, 0] * coef_ref[3, 0], coef_ref[1, 0]]
    emit_all(even, a_ref, b_ref, right, left)


def receiver_kernel(width, depth, which, meta, got, maps_ref, acc):
    rows = width * depth
    span = acc.shape[1]
    blocks, _, n = got.shape
    acc[...] = jnp.zeros(acc.shape, F32)
    first_row = meta[0:1, :] * (width * depth)
    row_at = lax.broadcasted_iota(jnp.int32, (rows, n), 0).astype(F32)
    y_at = lax.broadcasted_iota(jnp.int32, (span, n), 0).astype(F32)
    group = max(g for g in (1, 2, 4, 8) if blocks % g == 0)
    zero = jnp.zeros((rows, n), jnp.bfloat16)

    def block(k, carry):
        left = [[] for _ in which]
        right = []
        for b in range(group):
            at = k * group + b
            hot = row_at == got[at, 0:1, :] - first_row[:, :n]
            at_y = jnp.where(y_at == got[at, 1:2, :], 1.0, 0.0).astype(jnp.bfloat16)
            right += [at_y] * 3
            for part, s in zip(left, which):
                if s == 0:
                    part += [jnp.where(hot, 1.0, 0.0).astype(jnp.bfloat16), zero, zero]
                    continue
                v = got[at, 1 + s:2 + s, :]
                high = v.astype(jnp.bfloat16).astype(F32)
                mid = (v - high).astype(jnp.bfloat16).astype(F32)
                low = (v - high) - mid
                part += [jnp.where(hot, u, 0.0).astype(jnp.bfloat16) for u in (high, mid, low)]
        acc[...] += lax.dot_general(
            jnp.concatenate([jnp.concatenate(part, axis=1) for part in left], axis=0) if len(left) > 1 else jnp.concatenate(left[0], axis=1),
            jnp.concatenate(right, axis=1),
            (((1,), (1,)), ((), ())),
            preferred_element_type=F32,
        )
        return carry

    lax.fori_loop(0, blocks // group, block, 0)
    maps_ref[...] = acc[...].reshape(maps_ref.shape)


def round_body(planes, meta, coef_ref, coefh_ref, a_ref, b_ref, inject, dest, seen=None):
    even = is_even(meta, coef_ref.shape[2:])
    keep = meta[2:3, :]
    last = planes.last

    def coef_of(i):
        return [coef_ref[k, i] for k in range(4)]

    before, after = ([coefh_ref[side, k] for k in range(2)] for side in (0, 1))
    rest = {c: 0.0 for c in range(3)}
    zero = jnp.zeros(coef_ref.shape[2:], F32)
    none = {c: zero for c in range(3)}

    def store(kind, c, i, level, value):
        ref, idx = dest(kind, c, i, level)
        ref[idx] = value
        planes.put((kind, c, i), ref, *idx)

    low_e = low_h = high_e = high_h = None
    for level in range(1, ROUND + 1):
        sent = 2 * (level - 1)
        edge = {c: planes.get("E", c, 0) * keep for c in (1, 2)}
        if level == 1:
            low_h = {0: zero, 1: 0.5 * edge[2], 2: -0.5 * edge[1]}
            far = None
        else:
            far = {1: 0.5 * low_e[2], 2: -0.5 * low_e[1]}
            low_h.update(h_step(low_h, low_e, edge, parts=(0, 1, 2) if level < ROUND else (1, 2)))
        if level == 1:
            low_e = {0: before[1] * (dby(low_h[2]) - dbz(low_h[1])), 1: -(before[1] * low_h[2]), 2: before[1] * low_h[1]}
        elif level < ROUND:
            low_e = e_step(low_e, low_h, far, rest, before, 0.0)
        h_prev = {c: low_h[c] + pick(even, a_ref, b_ref, sent + c - 1, True) for c in (1, 2)}
        now_h = {}
        for i in range(last + 1):
            h = planes.triple("H", i)
            if level > 1 or i == last:
                if i < last:
                    e_next = planes.triple("E", i + 1, (1, 2))
                else:
                    e_next = {c: pick(even, a_ref, b_ref, sent + c - 1, False) for c in (1, 2)}
                    if level > 1:
                        e_next = {c: e_next[c] + high_e[c] for c in (1, 2)}
                h = h_step(h, planes.triple("E", i), e_next)
                for c in range(3):
                    store("H", c, i, level, h[c])
            now_h[i] = h
        for i in range(last + 1):
            h = now_h[i]
            cf = coef_of(i)
            new = e_step(planes.triple("E", i), h, h_prev, planes.triple("P", i), cf, inject(level, i))
            pn = p_step(planes.triple("P", i), new, cf)
            for c in range(3):
                store("E", c, i, level, new[c])
                store("P", c, i, level, pn[c])
            if seen is not None:
                seen(level, i, new)
            h_prev = h
        if level == 1:
            high_e = {0: zero, 1: after[1] * h_prev[2], 2: -(after[1] * h_prev[1])}
            high_h = none
        elif level < ROUND:
            high_h = h_step(high_h, high_e, None)
            high_e = e_step(high_e, high_h, h_prev, rest, after, 0.0)


def store_in(e_ref, h_ref, p_ref, by_level=False):
    refs = {"E": e_ref, "H": h_ref, "P": p_ref}

    def dest(kind, c, i, level):
        return refs[kind], ((level - 1, c, i) if kind == "E" and by_level else (c, i))

    return dest


def forward_one_kernel(meta, tab_ref, e_ref, h_ref, p_ref, coef_ref, src_ref, b_ref, a_ref,
                       hist_ref, hs_ref, ps_ref, coefh_ref, oa_ref, ob_ref):
    even = is_even(meta, e_ref.shape[2:])
    wavelet = 0
    for side in (0, 1):
        for k in range(2):
            coefh_ref[side, k] = pick(even, a_ref, b_ref, 2 * ROUND + k, side == 0)
    planes = own_planes(e_ref, h_ref, p_ref)

    def inject(level, i):
        return src_ref[i] * tab_ref[wavelet + level - 1:wavelet + level, :]

    round_body(planes, meta, coef_ref, coefh_ref, a_ref, b_ref, inject, store_in(hist_ref, hs_ref, ps_ref, True))
    right, left = edge_values(planes, lambda i: [coef_ref[k, i] for k in range(4)], lambda step, i: inject(ROUND + step, i), hs_ref)
    emit_all(even, oa_ref, ob_ref, right, left)


def forward_two_kernel(meta, tab_ref, hist_in, hs_in, ps_in, coef_ref, coefh_ref, src_ref, maps_ref, e_ref, h_ref, p_ref,
                       b_ref, a_ref, hist_ref, h_out, oa_ref, ob_ref, hs_ref, ps_ref):
    wavelet = ROUND
    round_body(own_planes(hist_in, hs_in, ps_in, ROUND - 1), meta, coef_ref, coefh_ref, a_ref, b_ref,
               lambda level, i: src_ref[i] * tab_ref[wavelet + level - 1:wavelet + level, :],
               store_in(hist_ref, hs_ref, ps_ref, True))

    def inject(step, i):
        return maps_ref[0, i] * hist_ref[ROUND - step, 1, i] - maps_ref[step, i]

    right, left = edge_values(own_planes(e_ref, h_ref, p_ref), lambda i: [coef_ref[k, i] for k in range(4)], inject, h_out)
    emit_all(is_even(meta, e_ref.shape[2:]), oa_ref, ob_ref, right, left)


def correlate(corr_ref, i, b, now, prev, add):
    eps = b[0] * (now[0] - prev[0]) + b[1] * (now[1] - prev[1]) + b[2] * (now[2] - prev[2])
    sig = b[0] * now[0] + b[1] * now[1] + b[2] * now[2]
    if add is not None:
        eps, sig = eps + add[0, i], sig + add[1, i]
    corr_ref[0, i] = eps
    corr_ref[1, i] = sig


def adjoint_one_kernel(meta, e_ref, h_ref, p_ref, coef_ref, coefh_ref, maps_ref, maps2_ref, hist1_ref, hist2_ref,
                       b_ref, a_ref, e_out, hs_ref, ps_ref, oa_ref, ob_ref):
    planes = own_planes(e_ref, h_ref, p_ref)

    def inject(level, i):
        return maps_ref[0, i] * hist2_ref[ROUND - level, 1, i] - maps_ref[level, i]

    def inject_next(step, i):
        return maps_ref[0, i] * hist1_ref[ROUND - step, 1, i] - maps2_ref[step - 1, i]

    round_body(planes, meta, coef_ref, coefh_ref, a_ref, b_ref, inject, store_in(e_out, hs_ref, ps_ref, True))
    right, left = edge_values(planes, lambda i: [coef_ref[k, i] for k in range(4)], inject_next, hs_ref)
    emit_all(is_even(meta, e_ref.shape[2:]), oa_ref, ob_ref, right, left)


def correlation_kernel(adj_ref, hist1_ref, hist2_ref, corr_ref):
    for i in range(corr_ref.shape[1]):
        for level in range(1, ROUND + 1):
            n = ROUND - level
            e = [adj_ref[level - 1, c, i] for c in range(3)]
            now = [hist2_ref[n, c, i] for c in range(3)]
            prev = [hist2_ref[n - 1, c, i] if n > 0 else hist1_ref[ROUND - 1, c, i] for c in range(3)]
            correlate(corr_ref, i, e, now, prev, corr_ref if level > 1 else None)


def adjoint_two_kernel(meta, e_ref, hs_in, ps_in, coef_ref, coefh_ref, maps_ref, maps2_ref, e0_ref, hist1_ref,
                       corr_in, b_ref, a_ref, corr_ref, es_ref, hs_ref, ps_ref):
    def seen(level, i, e):
        n = ROUND - level
        now = [hist1_ref[n, c, i] for c in range(3)]
        prev = [hist1_ref[n - 1, c, i] if n > 0 else e0_ref[c, i] for c in range(3)]
        correlate(corr_ref, i, e, now, prev, corr_ref if level > 1 else corr_in)

    def inject(level, i):
        return maps_ref[0, i] * hist1_ref[ROUND - level, 1, i] - maps2_ref[level - 1, i]

    round_body(own_planes(e_ref, hs_in, ps_in, ROUND - 1), meta, coef_ref, coefh_ref, a_ref, b_ref, inject,
               store_in(es_ref, hs_ref, ps_ref), seen)


def call(body, name, inputs, outs, scratch=(), remote=(), work=10**10):
    vmem = pl.BlockSpec(memory_space=pltpu.VMEM)
    stay = pl.BlockSpec(memory_space=pltpu.HBM)
    return pl.pallas_call(
        body,
        name=name,
        out_shape=[jax.ShapeDtypeStruct(s, F32) for s in outs],
        in_specs=[vmem] * len(inputs) + [stay] * len(remote),
        out_specs=[vmem] * len(outs),
        scratch_shapes=[s if not isinstance(s, tuple) else pltpu.VMEM(s, F32) for s in scratch],
        cost_estimate=pl.CostEstimate(flops=work, transcendentals=0, bytes_accessed=0),
        compiler_params=pltpu.CompilerParams(vmem_limit_bytes=48 * 1024 * 1024),
    )(*inputs, *[pltpu.with_memory_space_constraint(x, pltpu.HBM) for x in remote])


def per_device(
    electric,
    magnetic,
    polar,
    adj_electric,
    adj_magnetic,
    adj_polar,
    permittivity,
    conductivity,
    debye_class,
    debye_rate,
    debye_strength,
    wavelet,
    src_cell,
    src_sign,
    rec_owner,
    rec_pos,
    observed,
):
    width, depth, span = permittivity.shape
    steps = wavelet.shape[0]
    nsub = lax.axis_size("sub")
    nshot = lax.axis_size("shot")
    mine = lax.axis_index("sub")
    facts = jnp.stack([mine, 1 - mine % 2, jnp.minimum(mine, 1)]).astype(F32)
    meta = jnp.broadcast_to(jnp.pad(facts, (0, 5))[:, None], (8, 128))
    plane = (depth, span)

    in_x, rest = split_index(rec_pos[0], width)
    rec_y, rec_z = split_index(rest, span)
    rec_row = (rec_owner[0, :, 0] * width + in_x) * depth + rec_z
    listed = jnp.concatenate([rec_row[None].astype(F32), rec_y[None].astype(F32), observed[0]], axis=0)
    def receivers(name, which):
        (maps,) = call(
            lambda *refs: receiver_kernel(width, depth, which, *refs),
            name,
            [meta, got],
            [(len(which), width, *plane)],
            [(len(which) * width * depth, span)],
            work=10**9,
        )
        return maps

    fields = (electric[0], magnetic[0], polar[0])
    adjoint = (adj_electric[0], adj_magnetic[0], adj_polar[0])

    own = (3, width, *plane)
    *fields, coef, src, tab, a1, b1 = call(
        lambda *refs: first_kernel(width * nsub, *refs),
        "first",
        [meta],
        [own, own, own, (4, width, *plane), (width, *plane), (steps, span), *[(2 * ROUND + 2, *plane)] * 2],
        [
            (width, *plane),
            (width, *plane),
            pltpu.VMEM((width, *plane), jnp.int32),
            pltpu.VMEM(src_cell.shape, jnp.int32),
            pltpu.VMEM(src_sign.shape, jnp.int32),
            pltpu.SMEM(debye_rate.shape, F32),
            pltpu.SMEM(debye_strength.shape, F32),
            pltpu.SMEM(wavelet.shape, F32),
            pltpu.SemaphoreType.DMA((11,)),
        ],
        [*fields, permittivity, conductivity, debye_class, src_cell, src_sign, debye_rate, debye_strength, wavelet],
    )
    got_a1, got_b1 = exchange(a1, b1)
    listed, a1 = lax.optimization_barrier((listed, a1))
    got = lax.all_to_all(jnp.broadcast_to(listed[None], (nsub, *listed.shape)), "sub", 0, 0)
    edges = [(2 * ROUND, *plane)] * 2
    hist1, hs, ps, coefh, a2, b2 = call(
        forward_one_kernel,
        "forward_one",
        [meta, tab, *fields, coef, src, got_b1, got_a1],
        [(ROUND, *own), own, own, (2, 2, *plane), *edges],
    )
    got, hs = lax.optimization_barrier((got, hs))
    got_a2, got_b2 = exchange(a2, b2)
    maps = receivers("receivers_late", (0, *range(steps, ROUND, -1)))
    hist2, adj_h, a3, b3 = call(
        forward_two_kernel,
        "forward_two",
        [meta, tab, hist1, hs, ps, coef, coefh, src, maps, *adjoint, got_b2, got_a2],
        [(ROUND, *own), own, *edges],
        [own, own],
    )
    got, hist2 = lax.optimization_barrier((got, hist2))
    got_a3, got_b3 = exchange(a3, b3)
    maps2 = receivers("receivers_early", tuple(range(ROUND, 0, -1)))
    adj, hs, ps, a4, b4 = call(
        adjoint_one_kernel,
        "adjoint_one",
        [meta, adjoint[0], adj_h, adjoint[2], coef, coefh, maps, maps2, hist1, hist2, got_b3, got_a3],
        [(ROUND, *own), own, own, *edges],
    )
    got_a4, got_b4 = exchange(a4, b4)
    (corr,) = call(correlation_kernel, "correlation", [adj, hist1, hist2], [(2, width, *plane)], work=10**9)
    (corr,) = call(
        adjoint_two_kernel,
        "adjoint_two",
        [meta, adj, hs, ps, coef, coefh, maps, maps2, fields[0], hist1, corr, got_b4, got_a4],
        [(2, width, *plane)],
        [own, own, own],
    )
    total = shot_sum(corr)
    return (-(total[0] / (steps * nshot)), -(total[1] / (steps * nshot)))


def solution(mesh):
    in_specs = (
        P("shot", None, "sub", None, None),
        P("shot", None, "sub", None, None),
        P("shot", None, "sub", None, None),
        P("shot", None, "sub", None, None),
        P("shot", None, "sub", None, None),
        P("shot", None, "sub", None, None),
        P("sub", None, None),
        P("sub", None, None),
        P("sub", None, None),
        P(),
        P(),
        P(),
        P("shot", None),
        P("shot", None),
        P("shot", "sub", None),
        P("shot", "sub"),
        P("shot", None, "sub"),
    )
    out_specs = (P("sub", None, None), P("sub", None, None))
    return jax.shard_map(
        per_device, mesh=mesh, in_specs=in_specs, out_specs=out_specs, check_vma=False
    )
```

```python
import jax
import jax.numpy as jnp
from jax import lax
from jax.experimental import pallas as pl
from jax.experimental.pallas import tpu as pltpu
from jax.sharding import PartitionSpec as P

ROUND = 3
F32 = jnp.float32


def pair_swap(block, axis, first):
    route = []
    for i in range(first, lax.axis_size(axis) - 1, 2):
        route += [(i, i + 1), (i + 1, i)]
    return lax.ppermute(block, axis, route)


def exchange(inner, outer):
    got_outer = pair_swap(outer, "sub", 1)
    got_inner = pair_swap(inner, "sub", 0)
    return got_inner, got_outer


def shot_sum(x):
    n = lax.axis_size("shot")
    if n & (n - 1):
        return lax.psum(x, "shot")
    flip = 1
    while flip < n:
        x = x + lax.ppermute(x, "shot", [(i, i ^ flip) for i in range(n)])
        flip = 2 * flip + 1
    return x


def split_index(v, n):
    if n & (n - 1) == 0:
        return v & (n - 1), v >> (n.bit_length() - 1)
    return v % n, v // n


def ahead(u, axis):
    n = u.shape[axis]
    edge = lax.broadcasted_iota(jnp.int32, u.shape, axis) == n - 1
    return jnp.where(edge, 0.0, pltpu.roll(u, n - 1, axis))


def behind(u, axis):
    edge = lax.broadcasted_iota(jnp.int32, u.shape, axis) == 0
    return jnp.where(edge, 0.0, pltpu.roll(u, 1, axis))


def dfy(u):
    return ahead(u, 1) - u


def dfz(u):
    return ahead(u, 0) - u


def dby(u):
    return u - behind(u, 1)


def dbz(u):
    return u - behind(u, 0)


def h_step(h, e, e_next, keep=None, parts=(0, 1, 2)):
    ex, ey, ez = e[0], e[1], e[2]
    new = {}
    if 0 in parts:
        new[0] = h[0] - 0.5 * (dfy(ez) - dfz(ey))
    if 1 in parts:
        ahead_z = -ez if e_next is None else (e_next[2] if keep is None else e_next[2] * keep) - ez
        new[1] = h[1] - 0.5 * (dfz(ex) - ahead_z)
    if 2 in parts:
        ahead_y = -ey if e_next is None else (e_next[1] if keep is None else e_next[1] * keep) - ey
        new[2] = h[2] - 0.5 * (ahead_y - dfy(ex))
    return new


def e_step(e, h, h_prev, p, coef, inject, parts=(0, 1, 2)):
    ca, cb = coef[0], coef[1]
    new = {}
    for c in parts:
        if c == 0:
            curl = dby(h[2]) - dbz(h[1])
        elif c == 1:
            curl = dbz(h[0]) - (h[2] if h_prev is None else h[2] - h_prev[2])
        else:
            curl = (h[1] if h_prev is None else h[1] - h_prev[1]) - dby(h[0])
        new[c] = ca * e[c] + cb * (curl - p[c])
        if c == 1:
            new[c] = new[c] + inject
    return new


def p_step(p, e_new, coef):
    return {c: coef[2] * p[c] + coef[3] * e_new[c] for c in e_new}


class Planes:
    def __init__(self):
        self.at = {}

    def put(self, key, ref, *idx):
        self.at[key] = (ref, idx)

    def get(self, kind, c, i):
        ref, idx = self.at[kind, c, i]
        return ref[idx]

    def triple(self, kind, i, parts=(0, 1, 2)):
        return {c: self.get(kind, c, i) for c in parts}


def is_even(meta, shape):
    return jnp.broadcast_to(meta[1:2, :], shape) > 0.5


def pick(even, a_ref, b_ref, k, low):
    a, b = a_ref[k], b_ref[k]
    return jnp.where(even, b, a) if low else jnp.where(even, a, b)


def emit(even, a_ref, b_ref, k, right, left):
    a_ref[k] = jnp.where(even, right, left)
    b_ref[k] = jnp.where(even, left, right)


def edge_values(planes, coef_of, inject, h_out):
    last = planes.last
    lo = last - ROUND + 1
    e0 = {i: planes.triple("E", i) for i in range(last + 1)}
    h1 = {i: h_step(planes.triple("H", i), e0[i], e0[i + 1] if i < last else None) for i in range(last + 1)}
    p0 = {i: planes.triple("P", i) for i in range(last + 1)}
    raw = planes.triple("H", last)
    for c in range(3):
        for i in range(last):
            h_out[c, i] = h1[i][c]
        h_out[c, last] = raw[c]
    e, h, p = dict(e0), dict(h1), dict(p0)
    right = []
    for step in range(1, ROUND + 1):
        if step > 1:
            parts = (1, 2) if step == ROUND else (0, 1, 2)
            for i in range(lo + step - 1, last + 1):
                h[i] = {**h[i], **h_step(h[i], e[i], e[i + 1] if i < last else None, parts=parts)}
        right += [h[last][1], h[last][2]]
        if step < ROUND:
            for i in range(lo + step, last + 1):
                e[i] = e_step(e[i], h[i], h[i - 1], p[i], coef_of(i), inject(step, i))
                p[i] = p_step(p[i], e[i], coef_of(i))
    e, h, p = dict(e0), dict(h1), dict(p0)
    left = [e[0][1], e[0][2]]
    for step in range(1, ROUND):
        if step > 1:
            for i in range(ROUND - step):
                h[i] = h_step(h[i], e[i], e[i + 1])
        for i in range(ROUND - step):
            parts = (0, 1, 2) if i < ROUND - step - 1 else (1, 2)
            e[i] = e_step(e[i], h[i], h[i - 1] if i > 0 else None, p[i], coef_of(i), inject(step, i), parts)
            p[i] = p_step(p[i], e[i], coef_of(i))
        left += [e[0][1], e[0][2]]
    return right, left


def emit_all(even, a_ref, b_ref, right, left, first=0):
    for k, (r, l) in enumerate(zip(right, left)):
        emit(even, a_ref, b_ref, first + k, r, l)


def own_planes(e_ref, h_ref, p_ref, level=None):
    planes = Planes()
    width = h_ref.shape[1]
    planes.last = width - 1
    for i in range(width):
        for c in range(3):
            planes.put(("E", c, i), e_ref, *((c, i) if level is None else (level, c, i)))
            planes.put(("H", c, i), h_ref, c, i)
            planes.put(("P", c, i), p_ref, c, i)
    return planes


def source_map(cell_ref, sign_ref, mine, width, depth, span, full_x):
    flat = cell_ref[...]
    x, rest = split_index(flat, full_x)
    y, z = split_index(rest, span)
    n = flat.shape[1]
    row = (x - jnp.broadcast_to(mine, (1, n)) * width) * depth + z
    rows = width * depth
    hot = lax.broadcasted_iota(jnp.int32, (rows, n), 0) == row
    amp = (2 * sign_ref[...] - 1).astype(F32)
    where_y = lax.broadcasted_iota(jnp.int32, (span, n), 0) == y
    left = jnp.where(hot, 1.0, 0.0).astype(jnp.bfloat16)
    right = jnp.where(where_y, amp, 0.0).astype(jnp.bfloat16)
    return lax.dot_general(left, right, (((1,), (1,)), ((), ())), preferred_element_type=F32)


def first_kernel(full_x, meta, e_in, h_in, p_in, perm_in, cond_in, cls_in, cells_in, signs_in, rate_in, strength_in,
                 wavelet_in, pos_in, owner_in, seen_in, e_ref, h_ref, p_ref, coef_ref, src_ref, tab_ref, list_out, a_ref,
                 b_ref, perm, cond, cls, cells, signs, rate_t, strength_t, wavelet, pos, owner, seen, listed, sems):
    width, depth, span = perm.shape
    even = is_even(meta, (depth, span))
    moves = [(cells_in, cells), (signs_in, signs), (wavelet_in, wavelet), (rate_in, rate_t), (strength_in, strength_t)]
    moves += [(pos_in, pos), (owner_in, owner), (seen_in, seen)]
    moves += [(perm_in, perm), (cond_in, cond), (cls_in, cls), (e_in, e_ref), (h_in, h_ref), (p_in, p_ref)]
    copies = [pltpu.make_async_copy(a, b, sems.at[k]) for k, (a, b) in enumerate(moves)]
    for copy in copies:
        copy.start()
    for copy in copies[:8]:
        copy.wait()
    in_x, rest = split_index(pos[...], width)
    rec_y, rec_z = split_index(rest, span)
    lines = [((owner[...] * width + in_x) * depth + rec_z).astype(F32), rec_y.astype(F32)]
    lines = jnp.concatenate(lines + [seen[k] for k in range(seen.shape[0])], axis=0)
    for slab in range(listed.shape[0]):
        listed[slab] = lines
    leave = pltpu.make_async_copy(listed, list_out, sems.at[len(moves)])
    leave.start()
    for k in range(wavelet.shape[0]):
        tab_ref[k:k + 1, :] = jnp.full((1, span), wavelet[k], F32)
    src = source_map(cells, signs, meta[0:1, 0:1].astype(jnp.int32), width, depth, span, full_x)
    src_ref[...] = src.reshape(width, depth, span)
    for copy in copies[8:11]:
        copy.wait()
    for i in range(width):
        double = 2.0 * perm[i]
        share = 1.0 / (double + cond[i])
        coef_ref[0, i] = (double - cond[i]) * share
        coef_ref[1, i] = share
        kind = cls[i]
        rate = jnp.zeros((depth, span), F32)
        gain = jnp.zeros((depth, span), F32)
        for k in range(rate_t.shape[0]):
            rate = jnp.where(kind == k, rate_t[k], rate)
            gain = jnp.where(kind == k, (1.0 - rate_t[k]) * strength_t[k], gain)
        coef_ref[2, i] = rate
        coef_ref[3, i] = gain
    for copy in copies[11:]:
        copy.wait()
    planes = own_planes(e_ref, h_ref, p_ref)
    right, left = edge_values(planes, lambda i: [coef_ref[k, i] for k in range(4)],
                              lambda step, i: src_ref[i] * wavelet[step - 1], h_ref)
    last = width - 1
    right += [coef_ref[0, last] - coef_ref[1, last] * coef_ref[3, last], coef_ref[1, last]]
    left += [coef_ref[0, 0] - coef_ref[1, 0] * coef_ref[3, 0], coef_ref[1, 0]]
    emit_all(even, a_ref, b_ref, right, left)
    leave.wait()


def receiver_kernel(width, depth, which, meta, got, maps_ref, acc):
    rows = width * depth
    span = acc.shape[1]
    blocks, _, n = got.shape
    acc[...] = jnp.zeros(acc.shape, F32)
    first_row = meta[0:1, :] * (width * depth)
    row_at = lax.broadcasted_iota(jnp.int32, (rows, n), 0).astype(F32)
    y_at = lax.broadcasted_iota(jnp.int32, (span, n), 0).astype(F32)
    group = max(g for g in (1, 2, 4, 8) if blocks % g == 0)
    zero = jnp.zeros((rows, n), jnp.bfloat16)

    def block(k, carry):
        left = [[] for _ in which]
        right = []
        for b in range(group):
            at = k * group + b
            hot = row_at == got[at, 0:1, :] - first_row[:, :n]
            at_y = jnp.where(y_at == got[at, 1:2, :], 1.0, 0.0).astype(jnp.bfloat16)
            right += [at_y] * 3
            for part, s in zip(left, which):
                if s == 0:
                    part += [jnp.where(hot, 1.0, 0.0).astype(jnp.bfloat16), zero, zero]
                    continue
                v = got[at, 1 + s:2 + s, :]
                high = v.astype(jnp.bfloat16).astype(F32)
                mid = (v - high).astype(jnp.bfloat16).astype(F32)
                low = (v - high) - mid
                part += [jnp.where(hot, u, 0.0).astype(jnp.bfloat16) for u in (high, mid, low)]
        acc[...] += lax.dot_general(
            jnp.concatenate([jnp.concatenate(part, axis=1) for part in left], axis=0) if len(left) > 1 else jnp.concatenate(left[0], axis=1),
            jnp.concatenate(right, axis=1),
            (((1,), (1,)), ((), ())),
            preferred_element_type=F32,
        )
        return carry

    lax.fori_loop(0, blocks // group, block, 0)
    maps_ref[...] = acc[...].reshape(maps_ref.shape)


def round_body(planes, meta, coef_ref, coefh_ref, a_ref, b_ref, inject, dest, seen=None, final=False):
    even = is_even(meta, coef_ref.shape[2:])
    keep = meta[2:3, :]
    last = planes.last

    def coef_of(i):
        return [coef_ref[k, i] for k in range(4)]

    before, after = ([coefh_ref[side, k] for k in range(2)] for side in (0, 1))
    rest = {c: 0.0 for c in range(3)}
    zero = jnp.zeros(coef_ref.shape[2:], F32)
    none = {c: zero for c in range(3)}

    def store(kind, c, i, level, value):
        ref, idx = dest(kind, c, i, level)
        ref[idx] = value
        planes.put((kind, c, i), ref, *idx)

    low_e = low_h = high_e = high_h = None
    for level in range(1, ROUND + 1):
        sent = 2 * (level - 1)
        edge = {c: planes.get("E", c, 0) * keep for c in (1, 2)}
        if level == 1:
            low_h = {0: zero, 1: 0.5 * edge[2], 2: -0.5 * edge[1]}
            far = None
        else:
            far = {1: 0.5 * low_e[2], 2: -0.5 * low_e[1]}
            low_h.update(h_step(low_h, low_e, edge, parts=(0, 1, 2) if level < ROUND else (1, 2)))
        if level == 1:
            low_e = {0: before[1] * (dby(low_h[2]) - dbz(low_h[1])), 1: -(before[1] * low_h[2]), 2: before[1] * low_h[1]}
        elif level < ROUND:
            low_e = e_step(low_e, low_h, far, rest, before, 0.0)
        h_prev = {c: low_h[c] + pick(even, a_ref, b_ref, sent + c - 1, True) for c in (1, 2)}
        now_h = {}
        for i in range(last + 1):
            h = planes.triple("H", i)
            if level > 1 or i == last:
                if i < last:
                    e_next = planes.triple("E", i + 1, (1, 2))
                else:
                    e_next = {c: pick(even, a_ref, b_ref, sent + c - 1, False) for c in (1, 2)}
                    if level > 1:
                        e_next = {c: e_next[c] + high_e[c] for c in (1, 2)}
                h = h_step(h, planes.triple("E", i), e_next)
                for c in range(3):
                    if not (final and level == ROUND):
                        store("H", c, i, level, h[c])
            now_h[i] = h
        for i in range(last + 1):
            h = now_h[i]
            cf = coef_of(i)
            new = e_step(planes.triple("E", i), h, h_prev, planes.triple("P", i), cf, inject(level, i))
            for c in range(3):
                store("E", c, i, level, new[c])
            if not (final and level == ROUND):
                pn = p_step(planes.triple("P", i), new, cf)
                for c in range(3):
                    store("P", c, i, level, pn[c])
            if seen is not None:
                seen(level, i, new)
            h_prev = h
        if level == 1:
            high_e = {0: zero, 1: after[1] * h_prev[2], 2: -(after[1] * h_prev[1])}
            high_h = none
        elif level < ROUND:
            high_h = h_step(high_h, high_e, None)
            high_e = e_step(high_e, high_h, h_prev, rest, after, 0.0)


def store_in(e_ref, h_ref, p_ref, by_level=False):
    refs = {"E": e_ref, "H": h_ref, "P": p_ref}

    def dest(kind, c, i, level):
        return refs[kind], ((level - 1, c, i) if kind == "E" and by_level else (c, i))

    return dest


def forward_one_kernel(meta, tab_ref, e_ref, h_ref, p_ref, coef_ref, src_ref, b_ref, a_ref,
                       hist_ref, hs_ref, ps_ref, coefh_ref, oa_ref, ob_ref):
    even = is_even(meta, e_ref.shape[2:])
    wavelet = 0
    for side in (0, 1):
        for k in range(2):
            coefh_ref[side, k] = pick(even, a_ref, b_ref, 2 * ROUND + k, side == 0)
    planes = own_planes(e_ref, h_ref, p_ref)

    def inject(level, i):
        return src_ref[i] * tab_ref[wavelet + level - 1:wavelet + level, :]

    round_body(planes, meta, coef_ref, coefh_ref, a_ref, b_ref, inject, store_in(hist_ref, hs_ref, ps_ref, True))
    right, left = edge_values(planes, lambda i: [coef_ref[k, i] for k in range(4)], lambda step, i: inject(ROUND + step, i), hs_ref)
    emit_all(even, oa_ref, ob_ref, right, left)


def forward_two_kernel(meta, tab_ref, hist_in, hs_in, ps_in, coef_ref, coefh_ref, src_ref, maps_ref, e_ref, h_ref, p_ref,
                       b_ref, a_ref, hist_ref, h_out, oa_ref, ob_ref, hs_ref, ps_ref):
    wavelet = ROUND
    round_body(own_planes(hist_in, hs_in, ps_in, ROUND - 1), meta, coef_ref, coefh_ref, a_ref, b_ref,
               lambda level, i: src_ref[i] * tab_ref[wavelet + level - 1:wavelet + level, :],
               store_in(hist_ref, hs_ref, ps_ref, True), final=True)

    def inject(step, i):
        return maps_ref[0, i] * hist_ref[ROUND - step, 1, i] - maps_ref[step, i]

    right, left = edge_values(own_planes(e_ref, h_ref, p_ref), lambda i: [coef_ref[k, i] for k in range(4)], inject, h_out)
    emit_all(is_even(meta, e_ref.shape[2:]), oa_ref, ob_ref, right, left)


def correlate(corr_ref, i, b, now, prev, add):
    eps = b[0] * (now[0] - prev[0]) + b[1] * (now[1] - prev[1]) + b[2] * (now[2] - prev[2])
    sig = b[0] * now[0] + b[1] * now[1] + b[2] * now[2]
    if add is not None:
        eps, sig = eps + add[0, i], sig + add[1, i]
    corr_ref[0, i] = eps
    corr_ref[1, i] = sig


def adjoint_one_kernel(meta, e_ref, h_ref, p_ref, coef_ref, coefh_ref, maps_ref, maps2_ref, hist1_ref, hist2_ref,
                       b_ref, a_ref, e_out, hs_ref, ps_ref, oa_ref, ob_ref):
    planes = own_planes(e_ref, h_ref, p_ref)

    def inject(level, i):
        return maps_ref[0, i] * hist2_ref[ROUND - level, 1, i] - maps_ref[level, i]

    def inject_next(step, i):
        return maps_ref[0, i] * hist1_ref[ROUND - step, 1, i] - maps2_ref[step - 1, i]

    round_body(planes, meta, coef_ref, coefh_ref, a_ref, b_ref, inject, store_in(e_out, hs_ref, ps_ref, True))
    right, left = edge_values(planes, lambda i: [coef_ref[k, i] for k in range(4)], inject_next, hs_ref)
    emit_all(is_even(meta, e_ref.shape[2:]), oa_ref, ob_ref, right, left)


def correlation_kernel(adj_ref, hist1_ref, hist2_ref, corr_ref):
    for i in range(corr_ref.shape[1]):
        for level in range(1, ROUND + 1):
            n = ROUND - level
            e = [adj_ref[level - 1, c, i] for c in range(3)]
            now = [hist2_ref[n, c, i] for c in range(3)]
            prev = [hist2_ref[n - 1, c, i] if n > 0 else hist1_ref[ROUND - 1, c, i] for c in range(3)]
            correlate(corr_ref, i, e, now, prev, corr_ref if level > 1 else None)


def adjoint_two_kernel(meta, e_ref, hs_in, ps_in, coef_ref, coefh_ref, maps_ref, maps2_ref, e0_ref, hist1_ref,
                       corr_in, b_ref, a_ref, corr_ref, es_ref, hs_ref, ps_ref):
    def seen(level, i, e):
        n = ROUND - level
        now = [hist1_ref[n, c, i] for c in range(3)]
        prev = [hist1_ref[n - 1, c, i] if n > 0 else e0_ref[c, i] for c in range(3)]
        correlate(corr_ref, i, e, now, prev, corr_ref if level > 1 else corr_in)

    def inject(level, i):
        return maps_ref[0, i] * hist1_ref[ROUND - level, 1, i] - maps2_ref[level - 1, i]

    round_body(own_planes(e_ref, hs_in, ps_in, ROUND - 1), meta, coef_ref, coefh_ref, a_ref, b_ref, inject,
               store_in(es_ref, hs_ref, ps_ref), seen, final=True)


def call(body, name, inputs, outs, scratch=(), remote=(), work=10**10, stay_out=()):
    vmem = pl.BlockSpec(memory_space=pltpu.VMEM)
    stay = pl.BlockSpec(memory_space=pltpu.HBM)
    return pl.pallas_call(
        body,
        name=name,
        out_shape=[jax.ShapeDtypeStruct(s, F32) for s in outs],
        in_specs=[vmem] * len(inputs) + [stay] * len(remote),
        out_specs=[stay if k in stay_out else vmem for k in range(len(outs))],
        scratch_shapes=[s if not isinstance(s, tuple) else pltpu.VMEM(s, F32) for s in scratch],
        cost_estimate=pl.CostEstimate(flops=work, transcendentals=0, bytes_accessed=0),
        compiler_params=pltpu.CompilerParams(vmem_limit_bytes=48 * 1024 * 1024),
    )(*inputs, *[pltpu.with_memory_space_constraint(x, pltpu.HBM) for x in remote])


def per_device(
    electric,
    magnetic,
    polar,
    adj_electric,
    adj_magnetic,
    adj_polar,
    permittivity,
    conductivity,
    debye_class,
    debye_rate,
    debye_strength,
    wavelet,
    src_cell,
    src_sign,
    rec_owner,
    rec_pos,
    observed,
):
    width, depth, span = permittivity.shape
    steps = wavelet.shape[0]
    nsub = lax.axis_size("sub")
    nshot = lax.axis_size("shot")
    mine = lax.axis_index("sub")
    line = lax.broadcasted_iota(jnp.int32, (8, 128), 0)
    meta = jnp.where(line == 0, mine, jnp.where(line == 1, 1 - mine % 2, jnp.minimum(mine, 1))).astype(F32)
    plane = (depth, span)

    def receivers(name, which):
        (maps,) = call(
            lambda *refs: receiver_kernel(width, depth, which, *refs),
            name,
            [meta, got],
            [(len(which), width, *plane)],
            [(len(which) * width * depth, span)],
            work=10**9,
        )
        return maps

    fields = (electric[0], magnetic[0], polar[0])
    adjoint = (adj_electric[0], adj_magnetic[0], adj_polar[0])

    own = (3, width, *plane)
    list_shape = (nsub, steps + 2, rec_pos.shape[1])
    *fields, coef, src, tab, listed, a1, b1 = call(
        lambda *refs: first_kernel(width * nsub, *refs),
        "first",
        [meta],
        [own, own, own, (4, width, *plane), (width, *plane), (steps, span), list_shape, *[(2 * ROUND + 2, *plane)] * 2],
        [
            (width, *plane),
            (width, *plane),
            pltpu.VMEM((width, *plane), jnp.int32),
            pltpu.VMEM(src_cell.shape, jnp.int32),
            pltpu.VMEM(src_sign.shape, jnp.int32),
            pltpu.SMEM(debye_rate.shape, F32),
            pltpu.SMEM(debye_strength.shape, F32),
            pltpu.SMEM(wavelet.shape, F32),
            pltpu.VMEM(rec_pos.shape, jnp.int32),
            pltpu.VMEM(rec_pos.shape, jnp.int32),
            (steps, *rec_pos.shape),
            list_shape,
            pltpu.SemaphoreType.DMA((15,)),
        ],
        [
            *fields, permittivity, conductivity, debye_class, src_cell, src_sign, debye_rate, debye_strength, wavelet,
            rec_pos, rec_owner[:, :, 0], jnp.swapaxes(observed, 0, 1),
        ],
        stay_out=(6,),
    )
    got_a1, got_b1 = exchange(a1, b1)
    listed, a1 = lax.optimization_barrier((listed, a1))
    got = lax.all_to_all(listed, "sub", 0, 0)
    edges = [(2 * ROUND, *plane)] * 2
    hist1, hs, ps, coefh, a2, b2 = call(
        forward_one_kernel,
        "forward_one",
        [meta, tab, *fields, coef, src, got_b1, got_a1],
        [(ROUND, *own), own, own, (2, 2, *plane), *edges],
    )
    got, hs = lax.optimization_barrier((got, hs))
    got_a2, got_b2 = exchange(a2, b2)
    maps = receivers("receivers_late", (0, *range(steps, ROUND, -1)))
    hist2, adj_h, a3, b3 = call(
        forward_two_kernel,
        "forward_two",
        [meta, tab, hist1, hs, ps, coef, coefh, src, maps, *adjoint, got_b2, got_a2],
        [(ROUND, *own), own, *edges],
        [own, own],
    )
    got, hist2 = lax.optimization_barrier((got, hist2))
    got_a3, got_b3 = exchange(a3, b3)
    maps2 = receivers("receivers_early", tuple(range(ROUND, 0, -1)))
    adj, hs, ps, a4, b4 = call(
        adjoint_one_kernel,
        "adjoint_one",
        [meta, adjoint[0], adj_h, adjoint[2], coef, coefh, maps, maps2, hist1, hist2, got_b3, got_a3],
        [(ROUND, *own), own, own, *edges],
    )
    got_a4, got_b4 = exchange(a4, b4)
    (corr,) = call(correlation_kernel, "correlation", [adj, hist1, hist2], [(2, width, *plane)], work=10**9)
    (corr,) = call(
        adjoint_two_kernel,
        "adjoint_two",
        [meta, adj, hs, ps, coef, coefh, maps, maps2, fields[0], hist1, corr, got_b4, got_a4],
        [(2, width, *plane)],
        [own, own, own],
    )
    total = shot_sum(corr)
    return (-(total[0] / (steps * nshot)), -(total[1] / (steps * nshot)))


def solution(mesh):
    in_specs = (
        P("shot", None, "sub", None, None),
        P("shot", None, "sub", None, None),
        P("shot", None, "sub", None, None),
        P("shot", None, "sub", None, None),
        P("shot", None, "sub", None, None),
        P("shot", None, "sub", None, None),
        P("sub", None, None),
        P("sub", None, None),
        P("sub", None, None),
        P(),
        P(),
        P(),
        P("shot", None),
        P("shot", None),
        P("shot", "sub", None),
        P("shot", "sub"),
        P("shot", None, "sub"),
    )
    out_specs = (P("sub", None, None), P("sub", None, None))
    return jax.shard_map(
        per_device, mesh=mesh, in_specs=in_specs, out_specs=out_specs, check_vma=False
    )
```

```python
import jax
import jax.numpy as jnp
from jax import lax
from jax.experimental import pallas as pl
from jax.experimental.pallas import tpu as pltpu
from jax.sharding import PartitionSpec as P

ROUND = 3
F32 = jnp.float32


def pair_swap(block, axis, first):
    route = []
    for i in range(first, lax.axis_size(axis) - 1, 2):
        route += [(i, i + 1), (i + 1, i)]
    return lax.ppermute(block, axis, route)


def exchange(inner, outer):
    got_outer = pair_swap(outer, "sub", 1)
    got_inner = pair_swap(inner, "sub", 0)
    return got_inner, got_outer


def shot_sum(x):
    n = lax.axis_size("shot")
    if n & (n - 1):
        return lax.psum(x, "shot")
    flip = 1
    while flip < n:
        x = x + lax.ppermute(x, "shot", [(i, i ^ flip) for i in range(n)])
        flip = 2 * flip + 1
    return x


def split_index(v, n):
    if n & (n - 1) == 0:
        return v & (n - 1), v >> (n.bit_length() - 1)
    return v % n, v // n


def ahead(u, axis):
    n = u.shape[axis]
    edge = lax.broadcasted_iota(jnp.int32, u.shape, axis) == n - 1
    return jnp.where(edge, 0.0, pltpu.roll(u, n - 1, axis))


def behind(u, axis):
    edge = lax.broadcasted_iota(jnp.int32, u.shape, axis) == 0
    return jnp.where(edge, 0.0, pltpu.roll(u, 1, axis))


def dfy(u):
    return ahead(u, 1) - u


def dfz(u):
    return ahead(u, 0) - u


def dby(u):
    return u - behind(u, 1)


def dbz(u):
    return u - behind(u, 0)


def h_step(h, e, e_next, keep=None, parts=(0, 1, 2)):
    ex, ey, ez = e[0], e[1], e[2]
    new = {}
    if 0 in parts:
        new[0] = h[0] - 0.5 * (dfy(ez) - dfz(ey))
    if 1 in parts:
        ahead_z = -ez if e_next is None else (e_next[2] if keep is None else e_next[2] * keep) - ez
        new[1] = h[1] - 0.5 * (dfz(ex) - ahead_z)
    if 2 in parts:
        ahead_y = -ey if e_next is None else (e_next[1] if keep is None else e_next[1] * keep) - ey
        new[2] = h[2] - 0.5 * (ahead_y - dfy(ex))
    return new


def e_step(e, h, h_prev, p, coef, inject, parts=(0, 1, 2)):
    ca, cb = coef[0], coef[1]
    new = {}
    for c in parts:
        if c == 0:
            curl = dby(h[2]) - dbz(h[1])
        elif c == 1:
            curl = dbz(h[0]) - (h[2] if h_prev is None else h[2] - h_prev[2])
        else:
            curl = (h[1] if h_prev is None else h[1] - h_prev[1]) - dby(h[0])
        new[c] = ca * e[c] + cb * (curl - p[c])
        if c == 1:
            new[c] = new[c] + inject
    return new


def p_step(p, e_new, coef):
    return {c: coef[2] * p[c] + coef[3] * e_new[c] for c in e_new}


class Planes:
    def __init__(self):
        self.at = {}

    def put(self, key, ref, *idx):
        self.at[key] = (ref, idx)

    def get(self, kind, c, i):
        ref, idx = self.at[kind, c, i]
        return ref[idx]

    def triple(self, kind, i, parts=(0, 1, 2)):
        return {c: self.get(kind, c, i) for c in parts}


def is_even(meta, shape):
    return jnp.broadcast_to(meta[1:2, :], shape) > 0.5


def pick(even, a_ref, b_ref, k, low):
    a, b = a_ref[k], b_ref[k]
    return jnp.where(even, b, a) if low else jnp.where(even, a, b)


def emit(even, a_ref, b_ref, k, right, left):
    a_ref[k] = jnp.where(even, right, left)
    b_ref[k] = jnp.where(even, left, right)


def edge_values(planes, coef_of, inject, h_out):
    last = planes.last
    lo = last - ROUND + 1
    e0 = {i: planes.triple("E", i) for i in range(last + 1)}
    h1 = {i: h_step(planes.triple("H", i), e0[i], e0[i + 1] if i < last else None) for i in range(last + 1)}
    p0 = {i: planes.triple("P", i) for i in range(last + 1)}
    raw = planes.triple("H", last)
    for c in range(3):
        for i in range(last):
            h_out[c, i] = h1[i][c]
        h_out[c, last] = raw[c]
    e, h, p = dict(e0), dict(h1), dict(p0)
    right = []
    for step in range(1, ROUND + 1):
        if step > 1:
            parts = (1, 2) if step == ROUND else (0, 1, 2)
            for i in range(lo + step - 1, last + 1):
                h[i] = {**h[i], **h_step(h[i], e[i], e[i + 1] if i < last else None, parts=parts)}
        right += [h[last][1], h[last][2]]
        if step < ROUND:
            for i in range(lo + step, last + 1):
                e[i] = e_step(e[i], h[i], h[i - 1], p[i], coef_of(i), inject(step, i))
                p[i] = p_step(p[i], e[i], coef_of(i))
    e, h, p = dict(e0), dict(h1), dict(p0)
    left = [e[0][1], e[0][2]]
    for step in range(1, ROUND):
        if step > 1:
            for i in range(ROUND - step):
                h[i] = h_step(h[i], e[i], e[i + 1])
        for i in range(ROUND - step):
            parts = (0, 1, 2) if i < ROUND - step - 1 else (1, 2)
            e[i] = e_step(e[i], h[i], h[i - 1] if i > 0 else None, p[i], coef_of(i), inject(step, i), parts)
            p[i] = p_step(p[i], e[i], coef_of(i))
        left += [e[0][1], e[0][2]]
    return right, left


def emit_all(even, a_ref, b_ref, right, left, first=0):
    for k, (r, l) in enumerate(zip(right, left)):
        emit(even, a_ref, b_ref, first + k, r, l)


def own_planes(e_ref, h_ref, p_ref, level=None):
    planes = Planes()
    width = h_ref.shape[1]
    planes.last = width - 1
    for i in range(width):
        for c in range(3):
            planes.put(("E", c, i), e_ref, *((c, i) if level is None else (level, c, i)))
            planes.put(("H", c, i), h_ref, c, i)
            planes.put(("P", c, i), p_ref, c, i)
    return planes


def source_map(cell_ref, sign_ref, mine, width, depth, span, full_x):
    flat = cell_ref[...]
    x, rest = split_index(flat, full_x)
    y, z = split_index(rest, span)
    n = flat.shape[1]
    row = (x - jnp.broadcast_to(mine, (1, n)) * width) * depth + z
    rows = width * depth
    hot = lax.broadcasted_iota(jnp.int32, (rows, n), 0) == row
    amp = (2 * sign_ref[...] - 1).astype(F32)
    where_y = lax.broadcasted_iota(jnp.int32, (span, n), 0) == y
    left = jnp.where(hot, 1.0, 0.0).astype(jnp.bfloat16)
    right = jnp.where(where_y, amp, 0.0).astype(jnp.bfloat16)
    return lax.dot_general(left, right, (((1,), (1,)), ((), ())), preferred_element_type=F32)


def first_kernel(full_x, meta, e_in, h_in, p_in, perm_in, cond_in, cls_in, cells_in, signs_in, rate_in, strength_in,
                 wavelet_in, pos_in, owner_in, seen_in, e_ref, h_ref, p_ref, coef_ref, src_ref, tab_ref, list_out, a_ref,
                 b_ref, perm, cond, cls, cells, signs, rate_t, strength_t, wavelet, pos, owner, seen, listed, sems):
    width, depth, span = perm.shape
    even = is_even(meta, (depth, span))
    moves = [(cells_in, cells), (signs_in, signs), (wavelet_in, wavelet), (rate_in, rate_t), (strength_in, strength_t)]
    moves += [(pos_in, pos), (owner_in, owner), (seen_in, seen)]
    moves += [(perm_in, perm), (cond_in, cond), (cls_in, cls), (e_in, e_ref), (h_in, h_ref), (p_in, p_ref)]
    copies = [pltpu.make_async_copy(a, b, sems.at[k]) for k, (a, b) in enumerate(moves)]
    for copy in copies:
        copy.start()
    for copy in copies[:8]:
        copy.wait()
    in_x, rest = split_index(pos[...], width)
    rec_y, rec_z = split_index(rest, span)
    lines = [((owner[...] * width + in_x) * depth + rec_z).astype(F32), rec_y.astype(F32)]
    lines = jnp.concatenate(lines + [seen[k] for k in range(seen.shape[0])], axis=0)
    for slab in range(listed.shape[0]):
        listed[slab] = lines
    leave = pltpu.make_async_copy(listed, list_out, sems.at[len(moves)])
    leave.start()
    for k in range(wavelet.shape[0]):
        tab_ref[k:k + 1, :] = jnp.full((1, span), wavelet[k], F32)
    src = source_map(cells, signs, meta[0:1, 0:1].astype(jnp.int32), width, depth, span, full_x)
    src_ref[...] = src.reshape(width, depth, span)
    for copy in copies[8:11]:
        copy.wait()
    for i in range(width):
        double = 2.0 * perm[i]
        share = 1.0 / (double + cond[i])
        coef_ref[0, i] = (double - cond[i]) * share
        coef_ref[1, i] = share
        kind = cls[i]
        rate = jnp.zeros((depth, span), F32)
        gain = jnp.zeros((depth, span), F32)
        for k in range(rate_t.shape[0]):
            rate = jnp.where(kind == k, rate_t[k], rate)
            gain = jnp.where(kind == k, (1.0 - rate_t[k]) * strength_t[k], gain)
        coef_ref[2, i] = rate
        coef_ref[3, i] = gain
    for copy in copies[11:]:
        copy.wait()
    planes = own_planes(e_ref, h_ref, p_ref)
    right, left = edge_values(planes, lambda i: [coef_ref[k, i] for k in range(4)],
                              lambda step, i: src_ref[i] * wavelet[step - 1], h_ref)
    last = width - 1
    right += [coef_ref[0, last] - coef_ref[1, last] * coef_ref[3, last], coef_ref[1, last]]
    left += [coef_ref[0, 0] - coef_ref[1, 0] * coef_ref[3, 0], coef_ref[1, 0]]
    emit_all(even, a_ref, b_ref, right, left)
    leave.wait()


def receiver_kernel(width, depth, which, meta, got, maps_ref, acc):
    rows = width * depth
    span = acc.shape[1]
    blocks, _, n = got.shape
    acc[...] = jnp.zeros(acc.shape, F32)
    first_row = meta[0:1, :] * (width * depth)
    row_at = lax.broadcasted_iota(jnp.int32, (rows, n), 0).astype(F32)
    y_at = lax.broadcasted_iota(jnp.int32, (span, n), 0).astype(F32)
    group = max(g for g in (1, 2, 4, 8) if blocks % g == 0)
    zero = jnp.zeros((rows, n), jnp.bfloat16)

    def block(k, carry):
        left = [[] for _ in which]
        right = []
        for b in range(group):
            at = k * group + b
            hot = row_at == got[at, 0:1, :] - first_row[:, :n]
            at_y = jnp.where(y_at == got[at, 1:2, :], 1.0, 0.0).astype(jnp.bfloat16)
            right += [at_y] * 3
            for part, s in zip(left, which):
                if s == 0:
                    part += [jnp.where(hot, 1.0, 0.0).astype(jnp.bfloat16), zero, zero]
                    continue
                v = got[at, 1 + s:2 + s, :]
                high = v.astype(jnp.bfloat16).astype(F32)
                mid = (v - high).astype(jnp.bfloat16).astype(F32)
                low = (v - high) - mid
                part += [jnp.where(hot, u, 0.0).astype(jnp.bfloat16) for u in (high, mid, low)]
        acc[...] += lax.dot_general(
            jnp.concatenate([jnp.concatenate(part, axis=1) for part in left], axis=0) if len(left) > 1 else jnp.concatenate(left[0], axis=1),
            jnp.concatenate(right, axis=1),
            (((1,), (1,)), ((), ())),
            preferred_element_type=F32,
        )
        return carry

    lax.fori_loop(0, blocks // group, block, 0)
    maps_ref[...] = acc[...].reshape(maps_ref.shape)


def round_body(planes, meta, coef_ref, coefh_ref, a_ref, b_ref, inject, dest, seen=None, final=False):
    even = is_even(meta, coef_ref.shape[2:])
    keep = meta[2:3, :]
    last = planes.last

    def coef_of(i):
        return [coef_ref[k, i] for k in range(4)]

    before, after = ([coefh_ref[side, k] for k in range(2)] for side in (0, 1))
    rest = {c: 0.0 for c in range(3)}
    zero = jnp.zeros(coef_ref.shape[2:], F32)
    none = {c: zero for c in range(3)}

    def store(kind, c, i, level, value):
        ref, idx = dest(kind, c, i, level)
        ref[idx] = value
        planes.put((kind, c, i), ref, *idx)

    low_e = low_h = high_e = high_h = None
    for level in range(1, ROUND + 1):
        sent = 2 * (level - 1)
        edge = {c: planes.get("E", c, 0) * keep for c in (1, 2)}
        if level == 1:
            low_h = {0: zero, 1: 0.5 * edge[2], 2: -0.5 * edge[1]}
            far = None
        else:
            far = {1: 0.5 * low_e[2], 2: -0.5 * low_e[1]}
            low_h.update(h_step(low_h, low_e, edge, parts=(0, 1, 2) if level < ROUND else (1, 2)))
        if level == 1:
            low_e = {0: before[1] * (dby(low_h[2]) - dbz(low_h[1])), 1: -(before[1] * low_h[2]), 2: before[1] * low_h[1]}
        elif level < ROUND:
            low_e = e_step(low_e, low_h, far, rest, before, 0.0)
        h_prev = {c: low_h[c] + pick(even, a_ref, b_ref, sent + c - 1, True) for c in (1, 2)}
        now_h = {}
        for i in range(last + 1):
            h = planes.triple("H", i)
            if level > 1 or i == last:
                if i < last:
                    e_next = planes.triple("E", i + 1, (1, 2))
                else:
                    e_next = {c: pick(even, a_ref, b_ref, sent + c - 1, False) for c in (1, 2)}
                    if level > 1:
                        e_next = {c: e_next[c] + high_e[c] for c in (1, 2)}
                h = h_step(h, planes.triple("E", i), e_next)
                for c in range(3):
                    if not (final and level == ROUND):
                        store("H", c, i, level, h[c])
            now_h[i] = h
        for i in range(last + 1):
            h = now_h[i]
            cf = coef_of(i)
            new = e_step(planes.triple("E", i), h, h_prev, planes.triple("P", i), cf, inject(level, i))
            if not (final and level == ROUND and seen is not None):
                for c in range(3):
                    store("E", c, i, level, new[c])
            if not (final and level == ROUND):
                pn = p_step(planes.triple("P", i), new, cf)
                for c in range(3):
                    store("P", c, i, level, pn[c])
            if seen is not None:
                seen(level, i, new)
            h_prev = h
        if level == 1:
            high_e = {0: zero, 1: after[1] * h_prev[2], 2: -(after[1] * h_prev[1])}
            high_h = none
        elif level < ROUND:
            high_h = h_step(high_h, high_e, None)
            high_e = e_step(high_e, high_h, h_prev, rest, after, 0.0)


def store_in(e_ref, h_ref, p_ref, by_level=False):
    refs = {"E": e_ref, "H": h_ref, "P": p_ref}

    def dest(kind, c, i, level):
        return refs[kind], ((level - 1, c, i) if kind == "E" and by_level else (c, i))

    return dest


def forward_one_kernel(meta, tab_ref, e_ref, h_ref, p_ref, coef_ref, src_ref, b_ref, a_ref,
                       hist_ref, hs_ref, ps_ref, coefh_ref, oa_ref, ob_ref):
    even = is_even(meta, e_ref.shape[2:])
    wavelet = 0
    for side in (0, 1):
        for k in range(2):
            coefh_ref[side, k] = pick(even, a_ref, b_ref, 2 * ROUND + k, side == 0)
    planes = own_planes(e_ref, h_ref, p_ref)

    def inject(level, i):
        return src_ref[i] * tab_ref[wavelet + level - 1:wavelet + level, :]

    round_body(planes, meta, coef_ref, coefh_ref, a_ref, b_ref, inject, store_in(hist_ref, hs_ref, ps_ref, True))
    right, left = edge_values(planes, lambda i: [coef_ref[k, i] for k in range(4)], lambda step, i: inject(ROUND + step, i), hs_ref)
    emit_all(even, oa_ref, ob_ref, right, left)


def forward_two_kernel(meta, tab_ref, hist_in, hs_in, ps_in, coef_ref, coefh_ref, src_ref, maps_ref, e_ref, h_ref, p_ref,
                       b_ref, a_ref, hist_ref, h_out, oa_ref, ob_ref, hs_ref, ps_ref):
    wavelet = ROUND
    round_body(own_planes(hist_in, hs_in, ps_in, ROUND - 1), meta, coef_ref, coefh_ref, a_ref, b_ref,
               lambda level, i: src_ref[i] * tab_ref[wavelet + level - 1:wavelet + level, :],
               store_in(hist_ref, hs_ref, ps_ref, True), final=True)

    def inject(step, i):
        return maps_ref[0, i] * hist_ref[ROUND - step, 1, i] - maps_ref[step, i]

    right, left = edge_values(own_planes(e_ref, h_ref, p_ref), lambda i: [coef_ref[k, i] for k in range(4)], inject, h_out)
    emit_all(is_even(meta, e_ref.shape[2:]), oa_ref, ob_ref, right, left)


def correlate(corr_ref, i, b, now, prev, add):
    eps = b[0] * (now[0] - prev[0]) + b[1] * (now[1] - prev[1]) + b[2] * (now[2] - prev[2])
    sig = b[0] * now[0] + b[1] * now[1] + b[2] * now[2]
    if add is not None:
        eps, sig = eps + add[0, i], sig + add[1, i]
    corr_ref[0, i] = eps
    corr_ref[1, i] = sig


def adjoint_one_kernel(meta, e_ref, h_ref, p_ref, coef_ref, coefh_ref, maps_ref, maps2_ref, hist1_ref, hist2_ref,
                       b_ref, a_ref, e_out, hs_ref, ps_ref, oa_ref, ob_ref):
    planes = own_planes(e_ref, h_ref, p_ref)

    def inject(level, i):
        return maps_ref[0, i] * hist2_ref[ROUND - level, 1, i] - maps_ref[level, i]

    def inject_next(step, i):
        return maps_ref[0, i] * hist1_ref[ROUND - step, 1, i] - maps2_ref[step - 1, i]

    round_body(planes, meta, coef_ref, coefh_ref, a_ref, b_ref, inject, store_in(e_out, hs_ref, ps_ref, True))
    right, left = edge_values(planes, lambda i: [coef_ref[k, i] for k in range(4)], inject_next, hs_ref)
    emit_all(is_even(meta, e_ref.shape[2:]), oa_ref, ob_ref, right, left)


def correlation_kernel(adj_ref, hist1_ref, hist2_ref, corr_ref):
    for i in range(corr_ref.shape[1]):
        for level in range(1, ROUND + 1):
            n = ROUND - level
            e = [adj_ref[level - 1, c, i] for c in range(3)]
            now = [hist2_ref[n, c, i] for c in range(3)]
            prev = [hist2_ref[n - 1, c, i] if n > 0 else hist1_ref[ROUND - 1, c, i] for c in range(3)]
            correlate(corr_ref, i, e, now, prev, corr_ref if level > 1 else None)


def adjoint_two_kernel(meta, e_ref, hs_in, ps_in, coef_ref, coefh_ref, maps_ref, maps2_ref, e0_ref, hist1_ref,
                       corr_in, b_ref, a_ref, corr_ref, es_ref, hs_ref, ps_ref):
    def seen(level, i, e):
        n = ROUND - level
        now = [hist1_ref[n, c, i] for c in range(3)]
        prev = [hist1_ref[n - 1, c, i] if n > 0 else e0_ref[c, i] for c in range(3)]
        correlate(corr_ref, i, e, now, prev, corr_ref if level > 1 else corr_in)

    def inject(level, i):
        return maps_ref[0, i] * hist1_ref[ROUND - level, 1, i] - maps2_ref[level - 1, i]

    round_body(own_planes(e_ref, hs_in, ps_in, ROUND - 1), meta, coef_ref, coefh_ref, a_ref, b_ref, inject,
               store_in(es_ref, hs_ref, ps_ref), seen, final=True)


def call(body, name, inputs, outs, scratch=(), remote=(), work=10**10, stay_out=()):
    vmem = pl.BlockSpec(memory_space=pltpu.VMEM)
    stay = pl.BlockSpec(memory_space=pltpu.HBM)
    return pl.pallas_call(
        body,
        name=name,
        out_shape=[jax.ShapeDtypeStruct(s, F32) for s in outs],
        in_specs=[vmem] * len(inputs) + [stay] * len(remote),
        out_specs=[stay if k in stay_out else vmem for k in range(len(outs))],
        scratch_shapes=[s if not isinstance(s, tuple) else pltpu.VMEM(s, F32) for s in scratch],
        cost_estimate=pl.CostEstimate(flops=work, transcendentals=0, bytes_accessed=0),
        compiler_params=pltpu.CompilerParams(vmem_limit_bytes=48 * 1024 * 1024),
    )(*inputs, *[pltpu.with_memory_space_constraint(x, pltpu.HBM) for x in remote])


def per_device(
    electric,
    magnetic,
    polar,
    adj_electric,
    adj_magnetic,
    adj_polar,
    permittivity,
    conductivity,
    debye_class,
    debye_rate,
    debye_strength,
    wavelet,
    src_cell,
    src_sign,
    rec_owner,
    rec_pos,
    observed,
):
    width, depth, span = permittivity.shape
    steps = wavelet.shape[0]
    nsub = lax.axis_size("sub")
    nshot = lax.axis_size("shot")
    mine = lax.axis_index("sub")
    line = lax.broadcasted_iota(jnp.int32, (8, 128), 0)
    meta = jnp.where(line == 0, mine, jnp.where(line == 1, 1 - mine % 2, jnp.minimum(mine, 1))).astype(F32)
    plane = (depth, span)

    def receivers(name, which):
        (maps,) = call(
            lambda *refs: receiver_kernel(width, depth, which, *refs),
            name,
            [meta, got],
            [(len(which), width, *plane)],
            [(len(which) * width * depth, span)],
            work=10**9,
        )
        return maps

    fields = (electric[0], magnetic[0], polar[0])
    adjoint = (adj_electric[0], adj_magnetic[0], adj_polar[0])

    own = (3, width, *plane)
    list_shape = (nsub, steps + 2, rec_pos.shape[1])
    *fields, coef, src, tab, listed, a1, b1 = call(
        lambda *refs: first_kernel(width * nsub, *refs),
        "first",
        [meta],
        [own, own, own, (4, width, *plane), (width, *plane), (steps, span), list_shape, *[(2 * ROUND + 2, *plane)] * 2],
        [
            (width, *plane),
            (width, *plane),
            pltpu.VMEM((width, *plane), jnp.int32),
            pltpu.VMEM(src_cell.shape, jnp.int32),
            pltpu.VMEM(src_sign.shape, jnp.int32),
            pltpu.SMEM(debye_rate.shape, F32),
            pltpu.SMEM(debye_strength.shape, F32),
            pltpu.SMEM(wavelet.shape, F32),
            pltpu.VMEM(rec_pos.shape, jnp.int32),
            pltpu.VMEM(rec_pos.shape, jnp.int32),
            (steps, *rec_pos.shape),
            list_shape,
            pltpu.SemaphoreType.DMA((15,)),
        ],
        [
            *fields, permittivity, conductivity, debye_class, src_cell, src_sign, debye_rate, debye_strength, wavelet,
            rec_pos, rec_owner[:, :, 0], jnp.swapaxes(observed, 0, 1),
        ],
        stay_out=(6,),
    )
    got_a1, got_b1 = exchange(a1, b1)
    got = lax.all_to_all(listed, "sub", 0, 0)
    edges = [(2 * ROUND, *plane)] * 2
    hist1, hs, ps, coefh, a2, b2 = call(
        forward_one_kernel,
        "forward_one",
        [meta, tab, *fields, coef, src, got_b1, got_a1],
        [(ROUND, *own), own, own, (2, 2, *plane), *edges],
    )
    got, hs = lax.optimization_barrier((got, hs))
    got_a2, got_b2 = exchange(a2, b2)
    maps = receivers("receivers_late", (0, *range(steps, ROUND, -1)))
    hist2, adj_h, a3, b3 = call(
        forward_two_kernel,
        "forward_two",
        [meta, tab, hist1, hs, ps, coef, coefh, src, maps, *adjoint, got_b2, got_a2],
        [(ROUND, *own), own, *edges],
        [own, own],
    )
    got, hist2 = lax.optimization_barrier((got, hist2))
    got_a3, got_b3 = exchange(a3, b3)
    maps2 = receivers("receivers_early", tuple(range(ROUND, 0, -1)))
    adj, hs, ps, a4, b4 = call(
        adjoint_one_kernel,
        "adjoint_one",
        [meta, adjoint[0], adj_h, adjoint[2], coef, coefh, maps, maps2, hist1, hist2, got_b3, got_a3],
        [(ROUND, *own), own, own, *edges],
    )
    got_a4, got_b4 = exchange(a4, b4)
    (corr,) = call(correlation_kernel, "correlation", [adj, hist1, hist2], [(2, width, *plane)], work=10**9)
    (corr,) = call(
        adjoint_two_kernel,
        "adjoint_two",
        [meta, adj, hs, ps, coef, coefh, maps, maps2, fields[0], hist1, corr, got_b4, got_a4],
        [(2, width, *plane)],
        [own, own, own],
    )
    total = shot_sum(corr)
    return (-(total[0] / (steps * nshot)), -(total[1] / (steps * nshot)))


def solution(mesh):
    in_specs = (
        P("shot", None, "sub", None, None),
        P("shot", None, "sub", None, None),
        P("shot", None, "sub", None, None),
        P("shot", None, "sub", None, None),
        P("shot", None, "sub", None, None),
        P("shot", None, "sub", None, None),
        P("sub", None, None),
        P("sub", None, None),
        P("sub", None, None),
        P(),
        P(),
        P(),
        P("shot", None),
        P("shot", None),
        P("shot", "sub", None),
        P("shot", "sub"),
        P("shot", None, "sub"),
    )
    out_specs = (P("sub", None, None), P("sub", None, None))
    return jax.shard_map(
        per_device, mesh=mesh, in_specs=in_specs, out_specs=out_specs, check_vma=False
    )
```
